128 devices in a mesh: dom: 16 (over y_hi, x, core), feat: 8 (over z, y_lo).
Axes of the slice: x: 4, y: 4 (y_hi: 2, y_lo: 2; y = y_hi * 2 + y_lo), z: 4, core: 2. Of those that a mesh axis runs over, the one named last changes fastest.
Arguments:
- state: bfloat16 [512, 32768], P('feat', 'dom'), may hold values from -3 to 3
- inputs: bfloat16 [2, 32768], P(None, 'dom'), may hold values from -6 to 6
- adj_tiles: bfloat16 [256, 4, 128, 128], P('dom'), may hold values from -0.25 to 0.25
- adj_cols: int32 [256, 4], P('dom'), may hold values from 0 to 17, as said below
- valid_rows: int32 [16], P('dom'), may hold values from 1024 to 2048, as said below
- cluster_of: int32 [32768], P('dom'), may hold values from 0 to 4095
- w_gates: bfloat16 [3, 512, 4, 512], P(None, 'feat'), may hold values from -0.125 to 0.125
- w_input: bfloat16 [3, 512, 2], P(None, 'feat'), may hold values from -4 to 4
- bias: float32 [3, 512], P(None, 'feat'), may hold values from -4 to 4
- w_value: bfloat16 [8, 64, 64], P('feat'), may hold values from -0.75 to 0.75
- source_emb: float32 [8, 10, 4096], P('feat'), may hold values from -5 to 5
- target_emb: float32 [8, 10, 4096], P('feat'), may hold values from -5 to 5
- coarse_tiles: bfloat16 [32, 2, 128, 128], replicated, may hold values from -0.375 to 0.375
- coarse_cols: int32 [32, 2], replicated, may hold values from 0 to 31
Outputs:
- new_state: bfloat16 [512, 32768], P('feat', 'dom')
The draws below stay inside these ranges and needn't reach their ends.
Inputs may be any that keep to these rules, and one draw needn't show every extreme that they name: `adj_cols`: for local row tile t of a partition (t counted from 0 in the partition), every entry lies in t to t + 2, the first is t and the last is t + 2. `valid_rows`: some partition has all 2048 rows valid and another exactly half of them.
All inputs are finite; a program needn't handle non-finite values.
Results may differ from the reference program's by a relative error of at most 0.003.
Values may be sent and summed in bfloat16 or wider, within the bound.
A program may use at most 64 MiB of HBM per device.

```python
import math
import jax
import jax.numpy as jnp
from jax import lax

H = 512
HEAD = 64
HEADS = 8
EMB = 10
F_IN = 2
TILE = 128
KB = 4
KC = 2
ROWS_DEV = 2048
SENSORS = 32768
CLUSTERS = 4096
N_DOM = 16


def embed_pair(key):
    base_key = jax.random.fold_in(key, 7001)
    key_source, key_target = jax.random.split(base_key, 2)
    shape = (HEADS, EMB, CLUSTERS)
    source = jnp.clip(jax.random.normal(key_source, shape, jnp.float32), -4.0, 4.0)
    target = jnp.clip(jax.random.normal(key_target, shape, jnp.float32), -4.0, 4.0)
    return (source, target)


def draw_source_emb(key, part):
    return embed_pair(key)[0]


def draw_target_emb(key, part):
    return embed_pair(key)[1]


def draw_adj_cols(key, part):
    tile_rows = SENSORS // TILE
    per_part = ROWS_DEV // TILE
    local_tile = jnp.arange(tile_rows, dtype=jnp.int32) % per_part
    offsets = jax.random.randint(jax.random.fold_in(key, 7002), (tile_rows, KB), 0, 3, dtype=jnp.int32)
    offsets = offsets.at[:, 0].set(0)
    offsets = offsets.at[:, KB - 1].set(2)
    return (local_tile[:, None] + offsets).astype(jnp.int32)


def draw_valid_rows(key, part):
    parts = SENSORS // ROWS_DEV
    key_rows, key_full, key_half = jax.random.split(jax.random.fold_in(key, 7003), 3)
    counts = jax.random.randint(key_rows, (parts,), ROWS_DEV // 2, ROWS_DEV + 1, dtype=jnp.int32)
    full_part = jax.random.randint(key_full, (), 0, parts, dtype=jnp.int32)
    half_part = (full_part + 1 + jax.random.randint(key_half, (), 0, parts - 1, dtype=jnp.int32)) % parts
    counts = counts.at[full_part].set(ROWS_DEV)
    counts = counts.at[half_part].set(ROWS_DEV // 2)
    return counts.astype(jnp.int32)


def place_ends(values, own_key, low, high):
    extent = values.shape
    spot = [jax.random.randint(jax.random.fold_in(own_key, axis), (), 0, extent[axis]) for axis in range(len(extent))]
    values = values.at[tuple(spot)].set(low)
    longest = extent.index(max(extent))
    spot[longest] = (spot[longest] + 1) % extent[longest]
    return values.at[tuple(spot)].set(high)


def block_levels(rng, extent, pieces, low, largest):
    def one(axis_at, shards_of):
        steps = jax.random.uniform(jax.random.fold_in(jax.random.fold_in(rng, 6), axis_at), (shards_of,), jnp.float32, low / len(pieces), largest / len(pieces))
        return jnp.repeat(jnp.exp(steps), extent[axis_at] // shards_of).reshape((-1,) + (1,) * (len(extent) - axis_at - 1))

    gain = one(*pieces[0])
    for cut in pieces[1:]:
        gain = gain * one(*cut)
    return gain


def bell_draw(own_key, shape, width, limit, pieces=(), held_as=jnp.bfloat16):
    values = width * jax.random.normal(own_key, shape, jnp.float32)
    if pieces:
        values = values * block_levels(own_key, shape, pieces, -0.22, 0.18)
    return jnp.clip(values, -limit, limit).astype(held_as)


def setup_inputs(seed: int = 0) -> dict:
    splits = jax.random.split(jax.random.key(seed), 15)
    state = bell_draw(splits[0], (H, SENSORS), 0.5, 3.0, ((0, 8), (1, 16)))
    inputs = bell_draw(splits[1], (F_IN, SENSORS), 1.0, 6.0, ((1, 16),))
    adj_tiles = bell_draw(splits[2], (SENSORS // TILE, KB, TILE, TILE), (KB * TILE) ** -0.5, 0.25, ((0, 16),))
    adj_cols = draw_adj_cols(jax.random.fold_in(splits[14], 71), 0)
    valid_rows = draw_valid_rows(jax.random.fold_in(splits[14], 71), 0)
    cluster_of = place_ends(jax.random.randint(splits[5], (SENSORS,), 0, CLUSTERS), jax.random.fold_in(splits[5], 1), 0, CLUSTERS - 1).astype(jnp.int32)
    w_gates = bell_draw(splits[6], (3, H, 4, H), (4 * H) ** -0.5, 0.125, ((1, 8),))
    w_input = bell_draw(splits[7], (3, H, F_IN), F_IN ** -0.5, 4.0, ((1, 8),))
    bias = bell_draw(splits[8], (3, H), 1.0, 4.0, ((1, 8),), jnp.float32)
    w_value = bell_draw(splits[9], (HEADS, HEAD, HEAD), HEAD ** -0.5, 0.75, ((0, 8),))
    source_emb = draw_source_emb(jax.random.fold_in(splits[14], 71), 0)
    target_emb = draw_target_emb(jax.random.fold_in(splits[14], 71), 0)
    coarse_tiles = bell_draw(splits[12], (CLUSTERS // TILE, KC, TILE, TILE), (KC * TILE) ** -0.5, 0.375)
    coarse_cols = place_ends(jax.random.randint(splits[13], (CLUSTERS // TILE, KC), 0, CLUSTERS // TILE), jax.random.fold_in(splits[13], 1), 0, (CLUSTERS // TILE) - 1).astype(jnp.int32)
    return dict(state=state, inputs=inputs, adj_tiles=adj_tiles, adj_cols=adj_cols, valid_rows=valid_rows, cluster_of=cluster_of, w_gates=w_gates, w_input=w_input, bias=bias, w_value=w_value, source_emb=source_emb, target_emb=target_emb, coarse_tiles=coarse_tiles, coarse_cols=coarse_cols)


def pick_tiles(extended, columns):
    return extended[:, columns]


def diffuse(states, adj_tiles, adj_cols, row_mask):
    tile_count = ROWS_DEV // TILE
    grouped = states.reshape(H, N_DOM, ROWS_DEV)
    before = jnp.roll(grouped, 1, axis=1)[:, :, ROWS_DEV - TILE:]
    after = jnp.roll(grouped, -1, axis=1)[:, :, :TILE]
    extended = jnp.concatenate([before, grouped, after], axis=2)
    extended = extended.reshape(H, N_DOM, tile_count + 2, TILE)
    columns = adj_cols.reshape(N_DOM, tile_count, KB)
    picked = jax.vmap(pick_tiles, in_axes=(1, 0), out_axes=1)(extended, columns)
    tiles = adj_tiles.reshape(N_DOM, tile_count, KB, TILE, TILE)
    result = jnp.einsum("hpnkj,pnkji->hpni", picked.astype(jnp.float32), tiles.astype(jnp.float32))
    return (result.reshape(H, SENSORS) * row_mask).astype(jnp.bfloat16)


def attend(source_emb, target_emb, values):
    heads_here, emb_dim, query_count = source_emb.shape
    block_rows = math.gcd(query_count, 512)
    blocks = source_emb.reshape(heads_here, emb_dim, query_count // block_rows, block_rows)
    blocks = jnp.moveaxis(blocks, 2, 0)

    def one_block(source_block):
        scores = jnp.einsum("hei,hej->hij", source_block, target_emb, precision=lax.Precision.HIGHEST)
        scores = jnp.maximum(scores, 0.0)
        row_peak = jnp.max(scores, axis=2, keepdims=True)
        raised = jnp.exp(scores - row_peak)
        weights = (raised / jnp.sum(raised, axis=2, keepdims=True)).astype(jnp.bfloat16)
        return jnp.einsum("hdj,hij->hdi", values.astype(jnp.float32), weights.astype(jnp.float32))

    outputs = lax.map(one_block, blocks)
    outputs = jnp.moveaxis(outputs, 0, 2)
    return outputs.reshape(heads_here, values.shape[1], query_count)


def reference(state, inputs, adj_tiles, adj_cols, valid_rows, cluster_of, w_gates, w_input, bias, w_value, source_emb, target_emb, coarse_tiles, coarse_cols):
    position = jnp.arange(SENSORS, dtype=jnp.int32)
    partition = position // ROWS_DEV
    local_row = position % ROWS_DEV
    row_mask = (local_row < valid_rows[partition]).astype(jnp.float32)
    masked = (state.astype(jnp.float32) * row_mask).astype(jnp.bfloat16)
    hop_one = diffuse(masked, adj_tiles, adj_cols, row_mask)
    hop_two = diffuse(hop_one, adj_tiles, adj_cols, row_mask)
    cluster_sums = jax.ops.segment_sum(masked.astype(jnp.float32).T, cluster_of, CLUSTERS).T
    counts = jax.ops.segment_sum(row_mask, cluster_of, CLUSTERS)
    pooled = cluster_sums / jnp.maximum(counts, 1.0)[None, :]
    grouped = pooled.reshape(HEADS, HEAD, CLUSTERS)
    values = jnp.einsum("hde,hec->hdc", w_value.astype(jnp.float32), grouped, precision=lax.Precision.HIGHEST).astype(jnp.bfloat16)
    attended = attend(source_emb, target_emb, values).reshape(H, CLUSTERS)
    coarse_attn = (pooled + attended).astype(jnp.bfloat16)
    coarse_grid = coarse_attn.reshape(H, CLUSTERS // TILE, TILE)
    picked = coarse_grid[:, coarse_cols]
    coarse_terms = jnp.einsum("hnkj,nkji->hni", picked.astype(jnp.float32), coarse_tiles.astype(jnp.float32))
    coarse = (coarse_attn.astype(jnp.float32) + coarse_terms.reshape(H, CLUSTERS)).astype(jnp.bfloat16)
    unpooled = jnp.take(coarse, cluster_of, axis=1)
    features = jnp.stack([masked, hop_one, hop_two, unpooled]).astype(jnp.float32)
    gate_sums = jnp.einsum("ghkc,kcs->ghs", w_gates.astype(jnp.float32), features)
    input_terms = jnp.einsum("ghf,fs->ghs", w_input.astype(jnp.float32), inputs.astype(jnp.float32)) + bias[:, :, None]
    update = jax.nn.sigmoid(input_terms[0] + gate_sums[0])
    reset = jax.nn.sigmoid(input_terms[1] + gate_sums[1])
    candidate = jnp.tanh(input_terms[2] + reset * gate_sums[2])
    fresh_state = (update * masked.astype(jnp.float32) + (1.0 - update) * candidate) * row_mask
    return fresh_state.astype(jnp.bfloat16)
```

```python
import jax
import jax.numpy as jnp
from jax import lax
from jax.experimental import pallas as pl
from jax.experimental.pallas import tpu as pltpu
from jax.sharding import PartitionSpec as P

MESH = pl.DeviceIdType.MESH
BF = jnp.bfloat16
F32 = jnp.float32
N_MSG = 80


def dot(a, b, dims=((1,), (0,))):
    return lax.dot_general(a, b, (dims, ((), ())), preferred_element_type=F32)


def split3(v):
    a = v.astype(BF)
    r = v - a.astype(F32)
    b = r.astype(BF)
    c = (r - b.astype(F32)).astype(BF)
    return a, b, c


def split_counts(total):
    high = jnp.floor(total * (1.0 / 256.0)) * 256.0
    low = total - high
    row = lax.broadcasted_iota(jnp.int32, (16, total.shape[1]), 0)
    return jnp.where(row == 0, high, jnp.where(row == 1, low, 0.0))


def kernel(
    state, xin, adj_hbm, adj_cols, valid, cluster, wg_hbm, w_in, bias, w_val, src, tgt,
    ct_hbm, ccols, out,
    mext, halo, ohlo, base, pl_lhs, pool, r1, s1, r2, s2, r3, t6, s6, scores, expo,
    vals, ca, gall, gmix, ubuf, vbuf, w1m, gsum, adj, wg, ct,
    ssem, rsem, lsem,
):
    d = lax.axis_index("dom")
    f = lax.axis_index("feat")
    core, x, yh = d % 2, (d // 2) % 4, d // 8
    z, yl = f // 2, f % 2
    partner = d + 1 - 2 * core
    xp, xm, x2 = (x + 1) % 4, (x + 3) % 4, (x + 2) % 4
    zp, zm, z2 = (z + 1) % 4, (z + 3) % 4, (z + 2) % 4
    fy = f + 1 - 2 * yl
    yother = (d + 8) % 16
    dleft, dright = (d + 15) % 16, (d + 1) % 16
    didx = lambda a, b, c: a * 8 + b * 2 + c
    fidx = lambda a, b: a * 2 + b
    to_dom = lambda i: (i, f)
    to_feat = lambda i: (d, i)

    msgs = []

    def send(src_ref, dst_ref, dev):
        i = len(msgs)
        cp = pltpu.make_async_remote_copy(
            src_ref=src_ref, dst_ref=dst_ref, send_sem=ssem.at[i], recv_sem=rsem.at[i],
            device_id=dev, device_id_type=MESH,
        )
        cp.start()
        msgs.append(cp)
        return cp

    loc = [
        pltpu.make_async_copy(wg_hbm, wg, lsem.at[0]),
        pltpu.make_async_copy(adj_hbm, adj, lsem.at[1]),
        pltpu.make_async_copy(ct_hbm, ct, lsem.at[2]),
    ]
    for c in loc:
        c.start()

    barrier = pltpu.get_barrier_semaphore()
    x_peers = [didx(yh, xp, core), didx(yh, xm, core), didx(yh, x2, core)]
    f_peers = [(f + k) % 8 for k in range(1, 8)]
    cross = (d + 15 + 2 * core) % 16
    dom_peers = [partner, cross, yother] + x_peers
    for p in dom_peers:
        pl.semaphore_signal(barrier, inc=1, device_id=to_dom(p), device_id_type=MESH)
    for p in f_peers:
        pl.semaphore_signal(barrier, inc=1, device_id=to_feat(p), device_id_type=MESH)

    nvalid = valid[0]
    mask = (lax.broadcasted_iota(jnp.int32, (1, 2048), 1) < nvalid).astype(F32)
    masked32 = state[...].astype(F32) * mask
    myrows = pl.ds(pl.multiple_of(f * 64, 64), 64)
    own = pl.ds(128, 2048)
    mext[myrows, own] = masked32.astype(BF)
    base[0:64, :] = masked32
    row16 = lax.broadcasted_iota(jnp.int32, (16, 2048), 0)
    base[64:80, :] = jnp.where(row16 == 0, mask, 0.0)
    low = cluster[...] & 255
    high = cluster[...] >> 8
    ohlo[...] = (lax.broadcasted_iota(jnp.int32, (256, 2048), 0) == low).astype(F32).astype(BF)

    for c in range(2):
        for xx in range(4):
            for yy in range(2):
                slot = c * 8 + xx * 2 + yy
                hit = high == (yy * 8 + xx * 2 + c)
                pl_lhs[slot * 80:(slot + 1) * 80, :] = jnp.where(hit, base[...], 0.0).astype(BF)

    for q in range(4):
        res = dot(pl_lhs[q * 320:(q + 1) * 320, :], ohlo[...], ((1,), (1,)))
        for k in range(4):
            slot = q * 4 + k
            r = res[k * 80:(k + 1) * 80]
            pool[slot // 8, (slot % 8) // 2, slot % 2] = jnp.concatenate(
                [r[:64], split_counts(r[64:65])], axis=0
            ).astype(BF)

    pl.semaphore_wait(barrier, len(dom_peers) + len(f_peers))

    m_r1 = send(pool.at[1 - core], r1, to_dom(partner))
    mrow = lambda i: mext.at[pl.ds(pl.multiple_of(i * 64, 64), 64), own]
    m_s1 = [
        send(mrow(f), mrow(f), to_feat(fy)),
        send(mrow(f), mrow(f), to_feat(fidx(zp, yl))),
        send(mrow(f), mrow(f), to_feat(fidx(zm, yl))),
    ]
    m_h = [
        send(mext.at[myrows, pl.ds(128, 128)], halo.at[f, 1], to_dom(dleft)),
        send(mext.at[myrows, pl.ds(2048, 128)], halo.at[f, 0], to_dom(dright)),
    ]

    t6[...] = jnp.zeros_like(t6)
    s6[...] = jnp.zeros_like(s6)
    ta, tb, tc = split3(tgt[...])
    sa, sb, sc = split3(src[:, pl.ds(pl.multiple_of(d * 256, 256), 256)])
    for k, (t, s) in enumerate([(ta, sa), (ta, sb), (tb, sa), (ta, sc), (tb, sb), (tc, sa)]):
        t6[k * 16:k * 16 + 10, :] = t
        s6[k * 16:k * 16 + 10, :] = s

    def score_step(j, peak):
        cols = pl.ds(pl.multiple_of(j * 512, 512), 512)
        s = jnp.maximum(dot(t6[:, cols], s6[...], ((0,), (0,))), 0.0)
        scores[cols, :] = s
        return jnp.maximum(peak, jnp.max(s.reshape(64, 8, 256), axis=0))

    peak = lax.fori_loop(0, 8, score_step, jnp.zeros((8, 256), F32))
    peak = jnp.max(peak, axis=0, keepdims=True)

    def add_blocks(blocks):
        total = blocks[0][...].astype(F32)
        for b in blocks[1:]:
            total = total + b[...].astype(F32)
        cnt = total[64:65] + total[65:66]
        return total[:64], cnt

    def packed(sums, cnt):
        return jnp.concatenate([sums, split_counts(cnt)], axis=0).astype(BF)

    m_r1.wait_recv()
    for xx in range(4):
        for yy in range(2):
            s1[xx, yy] = packed(*add_blocks([pool.at[core, xx, yy], r1.at[xx, yy]]))
    m_r2 = [
        send(s1.at[xp], r2.at[0], to_dom(x_peers[0])),
        send(s1.at[xm], r2.at[1], to_dom(x_peers[1])),
        send(s1.at[x2], r2.at[2], to_dom(x_peers[2])),
    ]

    m_s1[0].wait_recv()
    m_s2 = [
        send(mrow(fy), mrow(fy), to_feat(fidx(zp, yl))),
        send(mrow(fy), mrow(fy), to_feat(fidx(zm, yl))),
    ]
    for m in m_h:
        m.wait_recv()
    m_hf = [send(halo.at[f], halo.at[f], to_feat(p)) for p in f_peers]

    def exp_step(j, total):
        cols = pl.ds(pl.multiple_of(j * 512, 512), 512)
        e = jnp.exp(scores[cols, :] - peak)
        expo[cols, :] = e.astype(BF)
        return total + jnp.sum(e.reshape(64, 8, 256), axis=0)

    total = lax.fori_loop(0, 8, exp_step, jnp.zeros((8, 256), F32))
    inv = 1.0 / jnp.sum(total, axis=0, keepdims=True)

    for m in m_r2:
        m.wait_recv()
    for yy in range(2):
        s2[yy] = packed(*add_blocks([s1.at[x, yy]] + [r2.at[k, yy] for k in range(3)]))
    m_r3 = send(s2.at[1 - yh], r3, to_dom(yother))
    m_r3.wait_recv()
    sums, cnt = add_blocks([s2.at[yh], r3])
    pooled = sums / jnp.maximum(cnt, 1.0)
    pa, pb, pc = split3(pooled)
    wv = w_val[...]
    vals[d] = (dot(wv, pa) + dot(wv, pb) + dot(wv, pc)).astype(BF)

    def gather_start(buf):
        a = [send(buf(d), buf(d), to_dom(yother))]
        a += [send(buf(d), buf(d), to_dom(p)) for p in x_peers]
        return a, [send(buf(d), buf(d), to_dom(partner))]

    def gather_y(buf, a, p):
        a[0].wait_recv()
        b = [send(buf(yother), buf(yother), to_dom(i)) for i in x_peers]
        p.append(send(buf(yother), buf(yother), to_dom(partner)))
        return b

    x_from = [didx(yh, xm, core), didx(yh, xp, core), didx(yh, x2, core)]

    def gather_x(buf, msg, p, shift):
        for m, i in zip(msg, x_from):
            m.wait_recv()
            i = (i + shift) % 16
            p.append(send(buf(i), buf(i), to_dom(partner)))

    vslot = lambda i: vals.at[i]
    a, p = gather_start(vslot)
    b = gather_y(vslot, a, p)
    gather_x(vslot, a[1:], p, 0)
    gather_x(vslot, b, p, 8)
    for m in p:
        m.wait_recv()

    att = jnp.zeros((64, 256), F32)
    for k in range(16):
        att = att + dot(vals[k], expo[k * 256:(k + 1) * 256, :])
    ca[f] = (pooled + att * inv).astype(BF)
    m_ca = [send(ca.at[f], ca.at[f], to_feat(i)) for i in f_peers]

    def mhalf(i, h):
        return mext.at[pl.ds(pl.multiple_of(i * 64 + h * 32, 32), 32), own]

    m_s3 = []
    for m, i, h, to in (
        (m_s1[1], fidx(zm, yl), 0, zp),
        (m_s1[2], fidx(zp, yl), 1, zm),
        (m_s2[0], fidx(zm, 1 - yl), 0, zp),
        (m_s2[1], fidx(zp, 1 - yl), 1, zm),
    ):
        m.wait_recv()
        m_s3.append(send(mhalf(i, h), mhalf(i, h), to_feat(fidx(to, yl))))

    loc[0].wait()
    for m in m_ca:
        m.wait_recv()
    g = dot(wg[576:768, :], ca[...].reshape(512, 256)).astype(BF)
    gall[2 * d] = g[:, :128]
    gall[2 * d + 1] = g[:, 128:]
    gslot = lambda i: gall.at[pl.ds(2 * i, 2)]
    a, p = gather_start(gslot)

    for m in m_hf + m_s3:
        m.wait_recv()
    for i in range(8):
        mext[i * 64:(i + 1) * 64, 0:128] = halo[i, 0]
        mext[i * 64:(i + 1) * 64, 2176:2304] = halo[i, 1]
    b = gather_y(gslot, a, p)

    for c in range(9):
        cols = slice(c * 256, (c + 1) * 256)
        r = dot(wg[0:576, :], mext[:, cols])
        gsum[:, cols] = r[0:192]
        w1m[:, cols] = r[192:384]
        ubuf[:, cols] = r[384:576].astype(BF)

    gather_x(gslot, a[1:], p, 0)
    loc[1].wait()

    def diffuse(buf, t):
        lo, mid, hi = (buf[:, (t + k) * 128:(t + k + 1) * 128] for k in range(3))
        def pick(k):
            c = jnp.full((1, 128), adj_cols[t, k], jnp.int32)
            wlo, wmid, whi = ((c == t + i).astype(F32).astype(BF) for i in range(3))
            return lo * wlo + mid * wmid + hi * whi
        lhs = jnp.concatenate([lo, pick(1), pick(2), hi], axis=1)
        r = dot(lhs, adj[t])
        pos = lax.broadcasted_iota(jnp.int32, (1, 128), 1) + t * 128
        return r * (pos < nvalid).astype(F32)

    def first(t):
        cols = slice((t + 1) * 128, (t + 2) * 128)
        vbuf[:, cols] = (w1m[:, cols] + diffuse(ubuf, t)).astype(BF)

    def second(t):
        cols = slice((t + 1) * 128, (t + 2) * 128)
        gsum[:, cols] = gsum[:, cols] + diffuse(vbuf, t)

    first(0)
    first(15)
    tile = lambda i: vbuf.at[:, pl.ds(i * 128, 128)]
    m_v = [
        send(tile(1), tile(17), to_dom(dleft)),
        send(tile(16), tile(0), to_dom(dright)),
    ]
    for t in range(1, 15):
        first(t)
    gather_x(gslot, b, p, 8)
    for t in range(1, 15):
        second(t)
    for m in m_v:
        m.wait_recv()
    second(0)
    second(15)

    for m in p:
        m.wait_recv()
    loc[2].wait()

    def mix_step(s, carry):
        parts = []
        for h in range(2):
            t = s * 2 + h
            cols = [ccols[t, k] for k in range(2)]
            lhs = jnp.concatenate(
                [gall[c] for c in cols],
                axis=1,
            )
            parts.append(gall[t].astype(F32) + dot(lhs, ct[t]))
        gmix[s] = jnp.concatenate(parts, axis=1).astype(BF)
        return carry

    lax.fori_loop(0, 16, mix_step, 0)

    eye = lax.broadcasted_iota(jnp.int32, (64, 64), 0) == lax.broadcasted_iota(
        jnp.int32, (64, 64), 1
    )
    bcol = [
        jnp.sum(jnp.where(eye, bias[g:g + 1, :], 0.0), axis=1, keepdims=True) for g in range(3)
    ]
    win = w_in[...].astype(F32)

    for n in range(8):
        cols = slice(n * 256, (n + 1) * 256)
        ecols = slice(n * 256 + 128, (n + 1) * 256 + 128)
        hi_n = cluster[:, cols] >> 8
        oh = ohlo[:, cols]
        acc = dot(gmix[0], oh)
        for s in range(1, 16):
            acc = jnp.where(hi_n == s, dot(gmix[s], oh), acc)
        pre = acc + gsum[:, ecols]
        xi = xin[:, cols].astype(F32)
        terms = [
            win[g * 64:(g + 1) * 64, 0:1] * xi[0:1] + win[g * 64:(g + 1) * 64, 1:2] * xi[1:2]
            + bcol[g]
            for g in range(3)
        ]
        update = jax.nn.sigmoid(terms[0] + pre[0:64])
        reset = jax.nn.sigmoid(terms[1] + pre[64:128])
        cand = jnp.tanh(terms[2] + reset * pre[128:192])
        mk = (lax.broadcasted_iota(jnp.int32, (1, 256), 1) + n * 256 < nvalid).astype(F32)
        ms = state[:, cols].astype(F32) * mk
        out[:, cols] = ((update * ms + (1.0 - update) * cand) * mk).astype(BF)

    for m in msgs:
        m.wait_send()
    assert len(msgs) <= N_MSG


def body(
    state, inputs, adj_tiles, adj_cols, valid_rows, cluster_of, w_gates, w_input, bias, w_value,
    source_emb, target_emb, coarse_tiles, coarse_cols,
):
    wg = jnp.transpose(w_gates, (2, 0, 1, 3)).reshape(768, 512)
    vm = pl.BlockSpec(memory_space=pltpu.VMEM)
    sm = pl.BlockSpec(memory_space=pltpu.SMEM)
    hb = pl.BlockSpec(memory_space=pl.ANY)
    V = pltpu.VMEM
    return pl.pallas_call(
        kernel,
        out_shape=jax.ShapeDtypeStruct(state.shape, BF),
        in_specs=[vm, vm, hb, sm, sm, vm, hb, vm, vm, vm, vm, vm, hb, sm],
        out_specs=vm,
        scratch_shapes=[
            V((512, 2304), BF),
            V((8, 2, 64, 128), BF),
            V((256, 2048), BF),
            V((80, 2048), F32),
            V((1280, 2048), BF),
            V((2, 4, 2, 80, 256), BF),
            V((4, 2, 80, 256), BF),
            V((4, 2, 80, 256), BF),
            V((3, 2, 80, 256), BF),
            V((2, 80, 256), BF),
            V((80, 256), BF),
            V((96, 4096), BF),
            V((96, 256), BF),
            V((4096, 256), F32),
            V((4096, 256), BF),
            V((16, 64, 256), BF),
            V((8, 64, 256), BF),
            V((32, 192, 128), BF),
            V((16, 192, 256), BF),
            V((192, 2304), BF),
            V((192, 2304), BF),
            V((192, 2304), F32),
            V((192, 2304), F32),
            V((16, 512, 128), BF),
            V((768, 512), BF),
            V((32, 256, 128), BF),
            pltpu.SemaphoreType.DMA((N_MSG,)),
            pltpu.SemaphoreType.DMA((N_MSG,)),
            pltpu.SemaphoreType.DMA((3,)),
        ],
        compiler_params=pltpu.CompilerParams(collective_id=0, has_side_effects=True),
    )(
        state, inputs, adj_tiles.reshape(16, 512, 128), adj_cols, valid_rows,
        cluster_of.reshape(1, 2048), wg, w_input.reshape(192, 2), bias, w_value.reshape(64, 64),
        source_emb.reshape(10, 4096), target_emb.reshape(10, 4096),
        coarse_tiles.reshape(32, 256, 128), coarse_cols,
    )


def solution(mesh):
    return jax.shard_map(
        body,
        mesh=mesh,
        in_specs=(
            P("feat", "dom"),
            P(None, "dom"),
            P("dom", None, None, None),
            P("dom", None),
            P("dom"),
            P("dom"),
            P(None, "feat", None, None),
            P(None, "feat", None),
            P(None, "feat"),
            P("feat", None, None),
            P("feat", None, None),
            P("feat", None, None),
            P(),
            P(),
        ),
        out_specs=P("feat", "dom"),
        check_vma=False,
    )
```

```python
import jax
import jax.numpy as jnp
from jax import lax
from jax.experimental import pallas as pl
from jax.experimental.pallas import tpu as pltpu
from jax.sharding import PartitionSpec as P

MESH = pl.DeviceIdType.MESH
BF = jnp.bfloat16
F32 = jnp.float32
N_MSG = 80


def dot(a, b, dims=((1,), (0,))):
    return lax.dot_general(a, b, (dims, ((), ())), preferred_element_type=F32)


def split3(v):
    a = v.astype(BF)
    r = v - a.astype(F32)
    b = r.astype(BF)
    c = (r - b.astype(F32)).astype(BF)
    return a, b, c


def split_counts(total):
    high = jnp.floor(total * (1.0 / 256.0)) * 256.0
    low = total - high
    row = lax.broadcasted_iota(jnp.int32, (16, total.shape[1]), 0)
    return jnp.where(row == 0, high, jnp.where(row == 1, low, 0.0))


def kernel(
    state, xin, adj_hbm, adj_cols, valid, cluster, wg_hbm, w_in, bias, w_val, src_hbm, tgt_hbm,
    ct_hbm, ccols, out,
    mext, halo, ohlo, base, pl_lhs, pool, r1, s1, r2, s2, r3, src, tgt, t6, s6, scores, expo,
    vals, pooled, ca, gall, gmix, ubuf, vbuf, w1m, gsum, adj, wraw, wg, ct,
    ssem, rsem, lsem,
):
    d = lax.axis_index("dom")
    f = lax.axis_index("feat")
    core, x, yh = d % 2, (d // 2) % 4, d // 8
    z, yl = f // 2, f % 2
    xp, xm, x2 = (x + 1) % 4, (x + 3) % 4, (x + 2) % 4
    zp, zm = (z + 1) % 4, (z + 3) % 4
    q, qp, qm, q2 = (i * 2 + core for i in (x, xp, xm, x2))
    dev = lambda i: (i, f)
    fdev = lambda i: (d, i)
    partner, yother = dev(d + 1 - 2 * core), dev((d + 8) % 16)
    dxp, dxm, dx2 = (dev(yh * 8 + i) for i in (qp, qm, q2))
    dleft, dright = dev((d + 15) % 16), dev((d + 1) % 16)
    fi = lambda a, b: a * 2 + b
    fy, fzp, fzm = f + 1 - 2 * yl, fi(zp, yl), fi(zm, yl)
    f_peers = [fdev((f + k) % 8) for k in range(1, 8)]

    msgs = []

    def send(src_ref, dst_ref, to):
        i = len(msgs)
        cp = pltpu.make_async_remote_copy(
            src_ref=src_ref, dst_ref=dst_ref, send_sem=ssem.at[i], recv_sem=rsem.at[i],
            device_id=to, device_id_type=MESH,
        )
        cp.start()
        msgs.append(cp)
        return cp

    same = lambda ref, to: send(ref, ref, to)

    mine = pl.ds(pl.multiple_of(d * 256, 256), 256)
    loc = [
        pltpu.make_async_copy(wg_hbm, wraw, lsem.at[0]),
        pltpu.make_async_copy(adj_hbm, adj, lsem.at[1]),
        pltpu.make_async_copy(ct_hbm, ct, lsem.at[2]),
    ]
    emb = []
    for r in range(10):
        emb.append(pltpu.make_async_copy(tgt_hbm.at[r], tgt.at[pl.ds(r, 1)], lsem.at[3 + r]))
        emb.append(
            pltpu.make_async_copy(src_hbm.at[r, :, mine], src.at[pl.ds(r, 1)], lsem.at[13 + r])
        )
    for c in emb + loc:
        c.start()

    barrier = pltpu.get_barrier_semaphore()
    cross = dev((d + 15 + 2 * core) % 16)
    peers = [partner, cross, yother, dxp, dxm, dx2] + f_peers
    for p in peers:
        pl.semaphore_signal(barrier, inc=1, device_id=p, device_id_type=MESH)

    nvalid = valid[0]
    mask = (lax.broadcasted_iota(jnp.int32, (1, 2048), 1) < nvalid).astype(F32)
    masked32 = state[...].astype(F32) * mask
    myrows = pl.ds(pl.multiple_of(f * 64, 64), 64)
    own = pl.ds(128, 2048)
    mext[myrows, own] = masked32.astype(BF)
    base[0:64, :] = masked32
    row16 = lax.broadcasted_iota(jnp.int32, (16, 2048), 0)
    base[64:80, :] = jnp.where(row16 == 0, mask, 0.0)
    low = cluster[...] & 255
    high = cluster[...] >> 8
    ohlo[...] = (lax.broadcasted_iota(jnp.int32, (256, 2048), 0) == low).astype(F32).astype(BF)

    def pool_part(c, to_core):
        for xx in range(4):
            for yy in range(2):
                slot = xx * 2 + yy
                hit = high == (yy * 8 + xx * 2) + to_core
                pl_lhs[slot * 80:(slot + 1) * 80, :] = jnp.where(hit, base[...], 0.0).astype(BF)
        for i in range(2):
            res = dot(pl_lhs[i * 320:(i + 1) * 320, :], ohlo[...], ((1,), (1,)))
            for k in range(4):
                slot = i * 4 + k
                r = res[k * 80:(k + 1) * 80]
                pool[c, slot // 2, slot % 2] = jnp.concatenate(
                    [r[:64], split_counts(r[64:65])], axis=0
                ).astype(BF)

    pool_part(0, 1 - core)

    pl.semaphore_wait(barrier, len(peers))

    m_r1 = send(pool.at[0], r1, partner)
    mrow = lambda i: mext.at[pl.ds(pl.multiple_of(i * 64, 64), 64), own]
    m_s1 = [same(mrow(f), fdev(i)) for i in (fy, fzp, fzm)]
    m_h = [
        send(mext.at[myrows, pl.ds(128, 128)], halo.at[f, 1], dleft),
        send(mext.at[myrows, pl.ds(2048, 128)], halo.at[f, 0], dright),
    ]
    pool_part(1, core)

    for c in emb:
        c.wait()
    t6[...] = jnp.zeros_like(t6)
    s6[...] = jnp.zeros_like(s6)
    ta, tb, tc = split3(tgt[0:10, :])
    sa, sb, sc = split3(src[0:10, :])
    for k, (t, s) in enumerate([(ta, sa), (ta, sb), (tb, sa), (ta, sc), (tb, sb), (tc, sa)]):
        t6[k * 16:k * 16 + 10, :] = t
        s6[k * 16:k * 16 + 10, :] = s

    def score_step(j, peak):
        cols = pl.ds(pl.multiple_of(j * 512, 512), 512)
        s = jnp.maximum(dot(t6[:, cols], s6[...], ((0,), (0,))), 0.0)
        scores[cols, :] = s
        return jnp.maximum(peak, jnp.max(s.reshape(64, 8, 256), axis=0))

    def add_blocks(blocks):
        total = blocks[0][...].astype(F32)
        for b in blocks[1:]:
            total = total + b[...].astype(F32)
        return total[:64], total[64:65] + total[65:66]

    def packed(sums, cnt):
        return jnp.concatenate([sums, split_counts(cnt)], axis=0).astype(BF)

    m_r1.wait_recv()
    for xx in range(4):
        for yy in range(2):
            s1[xx, yy] = packed(*add_blocks([pool.at[1, xx, yy], r1.at[xx, yy]]))
    m_r2 = [
        send(s1.at[x2], r2.at[2], dx2),
        send(s1.at[xp], r2.at[0], dxp),
        send(s1.at[xm], r2.at[1], dxm),
    ]

    peak = lax.fori_loop(0, 8, score_step, jnp.zeros((8, 256), F32))
    peak = jnp.max(peak, axis=0, keepdims=True)

    for m in m_r2:
        m.wait_recv()
    for yy in range(2):
        s2[yy] = packed(*add_blocks([s1.at[x, yy]] + [r2.at[k, yy] for k in range(3)]))
    m_r3 = send(s2, r3, yother)

    m_s1[0].wait_recv()
    m_s2 = [same(mrow(fy), fdev(i)) for i in (fzp, fzm)]
    for m in m_h:
        m.wait_recv()
    m_hf = [same(halo.at[f], p) for p in f_peers]

    def exp_step(j, total):
        cols = pl.ds(pl.multiple_of(j * 512, 512), 512)
        e = jnp.exp(scores[cols, :] - peak)
        expo[cols, :] = e.astype(BF)
        return total + jnp.sum(e.reshape(64, 8, 256), axis=0)

    total = lax.fori_loop(0, 8, exp_step, jnp.zeros((8, 256), F32))
    inv = 1.0 / jnp.sum(total, axis=0, keepdims=True)

    m_r3.wait_recv()
    wv = w_val[...]
    for yy in range(2):
        sums, cnt = add_blocks([s2.at[yy], r3.at[yy]])
        avg = sums / jnp.maximum(cnt, 1.0)
        pooled[yy] = avg
        pa, pb, pc = split3(avg)
        vals[q, yy] = (dot(wv, pa) + dot(wv, pb) + dot(wv, pc)).astype(BF)

    m_v = [same(vals.at[q], dxp), same(vals.at[q], dxm)]
    pv = [same(vals.at[q], partner)]
    m_v[0].wait_recv()
    m_v.append(same(vals.at[qm, 0], dxp))
    pv.append(same(vals.at[qm], partner))
    m_v[1].wait_recv()
    m_v.append(same(vals.at[qp, 1], dxm))
    pv.append(same(vals.at[qp], partner))
    mhalf = lambda i, h: mext.at[pl.ds(pl.multiple_of(i * 64 + h * 32, 32), 32), own]
    m_s1[1].wait_recv()
    m_s3 = [same(mhalf(fzm, 0), fdev(fzp))]
    m_s1[2].wait_recv()
    m_s3.append(same(mhalf(fzp, 1), fdev(fzm)))
    for h in range(2):
        m_v[2 + h].wait_recv()
        pv.append(same(vals.at[q2, h], partner))
    for m in pv:
        m.wait_recv()

    att = jnp.zeros((64, 256), F32)
    for k in range(16):
        att = att + dot(vals[k % 8, k // 8], expo[k * 256:(k + 1) * 256, :])
    ca[f] = (pooled[yh] + att * inv).astype(BF)
    m_ca = [same(ca.at[f], p) for p in f_peers]

    loc[0].wait()
    for k in range(4):
        wg[k * 192:(k + 1) * 192, :] = wraw[:, k, :]
    for m in m_ca:
        m.wait_recv()
    g = dot(wg[576:768, :], ca[...].reshape(512, 256)).astype(BF)
    gall[2 * d] = g[:, :128]
    gall[2 * d + 1] = g[:, 128:]
    gs = lambda a, b: gall.at[pl.ds(2 * (a * 8 + b), 2)]
    yo = 1 - yh
    g_y = same(gs(yh, q), yother)
    g_a = [same(gs(yh, q), dxp), same(gs(yh, q), dxm)]
    pg = [same(gs(yh, q), partner)]

    m_s2[0].wait_recv()
    m_s3.append(same(mhalf(fi(zm, 1 - yl), 0), fdev(fzp)))
    m_s2[1].wait_recv()
    m_s3.append(same(mhalf(fi(zp, 1 - yl), 1), fdev(fzm)))
    g_y.wait_recv()
    g_b = [same(gs(yo, q), dxp), same(gs(yo, q), dxm)]
    pg.append(same(gs(yo, q), partner))
    g_a[0].wait_recv()
    g_f = [same(gs(yh, qm), dxp)]
    pg.append(same(gs(yh, qm), partner))
    g_a[1].wait_recv()
    pg.append(same(gs(yh, qp), partner))

    for m in m_hf + m_s3:
        m.wait_recv()
    for i in range(8):
        mext[i * 64:(i + 1) * 64, 0:128] = halo[i, 0]
        mext[i * 64:(i + 1) * 64, 2176:2304] = halo[i, 1]

    for c in range(9):
        cols = slice(c * 256, (c + 1) * 256)
        r = dot(wg[0:576, :], mext[:, cols])
        gsum[:, cols] = r[0:192]
        w1m[:, cols] = r[192:384]
        ubuf[:, cols] = r[384:576].astype(BF)

    g_b[0].wait_recv()
    pg.append(same(gs(yo, qm), partner))
    g_b[1].wait_recv()
    g_f.append(same(gs(yo, qp), dxm))
    pg.append(same(gs(yo, qp), partner))
    loc[1].wait()

    def diffuse(buf, t):
        lo, mid, hi = (buf[:, (t + k) * 128:(t + k + 1) * 128] for k in range(3))

        def pick(k):
            c = jnp.full((1, 128), adj_cols[k, t], jnp.int32)
            wlo, wmid, whi = ((c == t + i).astype(F32).astype(BF) for i in range(3))
            return lo * wlo + mid * wmid + hi * whi

        lhs = jnp.concatenate([lo, pick(1), pick(2), hi], axis=1)
        r = dot(lhs, adj[t])
        pos = lax.broadcasted_iota(jnp.int32, (1, 128), 1) + t * 128
        return r * (pos < nvalid).astype(F32)

    def first(t):
        cols = slice((t + 1) * 128, (t + 2) * 128)
        vbuf[:, cols] = (w1m[:, cols] + diffuse(ubuf, t)).astype(BF)

    def second(t):
        cols = slice((t + 1) * 128, (t + 2) * 128)
        gsum[:, cols] = gsum[:, cols] + diffuse(vbuf, t)

    first(0)
    first(15)
    tile = lambda i: vbuf.at[:, pl.ds(i * 128, 128)]
    m_vh = [send(tile(1), tile(17), dleft), send(tile(16), tile(0), dright)]
    for t in range(1, 15):
        first(t)
    g_f[0].wait_recv()
    pg.append(same(gs(yh, q2), partner))
    g_f[1].wait_recv()
    pg.append(same(gs(yo, q2), partner))
    for t in range(1, 15):
        second(t)
    for m in m_vh:
        m.wait_recv()
    second(0)
    second(15)

    for m in pg:
        m.wait_recv()
    loc[2].wait()

    for s in range(16):
        parts = []
        for t in (2 * s, 2 * s + 1):
            lhs = jnp.concatenate([gall[ccols[k, t]] for k in range(2)], axis=1)
            parts.append(gall[t].astype(F32) + dot(lhs, ct[t]))
        gmix[s] = jnp.concatenate(parts, axis=1).astype(BF)

    eye = lax.broadcasted_iota(jnp.int32, (64, 64), 0) == lax.broadcasted_iota(
        jnp.int32, (64, 64), 1
    )
    column = lambda row: jnp.sum(jnp.where(eye, row, 0.0), axis=1, keepdims=True)
    bcol = [column(bias[g:g + 1, :]) for g in range(3)]
    win = [w_in[g].astype(F32) for g in range(3)]
    wcol = [[column(win[g][i:i + 1]) for i in range(2)] for g in range(3)]

    for n in range(8):
        cols = slice(n * 256, (n + 1) * 256)
        ecols = slice(n * 256 + 128, (n + 1) * 256 + 128)
        hi_n = cluster[:, cols] >> 8
        oh = ohlo[:, cols]
        acc = dot(gmix[0], oh)
        for s in range(1, 16):
            acc = jnp.where(hi_n == s, dot(gmix[s], oh), acc)
        pre = acc + gsum[:, ecols]
        xi = xin[:, cols].astype(F32)
        terms = [wcol[g][0] * xi[0:1] + wcol[g][1] * xi[1:2] + bcol[g] for g in range(3)]
        update = jax.nn.sigmoid(terms[0] + pre[0:64])
        reset = jax.nn.sigmoid(terms[1] + pre[64:128])
        cand = jnp.tanh(terms[2] + reset * pre[128:192])
        mk = (lax.broadcasted_iota(jnp.int32, (1, 256), 1) + n * 256 < nvalid).astype(F32)
        ms = state[:, cols].astype(F32) * mk
        out[:, cols] = ((update * ms + (1.0 - update) * cand) * mk).astype(BF)

    for m in msgs:
        m.wait_send()
    assert len(msgs) <= N_MSG


def body(
    state, inputs, adj_tiles, adj_cols, valid_rows, cluster_of, w_gates, w_input, bias, w_value,
    source_emb, target_emb, coarse_tiles, coarse_cols,
):
    vm = pl.BlockSpec(memory_space=pltpu.VMEM)
    sm = pl.BlockSpec(memory_space=pltpu.SMEM)
    hb = pl.BlockSpec(memory_space=pl.ANY)
    V = pltpu.VMEM
    return pl.pallas_call(
        kernel,
        out_shape=jax.ShapeDtypeStruct(state.shape, BF),
        in_specs=[vm, vm, hb, sm, sm, vm, hb, vm, vm, vm, hb, hb, hb, sm],
        out_specs=vm,
        scratch_shapes=[
            V((512, 2304), BF),
            V((8, 2, 64, 128), BF),
            V((256, 2048), BF),
            V((80, 2048), F32),
            V((640, 2048), BF),
            V((2, 4, 2, 80, 256), BF),
            V((4, 2, 80, 256), BF),
            V((4, 2, 80, 256), BF),
            V((3, 2, 80, 256), BF),
            V((2, 80, 256), BF),
            V((2, 80, 256), BF),
            V((16, 256), F32),
            V((16, 4096), F32),
            V((96, 4096), BF),
            V((96, 256), BF),
            V((4096, 256), F32),
            V((4096, 256), BF),
            V((8, 2, 64, 256), BF),
            V((2, 64, 256), F32),
            V((8, 64, 256), BF),
            V((32, 192, 128), BF),
            V((16, 192, 256), BF),
            V((192, 2304), BF),
            V((192, 2304), BF),
            V((192, 2304), F32),
            V((192, 2304), F32),
            V((16, 512, 128), BF),
            V((192, 4, 512), BF),
            V((768, 512), BF),
            V((32, 256, 128), BF),
            pltpu.SemaphoreType.DMA((N_MSG,)),
            pltpu.SemaphoreType.DMA((N_MSG,)),
            pltpu.SemaphoreType.DMA((23,)),
        ],
        compiler_params=pltpu.CompilerParams(collective_id=0, has_side_effects=True),
    )(
        state, inputs, adj_tiles.reshape(16, 512, 128), adj_cols.T, valid_rows,
        cluster_of.reshape(1, 2048), w_gates.reshape(192, 4, 512),
        jnp.transpose(w_input, (0, 2, 1)), bias, w_value.reshape(64, 64),
        jnp.transpose(source_emb, (1, 0, 2)), jnp.transpose(target_emb, (1, 0, 2)),
        coarse_tiles.reshape(32, 256, 128), coarse_cols.T,
    )


def solution(mesh):
    return jax.shard_map(
        body,
        mesh=mesh,
        in_specs=(
            P("feat", "dom"),
            P(None, "dom"),
            P("dom", None, None, None),
            P("dom", None),
            P("dom"),
            P("dom"),
            P(None, "feat", None, None),
            P(None, "feat", None),
            P(None, "feat"),
            P("feat", None, None),
            P("feat", None, None),
            P("feat", None, None),
            P(),
            P(),
        ),
        out_specs=P("feat", "dom"),
        check_vma=False,
    )
```

```python
import jax
import jax.numpy as jnp
from jax import lax
from jax.experimental import pallas as pl
from jax.experimental.pallas import tpu as pltpu
from jax.sharding import PartitionSpec as P

MESH = pl.DeviceIdType.MESH
BF = jnp.bfloat16
F32 = jnp.float32
N_MSG = 28


def dot(a, b, dims=((1,), (0,))):
    return lax.dot_general(a, b, (dims, ((), ())), preferred_element_type=F32)


def split3(v):
    a = v.astype(BF)
    r = v - a.astype(F32)
    b = r.astype(BF)
    c = (r - b.astype(F32)).astype(BF)
    return a, b, c


def split_counts(total):
    high = jnp.floor(total * (1.0 / 256.0)) * 256.0
    low = total - high
    row = lax.broadcasted_iota(jnp.int32, (16, total.shape[1]), 0)
    return jnp.where(row == 0, high, jnp.where(row == 1, low, 0.0))


def kernel(
    state, xin, adj_hbm, adj_cols, valid, cluster, wg_hbm, w_in, bias, w_val, src_hbm, tgt_hbm,
    ct_hbm, ccols, out_hbm,
    mext, ohlo, base, pl_lhs, pool, r1, s1, r2, s2, r3, src, tgt, t6, s6, scores, expo,
    vals, pooled, ca, gall0, gall1, gall2, gmix, ubuf, vbuf, w1m, gsum, out, adj, wraw, wg, ct,
    ssem, rsem, lsem,
):
    d = lax.axis_index("dom")
    f = lax.axis_index("feat")
    core, x, yh = d % 2, (d // 2) % 4, d // 8
    z, yl = f // 2, f % 2
    xp, xm, x2 = (x + 1) % 4, (x + 3) % 4, (x + 2) % 4
    zp, zm = (z + 1) % 4, (z + 3) % 4
    q, qp, qm, q2 = (i * 2 + core for i in (x, xp, xm, x2))
    dev = lambda i: (i, f)
    fdev = lambda i: (d, i)
    partner, yother = dev(d + 1 - 2 * core), dev((d + 8) % 16)
    dxp, dxm, dx2 = (dev(yh * 8 + i) for i in (qp, qm, q2))
    rq, rqp, rqm, rq2 = (i * 2 + 1 - core for i in (x, xp, xm, x2))
    pxp, pxm = (dev(yh * 8 + i) for i in (rqp, rqm))
    dleft, dright = dev((d + 15) % 16), dev((d + 1) % 16)
    fi = lambda a, b: a * 2 + b
    fy, fzp, fzm = f + 1 - 2 * yl, fi(zp, yl), fi(zm, yl)
    f_peers = [fdev((f + k) % 8) for k in range(1, 8)]

    groups = []

    class Group:
        def __init__(self, whole):
            self.whole, self.sems = whole, (ssem.at[len(groups)], rsem.at[len(groups)])
            groups.append(self)

        def copy(self, src_ref, dst_ref, to):
            return pltpu.make_async_remote_copy(
                src_ref=src_ref, dst_ref=dst_ref, send_sem=self.sems[0], recv_sem=self.sems[1],
                device_id=to, device_id_type=MESH,
            )

        def send(self, src_ref, dst_ref, to):
            self.copy(src_ref, dst_ref, to).start()

        def same(self, ref, *to):
            for i in to:
                self.send(ref, ref, i)

        def recv(self):
            self.copy(self.whole, self.whole, partner).wait_recv()

        def sent(self):
            self.copy(self.whole, self.whole, partner).wait_send()

    mine = pl.ds(pl.multiple_of(d * 256, 256), 256)
    loc = [
        pltpu.make_async_copy(wg_hbm, wraw, lsem.at[0]),
        pltpu.make_async_copy(adj_hbm, adj, lsem.at[1]),
        pltpu.make_async_copy(ct_hbm, ct, lsem.at[2]),
    ]
    emb = []
    for r in range(10):
        emb.append(pltpu.make_async_copy(tgt_hbm.at[r], tgt.at[pl.ds(r, 1)], lsem.at[3 + r]))
        emb.append(
            pltpu.make_async_copy(src_hbm.at[r, :, mine], src.at[pl.ds(r, 1)], lsem.at[13 + r])
        )
    for c in emb + loc:
        c.start()

    barrier = pltpu.get_barrier_semaphore()
    cross = dev((d + 15 + 2 * core) % 16)
    peers = [partner, cross, yother, dxp, dxm, dx2, pxp, pxm] + f_peers
    for p in peers:
        pl.semaphore_signal(barrier, inc=1, device_id=p, device_id_type=MESH)

    nvalid = valid[0]
    mask = (lax.broadcasted_iota(jnp.int32, (1, 2048), 1) < nvalid).astype(F32)
    masked32 = state[...].astype(F32) * mask
    myrows = pl.ds(pl.multiple_of(f * 64, 64), 64)
    own = pl.ds(128, 2048)
    mext[myrows, own] = masked32.astype(BF)
    base[0:64, :] = masked32
    row16 = lax.broadcasted_iota(jnp.int32, (16, 2048), 0)
    base[64:80, :] = jnp.where(row16 == 0, mask, 0.0)
    low = cluster[...] & 255
    high = cluster[...] >> 8
    ohlo[...] = (lax.broadcasted_iota(jnp.int32, (256, 2048), 0) == low).astype(F32).astype(BF)

    def pool_part(c, to_core):
        for xx in range(4):
            for yy in range(2):
                slot = xx * 2 + yy
                hit = high == (yy * 8 + xx * 2) + to_core
                pl_lhs[slot * 80:(slot + 1) * 80, :] = jnp.where(hit, base[...], 0.0).astype(BF)
        for i in range(2):
            res = dot(pl_lhs[i * 320:(i + 1) * 320, :], ohlo[...], ((1,), (1,)))
            for k in range(4):
                slot = i * 4 + k
                r = res[k * 80:(k + 1) * 80]
                pool[c, slot // 2, slot % 2] = jnp.concatenate(
                    [r[:64], split_counts(r[64:65])], axis=0
                ).astype(BF)

    pool_part(0, 1 - core)

    pl.semaphore_wait(barrier, len(peers))

    m_r1 = Group(r1)
    m_r1.send(pool.at[0], r1, partner)
    m_h = Group(mext.at[0:64, 0:256])
    m_h.send(mext.at[myrows, pl.ds(128, 128)], mext.at[myrows, pl.ds(2176, 128)], dleft)
    m_h.send(mext.at[myrows, pl.ds(2048, 128)], mext.at[myrows, pl.ds(0, 128)], dright)
    pool_part(1, core)

    for c in emb:
        c.wait()
    t6[...] = jnp.zeros_like(t6)
    s6[...] = jnp.zeros_like(s6)
    ta, tb, tc = split3(tgt[0:10, :])
    sa, sb, sc = split3(src[0:10, :])
    for k, (t, s) in enumerate([(ta, sa), (ta, sb), (tb, sa), (ta, sc), (tb, sb), (tc, sa)]):
        t6[k * 16:k * 16 + 10, :] = t
        s6[k * 16:k * 16 + 10, :] = s

    def score_step(j, peak):
        cols = pl.ds(pl.multiple_of(j * 512, 512), 512)
        s = jnp.maximum(dot(t6[:, cols], s6[...], ((0,), (0,))), 0.0)
        scores[cols, :] = s
        return jnp.maximum(peak, jnp.max(s.reshape(64, 8, 256), axis=0))

    def add_blocks(blocks):
        total = blocks[0][...].astype(F32)
        for b in blocks[1:]:
            total = total + b[...].astype(F32)
        return total[:64], total[64:65] + total[65:66]

    def packed(sums, cnt):
        return jnp.concatenate([sums, split_counts(cnt)], axis=0).astype(BF)

    m_r1.recv()
    for xx in range(4):
        for yy in range(2):
            s1[xx, yy] = packed(*add_blocks([pool.at[1, xx, yy], r1.at[xx, yy]]))
    m_r2 = Group(r2)
    m_r2.send(s1.at[x2], r2.at[2], dx2)
    m_r2.send(s1.at[xp], r2.at[0], dxp)
    m_r2.send(s1.at[xm], r2.at[1], dxm)

    peak = lax.fori_loop(0, 4, score_step, jnp.zeros((8, 256), F32))
    m_h.recv()
    mrow = lambda i: mext.at[pl.ds(pl.multiple_of(i * 64, 64), 64), :]
    mhalf = lambda i, h: mext.at[pl.ds(pl.multiple_of(i * 64 + h * 32, 32), 32), :]
    st_y, st_z = Group(mext.at[0:64]), Group(mext.at[0:128])
    st_y.same(mrow(f), fdev(fy))
    st_z.same(mrow(f), fdev(fzp), fdev(fzm))
    peak = lax.fori_loop(4, 8, score_step, peak)
    peak = jnp.max(peak, axis=0, keepdims=True)

    def exp_step(j, total):
        cols = pl.ds(pl.multiple_of(j * 512, 512), 512)
        e = jnp.exp(scores[cols, :] - peak)
        expo[cols, :] = e.astype(BF)
        return total + jnp.sum(e.reshape(64, 8, 256), axis=0)

    total = lax.fori_loop(0, 8, exp_step, jnp.zeros((8, 256), F32))
    inv = 1.0 / jnp.sum(total, axis=0, keepdims=True)

    m_r2.recv()
    for yy in range(2):
        s2[yy] = packed(*add_blocks([s1.at[x, yy]] + [r2.at[k, yy] for k in range(3)]))
    m_r3 = Group(s2)
    m_r3.send(s2, r3, yother)

    st_y.recv()
    st_yz = Group(mext.at[0:128])
    st_yz.same(mrow(fy), fdev(fzp), fdev(fzm))
    loc[0].wait()
    for k in range(4):
        wg[k * 192:(k + 1) * 192, :] = wraw[:, k, :]
    m_r3.recv()
    wv = w_val[...]
    for yy in range(2):
        sums, cnt = add_blocks([s2.at[yy], r3.at[yy]])
        avg = sums / jnp.maximum(cnt, 1.0)
        pooled[yy] = avg
        pa, pb, pc = split3(avg)
        vals[q, yy] = (dot(wv, pa) + dot(wv, pb) + dot(wv, pc)).astype(BF)

    m_v, m_pv = Group(vals.at[0:2]), Group(vals.at[0:3])
    m_v.same(vals.at[q], dxp, dxm)
    m_pv.same(vals.at[q], partner)

    def attend(total, i, halves=(0, 1)):
        for yy in halves:
            rows = pl.ds(pl.multiple_of((yy * 8 + i) * 256, 256), 256)
            total = total + dot(vals[i, yy], expo[rows, :])
        return total

    att = attend(jnp.zeros((64, 256), F32), q)
    st_z.recv()
    st_far = Group(mext.at[0:128])
    st_far.same(mhalf(fzm, 0), fdev(fzp))
    st_far.same(mhalf(fzp, 1), fdev(fzm))
    m_v.recv()
    m_far = Group(vals.at[0:2])
    m_far.same(vals.at[qm, 0], dxp, pxp)
    m_far.same(vals.at[qp, 1], dxm, pxm)
    m_pv.same(vals.at[qm], partner)
    m_pv.same(vals.at[qp], partner)
    att = attend(attend(att, qm), qp)
    m_pv.recv()
    for i in (rq, rqm, rqp):
        att = attend(att, i)
    st_yz.recv()
    st_far.same(mhalf(fi(zm, 1 - yl), 0), fdev(fzp))
    st_far.same(mhalf(fi(zp, 1 - yl), 1), fdev(fzm))
    m_far.recv()
    att = attend(attend(att, q2), rq2)
    ca[f] = (pooled[yh] + att * inv).astype(BF)
    m_ca = Group(ca.at[0:7])
    m_ca.same(ca.at[f], *f_peers)

    st_far.recv()
    for c in range(9):
        cols = slice(c * 256, (c + 1) * 256)
        r = dot(wg[0:576, :], mext[:, cols])
        gsum[:, cols] = r[0:192]
        w1m[:, cols] = r[192:384]
        ubuf[:, cols] = r[384:576].astype(BF)

    loc[1].wait()

    def diffuse(buf, t):
        lo, mid, hi = (buf[:, (t + k) * 128:(t + k + 1) * 128] for k in range(3))

        def pick(k):
            c = jnp.full((1, 128), adj_cols[k, t], jnp.int32)
            wlo, wmid, whi = ((c == t + i).astype(F32).astype(BF) for i in range(3))
            return lo * wlo + mid * wmid + hi * whi

        lhs = jnp.concatenate([lo, pick(1), pick(2), hi], axis=1)
        r = dot(lhs, adj[t])
        pos = lax.broadcasted_iota(jnp.int32, (1, 128), 1) + t * 128
        return r * (pos < nvalid).astype(F32)

    def first(t):
        cols = slice((t + 1) * 128, (t + 2) * 128)
        vbuf[:, cols] = (w1m[:, cols] + diffuse(ubuf, t)).astype(BF)

    def second(t):
        cols = slice((t + 1) * 128, (t + 2) * 128)
        gsum[:, cols] = gsum[:, cols] + diffuse(vbuf, t)

    first(0)
    first(15)
    tile = lambda i: vbuf.at[:, pl.ds(i * 128, 128)]
    m_vh = Group(vbuf.at[:, 0:256])
    m_vh.send(tile(1), tile(17), dleft)
    m_vh.send(tile(16), tile(0), dright)
    for t in range(1, 15):
        first(t)
    m_ca.recv()
    early = list(groups)
    gall = (gall0, gall1, gall2)
    slot = lambda g, a, b: gall[g].at[pl.ds(2 * (a * 8 + b), 2)]
    yo = 1 - yh
    several = lambda n: [Group(gall[g].at[0:2 * n]) for g in range(3)]
    g_x, g_y, g_b, g_f, g_p = several(2), several(1), several(2), several(2), several(8)
    for g in range(3):
        r = dot(wg[576 + g * 64:640 + g * 64, :], ca[...].reshape(512, 256)).astype(BF)
        gall[g][2 * d] = r[:, :128]
        gall[g][2 * d + 1] = r[:, 128:]
        g_y[g].same(slot(g, yh, q), yother)
        g_x[g].same(slot(g, yh, q), dxp, dxm)
        g_p[g].same(slot(g, yh, q), partner)

    for t in range(1, 15):
        second(t)
    for g in range(3):
        g_x[g].recv()
        g_f[g].same(slot(g, yh, qm), dxp)
        g_p[g].same(slot(g, yh, qm), partner)
        g_p[g].same(slot(g, yh, qp), partner)

    def pass_y(g):
        g_y[g].recv()
        g_b[g].same(slot(g, yo, q), dxp, dxm)
        g_p[g].same(slot(g, yo, q), partner)

    def pass_b(g):
        g_b[g].recv()
        g_f[g].same(slot(g, yo, qp), dxm)
        g_p[g].same(slot(g, yo, qp), partner)
        g_p[g].same(slot(g, yo, qm), partner)

    def pass_f(g):
        g_f[g].recv()
        g_p[g].same(slot(g, yh, q2), partner)
        g_p[g].same(slot(g, yo, q2), partner)

    pass_y(0)
    m_vh.recv()
    second(0)
    second(15)
    pass_y(1)
    for m in early:
        m.sent()
    loc[2].wait()
    eye = lax.broadcasted_iota(jnp.int32, (64, 64), 0) == lax.broadcasted_iota(
        jnp.int32, (64, 64), 1
    )
    column = lambda row: jnp.sum(jnp.where(eye, row, 0.0), axis=1, keepdims=True)
    bcol = [column(bias[g:g + 1, :]) for g in range(3)]
    win = [w_in[g].astype(F32) for g in range(3)]
    wcol = [[column(win[g][i:i + 1]) for i in range(2)] for g in range(3)]

    def unpool(g):
        g_p[g].recv()
        for s in range(16):
            parts = []
            for t in (2 * s, 2 * s + 1):
                lhs = jnp.concatenate([gall[g][ccols[k, t]] for k in range(2)], axis=1)
                parts.append(gall[g][t].astype(F32) + dot(lhs, ct[t]))
            gmix[s] = jnp.concatenate(parts, axis=1).astype(BF)
        if g < 2:
            pass_f(g + 1)
        rows = slice(g * 64, (g + 1) * 64)
        for n in range(8):
            cols = slice(n * 256, (n + 1) * 256)
            ecols = slice(n * 256 + 128, (n + 1) * 256 + 128)
            hi_n = cluster[:, cols] >> 8
            r = dot(gmix[...].reshape(1024, 256), ohlo[:, cols])
            acc = r[0:64]
            for s in range(1, 16):
                acc = jnp.where(hi_n == s, r[s * 64:(s + 1) * 64], acc)
            pre = acc + gsum[rows, ecols]
            xi = xin[:, cols].astype(F32)
            terms = wcol[g][0] * xi[0:1] + wcol[g][1] * xi[1:2] + bcol[g]
            if g < 2:
                gsum[rows, ecols] = jax.nn.sigmoid(terms + pre)
                continue
            update, reset = gsum[0:64, ecols], gsum[64:128, ecols]
            cand = jnp.tanh(terms + reset * pre)
            mk = (lax.broadcasted_iota(jnp.int32, (1, 256), 1) + n * 256 < nvalid).astype(F32)
            ms = state[:, cols].astype(F32) * mk
            out[:, cols] = ((update * ms + (1.0 - update) * cand) * mk).astype(BF)
            cp = pltpu.make_async_copy(out.at[:, cols], out_hbm.at[:, cols], lsem.at[23])
            cp.start()

    pass_b(0)
    pass_y(2)
    pass_b(1)
    pass_f(0)
    pass_b(2)
    unpool(0)
    unpool(1)
    unpool(2)

    for m in groups[len(early):]:
        m.sent()
    pltpu.make_async_copy(out, out_hbm, lsem.at[23]).wait()
    assert len(groups) == N_MSG


def body(
    state, inputs, adj_tiles, adj_cols, valid_rows, cluster_of, w_gates, w_input, bias, w_value,
    source_emb, target_emb, coarse_tiles, coarse_cols,
):
    vm = pl.BlockSpec(memory_space=pltpu.VMEM)
    sm = pl.BlockSpec(memory_space=pltpu.SMEM)
    hb = pl.BlockSpec(memory_space=pl.ANY)
    V = pltpu.VMEM
    return pl.pallas_call(
        kernel,
        out_shape=jax.ShapeDtypeStruct(state.shape, BF),
        in_specs=[vm, vm, hb, sm, sm, vm, hb, vm, vm, vm, hb, hb, hb, sm],
        out_specs=hb,
        scratch_shapes=[
            V((512, 2304), BF),
            V((256, 2048), BF),
            V((80, 2048), F32),
            V((640, 2048), BF),
            V((2, 4, 2, 80, 256), BF),
            V((4, 2, 80, 256), BF),
            V((4, 2, 80, 256), BF),
            V((3, 2, 80, 256), BF),
            V((2, 80, 256), BF),
            V((2, 80, 256), BF),
            V((16, 256), F32),
            V((16, 4096), F32),
            V((96, 4096), BF),
            V((96, 256), BF),
            V((4096, 256), F32),
            V((4096, 256), BF),
            V((8, 2, 64, 256), BF),
            V((2, 64, 256), F32),
            V((8, 64, 256), BF),
            V((32, 64, 128), BF),
            V((32, 64, 128), BF),
            V((32, 64, 128), BF),
            V((16, 64, 256), BF),
            V((192, 2304), BF),
            V((192, 2304), BF),
            V((192, 2304), F32),
            V((192, 2304), F32),
            V((64, 2048), BF),
            V((16, 512, 128), BF),
            V((192, 4, 512), BF),
            V((768, 512), BF),
            V((32, 256, 128), BF),
            pltpu.SemaphoreType.DMA((N_MSG,)),
            pltpu.SemaphoreType.DMA((N_MSG,)),
            pltpu.SemaphoreType.DMA((24,)),
        ],
        compiler_params=pltpu.CompilerParams(collective_id=0, has_side_effects=True),
    )(
        state, inputs, adj_tiles.reshape(16, 512, 128), adj_cols.T, valid_rows,
        cluster_of.reshape(1, 2048), w_gates.reshape(192, 4, 512),
        jnp.transpose(w_input, (0, 2, 1)), bias, w_value.reshape(64, 64),
        jnp.transpose(source_emb, (1, 0, 2)), jnp.transpose(target_emb, (1, 0, 2)),
        coarse_tiles.reshape(32, 256, 128), coarse_cols.T,
    )


def solution(mesh):
    return jax.shard_map(
        body,
        mesh=mesh,
        in_specs=(
            P("feat", "dom"),
            P(None, "dom"),
            P("dom", None, None, None),
            P("dom", None),
            P("dom"),
            P("dom"),
            P(None, "feat", None, None),
            P(None, "feat", None),
            P(None, "feat"),
            P("feat", None, None),
            P("feat", None, None),
            P("feat", None, None),
            P(),
            P(),
        ),
        out_specs=P("feat", "dom"),
        check_vma=False,
    )
```

```python
import jax
import jax.numpy as jnp
from jax import lax
from jax.experimental import pallas as pl
from jax.experimental.pallas import tpu as pltpu
from jax.sharding import PartitionSpec as P

MESH = pl.DeviceIdType.MESH
BF = jnp.bfloat16
F32 = jnp.float32
N_MSG = 21


def dot(a, b, dims=((1,), (0,))):
    return lax.dot_general(a, b, (dims, ((), ())), preferred_element_type=F32)


def split3(v):
    a = v.astype(BF)
    r = v - a.astype(F32)
    b = r.astype(BF)
    c = (r - b.astype(F32)).astype(BF)
    return a, b, c


def kernel(
    state, xin, adj_hbm, adj_cols, valid, cluster, wg_hbm, w_in, bias, w_val, src_hbm, tgt_hbm,
    ct_hbm, ccols, out_hbm,
    mext, ohlo, base, pl_lhs, pool, pcnt, r1, c1, s1, s1cnt, rs, rscnt, src, tgt, t6, s6, scores, expo,
    vals, ca, gall0, gall1, gall2, gmix, ubuf, vbuf, w1m, gsum, out, adj, wraw, wg, ct,
    ssem, rsem, lsem,
):
    d = lax.axis_index("dom")
    f = lax.axis_index("feat")
    core, x, yh = d % 2, (d // 2) % 4, d // 8
    z, yl = f // 2, f % 2
    zp, zm = (z + 1) % 4, (z + 3) % 4
    dev = lambda i: (i, f)
    fdev = lambda i: (d, i)
    partner = dev(d + 1 - 2 * core)
    hops = [(2, 1), (1, 1), (3, 1), (2, 0), (0, 1), (1, 0), (3, 0)]
    chip = lambda a, b: ((yh + b) % 2) * 8 + ((x + a) % 4) * 2
    chips = [dev(chip(a, b) + core) for a, b in hops]
    dleft, dright = dev((d + 15) % 16), dev((d + 1) % 16)
    fi = lambda a, b: a * 2 + b
    fy, fzp, fzm = f + 1 - 2 * yl, fi(zp, yl), fi(zm, yl)
    f_peers = [fdev((f + k) % 8) for k in range(1, 8)]

    groups = []

    class Group:
        def __init__(self, whole):
            self.whole, self.sems = whole, (ssem.at[len(groups)], rsem.at[len(groups)])
            groups.append(self)

        def copy(self, src_ref, dst_ref, to):
            return pltpu.make_async_remote_copy(
                src_ref=src_ref, dst_ref=dst_ref, send_sem=self.sems[0], recv_sem=self.sems[1],
                device_id=to, device_id_type=MESH,
            )

        def send(self, src_ref, dst_ref, to):
            self.copy(src_ref, dst_ref, to).start()

        def same(self, ref, *to):
            for i in to:
                self.send(ref, ref, i)

        def recv(self):
            self.copy(self.whole, self.whole, partner).wait_recv()

        def sent(self):
            self.copy(self.whole, self.whole, partner).wait_send()

    mine = pl.ds(pl.multiple_of(d * 256, 256), 256)
    loc = [
        pltpu.make_async_copy(wg_hbm, wraw, lsem.at[0]),
        pltpu.make_async_copy(adj_hbm, adj, lsem.at[1]),
        pltpu.make_async_copy(ct_hbm, ct, lsem.at[2]),
    ]
    emb = []
    for r in range(10):
        emb.append(pltpu.make_async_copy(tgt_hbm.at[r], tgt.at[pl.ds(r, 1)], lsem.at[3 + r]))
        emb.append(
            pltpu.make_async_copy(src_hbm.at[r, :, mine], src.at[pl.ds(r, 1)], lsem.at[13 + r])
        )
    for c in emb + loc:
        c.start()

    barrier = pltpu.get_barrier_semaphore()
    cross = dev((d + 15 + 2 * core) % 16)
    peers = [partner, cross] + chips + f_peers
    for p in peers:
        pl.semaphore_signal(barrier, inc=1, device_id=p, device_id_type=MESH)

    nvalid = valid[0]
    mask = (lax.broadcasted_iota(jnp.int32, (1, 2048), 1) < nvalid).astype(F32)
    masked32 = state[...].astype(F32) * mask
    myrows = pl.ds(pl.multiple_of(f * 64, 64), 64)
    own = pl.ds(128, 2048)
    mext[myrows, own] = masked32.astype(BF)
    base[...] = masked32
    row16 = lax.broadcasted_iota(jnp.int32, (16, 2048), 0)
    low = cluster[...] & 255
    high = cluster[...] >> 8
    ohlo[...] = (lax.broadcasted_iota(jnp.int32, (256, 2048), 0) == low).astype(F32).astype(BF)

    row8 = lax.broadcasted_iota(jnp.int32, (8, 2048), 0)
    row_high = (row8 & 1) * 8 + (row8 >> 1) * 2

    def pool_part(c, to_core):
        for xx in range(4):
            for yy in range(2):
                slot = xx * 2 + yy
                hit = high == (yy * 8 + xx * 2) + to_core
                pl_lhs[slot * 64:(slot + 1) * 64, :] = jnp.where(hit, base[...], 0.0).astype(BF)
        for i in range(2):
            res = dot(pl_lhs[i * 256:(i + 1) * 256, :], ohlo[...], ((1,), (1,))).astype(BF)
            for k in range(4):
                slot = i * 4 + k
                pool[c, slot // 2, slot % 2] = res[k * 64:(k + 1) * 64]
        lhs = jnp.where(high == row_high + to_core, mask, 0.0).astype(BF)
        pcnt[c] = dot(lhs, ohlo[...], ((1,), (1,)))

    pool_part(0, 1 - core)

    pl.semaphore_wait(barrier, len(peers))

    m_r1, m_c1 = Group(r1), Group(c1)
    m_r1.send(pool.at[0], r1, partner)
    m_c1.send(pcnt.at[0], c1, partner)
    mrow = lambda i, cols: mext.at[pl.ds(pl.multiple_of(i * 64, 64), 64), cols]
    mhalf = lambda i, h: mext.at[pl.ds(pl.multiple_of(i * 64 + h * 32, 32), 32), :]
    all_cols, left, right = pl.ds(0, 2304), pl.ds(0, 128), pl.ds(2176, 128)
    m_h = Group(mext.at[0:64, 0:256])
    m_h.send(mrow(f, pl.ds(128, 128)), mrow(f, right), dleft)
    m_h.send(mrow(f, pl.ds(2048, 128)), mrow(f, left), dright)
    st_y, st_z = Group(mext.at[0:64]), Group(mext.at[0:128])
    st_y.same(mrow(f, own), fdev(fy))
    st_z.same(mrow(f, own), fdev(fzp), fdev(fzm))
    pool_part(1, core)

    for c in emb:
        c.wait()
    t6[...] = jnp.zeros_like(t6)
    s6[...] = jnp.zeros_like(s6)
    ta, tb, tc = split3(tgt[0:10, :])
    sa, sb, sc = split3(src[0:10, :])
    for k, (t, s) in enumerate([(ta, sa), (ta, sb), (tb, sa), (ta, sc), (tb, sb), (tc, sa)]):
        t6[k * 16:k * 16 + 10, :] = t
        s6[k * 16:k * 16 + 10, :] = s

    def score_step(j, peak):
        cols = pl.ds(pl.multiple_of(j * 512, 512), 512)
        s = jnp.maximum(dot(t6[:, cols], s6[...], ((0,), (0,))), 0.0)
        scores[cols, :] = s
        return jnp.maximum(peak, jnp.max(s.reshape(64, 8, 256), axis=0))

    m_r1.recv()
    m_c1.recv()
    s1[...] = (pool[1].astype(F32) + r1[...].astype(F32)).astype(BF)
    s1cnt[...] = pcnt[1] + c1[...]
    m_rs, m_rc = Group(rs.at[0:7]), Group(rscnt.at[0:7])
    for k, (a, b) in enumerate(hops):
        xx, yy = (x + a) % 4, (yh + b) % 2
        m_rs.send(s1.at[xx, yy], rs.at[k], chips[k])
        m_rc.send(s1cnt.at[pl.ds(xx * 2 + yy, 1)], rscnt.at[k], chips[k])

    peak = lax.fori_loop(0, 4, score_step, jnp.zeros((8, 256), F32))
    m_h.recv()
    for cols in (left, right):
        st_y.same(mrow(f, cols), fdev(fy))
        st_z.same(mrow(f, cols), fdev(fzp), fdev(fzm))
    peak = lax.fori_loop(4, 8, score_step, peak)
    peak = jnp.max(peak, axis=0, keepdims=True)

    def exp_step(j, total):
        cols = pl.ds(pl.multiple_of(j * 512, 512), 512)
        e = jnp.exp(scores[cols, :] - peak)
        expo[cols, :] = e.astype(BF)
        return total + jnp.sum(e.reshape(64, 8, 256), axis=0)

    total = lax.fori_loop(0, 8, exp_step, jnp.zeros((8, 256), F32))
    inv = 1.0 / jnp.sum(total, axis=0, keepdims=True)

    st_y.recv()
    st_yz = Group(mext.at[0:128])
    st_yz.same(mrow(fy, all_cols), fdev(fzp), fdev(fzm))
    st_z.recv()
    st_far = Group(mext.at[0:128])
    st_far.same(mhalf(fzm, 0), fdev(fzp))
    st_far.same(mhalf(fzp, 1), fdev(fzm))
    m_rs.recv()
    m_rc.recv()
    sums, cnt = s1[x, yh].astype(F32), s1cnt[pl.ds(x * 2 + yh, 1), :]
    for k in range(7):
        sums = sums + rs[k].astype(F32)
        cnt = cnt + rscnt[k]
    pooled = sums / jnp.maximum(cnt, 1.0)
    pa, pb, pc = split3(pooled)
    wv = w_val[...]
    vals[d] = (dot(wv, pa) + dot(wv, pb) + dot(wv, pc)).astype(BF)

    near, far = Group(vals.at[0:4]), Group(vals.at[0:3])
    for k in range(7):
        (far if k < 3 else near).same(vals.at[d], chips[k])
    swap_near, swap_far = Group(vals.at[0:5]), Group(vals.at[0:3])
    swap_near.same(vals.at[d], partner)

    loc[0].wait()
    for k in range(4):
        wg[k * 192:(k + 1) * 192, :] = wraw[:, k, :]

    def attend(total, slots):
        for i in slots:
            rows = pl.ds(pl.multiple_of(i * 256, 256), 256)
            total = total + dot(vals[i], expo[rows, :])
        return total

    mine_of = lambda ks, c: [chip(*hops[k]) + c for k in ks]
    near.recv()
    for i in mine_of(range(3, 7), core):
        swap_near.same(vals.at[i], partner)
    att = attend(jnp.zeros((64, 256), F32), [d] + mine_of(range(3, 7), core))
    far.recv()
    for i in mine_of(range(3), core):
        swap_far.same(vals.at[i], partner)
    swap_near.recv()
    att = attend(att, mine_of(range(3), core) + [chip(0, 0) + 1 - core])
    att = attend(att, mine_of(range(3, 7), 1 - core))
    st_yz.recv()
    swap_far.recv()
    att = attend(att, mine_of(range(3), 1 - core))
    ca[f] = (pooled + att * inv).astype(BF)
    m_ca = Group(ca.at[0:7])
    m_ca.same(ca.at[f], *f_peers)
    st_far.same(mhalf(fi(zm, 1 - yl), 0), fdev(fzp))
    st_far.same(mhalf(fi(zp, 1 - yl), 1), fdev(fzm))

    st_far.recv()
    for c in range(9):
        cols = slice(c * 256, (c + 1) * 256)
        r = dot(wg[0:576, :], mext[:, cols])
        gsum[:, cols] = r[0:192]
        w1m[:, cols] = r[192:384]
        ubuf[:, cols] = r[384:576].astype(BF)

    loc[1].wait()

    def diffuse(buf, t):
        lo, mid, hi = (buf[:, (t + k) * 128:(t + k + 1) * 128] for k in range(3))

        def pick(k):
            c = jnp.full((1, 128), adj_cols[k, t], jnp.int32)
            wlo, wmid, whi = ((c == t + i).astype(F32).astype(BF) for i in range(3))
            return lo * wlo + mid * wmid + hi * whi

        lhs = jnp.concatenate([lo, pick(1), pick(2), hi], axis=1)
        r = dot(lhs, adj[t])
        pos = lax.broadcasted_iota(jnp.int32, (1, 128), 1) + t * 128
        return r * (pos < nvalid).astype(F32)

    def first(t):
        cols = slice((t + 1) * 128, (t + 2) * 128)
        vbuf[:, cols] = (w1m[:, cols] + diffuse(ubuf, t)).astype(BF)

    def second(t):
        cols = slice((t + 1) * 128, (t + 2) * 128)
        gsum[:, cols] = gsum[:, cols] + diffuse(vbuf, t)

    first(0)
    first(15)
    tile = lambda i: vbuf.at[:, pl.ds(i * 128, 128)]
    m_vh = Group(vbuf.at[:, 0:256])
    m_vh.send(tile(1), tile(17), dleft)
    m_vh.send(tile(16), tile(0), dright)
    for t in range(1, 15):
        first(t)
    m_ca.recv()
    early = list(groups)
    gall = (gall0, gall1, gall2)
    slot = lambda g, i: gall[g].at[pl.ds(2 * i, 2)]
    several = lambda n: [Group(gall[g].at[0:2 * n]) for g in range(3)]
    g_x, g_p = several(7), several(8)
    for g in range(3):
        r = dot(wg[576 + g * 64:640 + g * 64, :], ca[...].reshape(512, 256)).astype(BF)
        gall[g][2 * d] = r[:, :128]
        gall[g][2 * d + 1] = r[:, 128:]
        g_x[g].same(slot(g, d), *chips)
        g_p[g].same(slot(g, d), partner)

    for t in range(1, 15):
        second(t)
    def swap(g):
        g_x[g].recv()
        for i in mine_of(range(7), core):
            g_p[g].same(slot(g, i), partner)

    m_vh.recv()
    second(0)
    second(15)
    for m in early:
        m.sent()
    loc[2].wait()
    eye = lax.broadcasted_iota(jnp.int32, (64, 64), 0) == lax.broadcasted_iota(
        jnp.int32, (64, 64), 1
    )
    column = lambda row: jnp.sum(jnp.where(eye, row, 0.0), axis=1, keepdims=True)
    bcol = [column(bias[g:g + 1, :]) for g in range(3)]
    win = [w_in[g].astype(F32) for g in range(3)]
    wcol = [[column(win[g][i:i + 1]) for i in range(2)] for g in range(3)]

    def unpool(g):
        g_p[g].recv()
        for s in range(16):
            parts = []
            for t in (2 * s, 2 * s + 1):
                lhs = jnp.concatenate([gall[g][ccols[k, t]] for k in range(2)], axis=1)
                parts.append(gall[g][t].astype(F32) + dot(lhs, ct[t]))
            gmix[s] = jnp.concatenate(parts, axis=1).astype(BF)
        if g < 2:
            swap(g + 1)
        rows = slice(g * 64, (g + 1) * 64)
        for n in range(8):
            cols = slice(n * 256, (n + 1) * 256)
            ecols = slice(n * 256 + 128, (n + 1) * 256 + 128)
            hi_n = cluster[:, cols] >> 8
            r = dot(gmix[...].reshape(1024, 256), ohlo[:, cols])
            acc = r[0:64]
            for s in range(1, 16):
                acc = jnp.where(hi_n == s, r[s * 64:(s + 1) * 64], acc)
            pre = acc + gsum[rows, ecols]
            xi = xin[:, cols].astype(F32)
            terms = wcol[g][0] * xi[0:1] + wcol[g][1] * xi[1:2] + bcol[g]
            if g < 2:
                gsum[rows, ecols] = jax.nn.sigmoid(terms + pre)
                continue
            update, reset = gsum[0:64, ecols], gsum[64:128, ecols]
            cand = jnp.tanh(terms + reset * pre)
            mk = (lax.broadcasted_iota(jnp.int32, (1, 256), 1) + n * 256 < nvalid).astype(F32)
            ms = state[:, cols].astype(F32) * mk
            out[:, cols] = ((update * ms + (1.0 - update) * cand) * mk).astype(BF)
            cp = pltpu.make_async_copy(out.at[:, cols], out_hbm.at[:, cols], lsem.at[23])
            cp.start()

    swap(0)
    unpool(0)
    unpool(1)
    unpool(2)

    for m in groups[len(early):]:
        m.sent()
    pltpu.make_async_copy(out, out_hbm, lsem.at[23]).wait()
    assert len(groups) == N_MSG


def body(
    state, inputs, adj_tiles, adj_cols, valid_rows, cluster_of, w_gates, w_input, bias, w_value,
    source_emb, target_emb, coarse_tiles, coarse_cols,
):
    vm = pl.BlockSpec(memory_space=pltpu.VMEM)
    sm = pl.BlockSpec(memory_space=pltpu.SMEM)
    hb = pl.BlockSpec(memory_space=pl.ANY)
    V = pltpu.VMEM
    return pl.pallas_call(
        kernel,
        out_shape=jax.ShapeDtypeStruct(state.shape, BF),
        in_specs=[vm, vm, hb, sm, sm, vm, hb, vm, vm, vm, hb, hb, hb, sm],
        out_specs=hb,
        scratch_shapes=[
            V((512, 2304), BF),
            V((256, 2048), BF),
            V((64, 2048), F32),
            V((512, 2048), BF),
            V((2, 4, 2, 64, 256), BF),
            V((2, 8, 256), F32),
            V((4, 2, 64, 256), BF),
            V((8, 256), F32),
            V((4, 2, 64, 256), BF),
            V((8, 256), F32),
            V((7, 64, 256), BF),
            V((7, 1, 256), F32),
            V((16, 256), F32),
            V((16, 4096), F32),
            V((96, 4096), BF),
            V((96, 256), BF),
            V((4096, 256), F32),
            V((4096, 256), BF),
            V((16, 64, 256), BF),
            V((8, 64, 256), BF),
            V((32, 64, 128), BF),
            V((32, 64, 128), BF),
            V((32, 64, 128), BF),
            V((16, 64, 256), BF),
            V((192, 2304), BF),
            V((192, 2304), BF),
            V((192, 2304), F32),
            V((192, 2304), F32),
            V((64, 2048), BF),
            V((16, 512, 128), BF),
            V((192, 4, 512), BF),
            V((768, 512), BF),
            V((32, 256, 128), BF),
            pltpu.SemaphoreType.DMA((N_MSG,)),
            pltpu.SemaphoreType.DMA((N_MSG,)),
            pltpu.SemaphoreType.DMA((24,)),
        ],
        compiler_params=pltpu.CompilerParams(collective_id=0, has_side_effects=True),
    )(
        state, inputs, adj_tiles.reshape(16, 512, 128), adj_cols.T, valid_rows,
        cluster_of.reshape(1, 2048), w_gates.reshape(192, 4, 512),
        jnp.transpose(w_input, (0, 2, 1)), bias, w_value.reshape(64, 64),
        jnp.transpose(source_emb, (1, 0, 2)), jnp.transpose(target_emb, (1, 0, 2)),
        coarse_tiles.reshape(32, 256, 128), coarse_cols.T,
    )


def solution(mesh):
    return jax.shard_map(
        body,
        mesh=mesh,
        in_specs=(
            P("feat", "dom"),
            P(None, "dom"),
            P("dom", None, None, None),
            P("dom", None),
            P("dom"),
            P("dom"),
            P(None, "feat", None, None),
            P(None, "feat", None),
            P(None, "feat"),
            P("feat", None, None),
            P("feat", None, None),
            P("feat", None, None),
            P(),
            P(),
        ),
        out_specs=P("feat", "dom"),
        check_vma=False,
    )
```

```python
import jax
import jax.numpy as jnp
from jax import lax
from jax.experimental import pallas as pl
from jax.experimental.pallas import tpu as pltpu
from jax.sharding import PartitionSpec as P

MESH = pl.DeviceIdType.MESH
BF = jnp.bfloat16
F32 = jnp.float32
N_MSG = 24


def dot(a, b, dims=((1,), (0,))):
    return lax.dot_general(a, b, (dims, ((), ())), preferred_element_type=F32)


def split3(v):
    a = v.astype(BF)
    r = v - a.astype(F32)
    b = r.astype(BF)
    c = (r - b.astype(F32)).astype(BF)
    return a, b, c


def kernel(
    state, xin, adj_hbm, adj_cols, valid, cluster, wg_hbm, w_in, bias, w_val, src_hbm, tgt_hbm,
    ct_hbm, ccols, out_hbm,
    mext, halo, ohlo, base, pl_lhs, pool, pcnt, r1, c1, s1, s1cnt, rs, rscnt, src, tgt, t6, s6, scores, expo,
    vals, ca, gall0, gall1, gall2, gmix, ubuf, vbuf, w1m, gsum, out, adj, wraw, wg, ct,
    ssem, rsem, lsem,
):
    d = lax.axis_index("dom")
    f = lax.axis_index("feat")
    core, x, yh = d % 2, (d // 2) % 4, d // 8
    z, yl = f // 2, f % 2
    zp, zm = (z + 1) % 4, (z + 3) % 4
    dev = lambda i: (i, f)
    fdev = lambda i: (d, i)
    partner = dev(d + 1 - 2 * core)
    hops = [(2, 1), (1, 1), (3, 1), (2, 0), (0, 1), (1, 0), (3, 0)]
    chip = lambda a, b: ((yh + b) % 2) * 8 + ((x + a) % 4) * 2
    chips = [dev(chip(a, b) + core) for a, b in hops]
    dleft, dright = dev((d + 15) % 16), dev((d + 1) % 16)
    fi = lambda a, b: a * 2 + b
    fy, fzp, fzm = f + 1 - 2 * yl, fi(zp, yl), fi(zm, yl)
    f_peers = [fdev((f + k) % 8) for k in range(1, 8)]

    groups = []

    class Group:
        def __init__(self, whole):
            self.whole, self.sems = whole, (ssem.at[len(groups)], rsem.at[len(groups)])
            groups.append(self)

        def copy(self, src_ref, dst_ref, to):
            return pltpu.make_async_remote_copy(
                src_ref=src_ref, dst_ref=dst_ref, send_sem=self.sems[0], recv_sem=self.sems[1],
                device_id=to, device_id_type=MESH,
            )

        def send(self, src_ref, dst_ref, to):
            self.copy(src_ref, dst_ref, to).start()

        def same(self, ref, *to):
            for i in to:
                self.send(ref, ref, i)

        def recv(self):
            self.copy(self.whole, self.whole, partner).wait_recv()

        def sent(self):
            self.copy(self.whole, self.whole, partner).wait_send()

    mine = pl.ds(pl.multiple_of(d * 256, 256), 256)
    loc = [
        pltpu.make_async_copy(wg_hbm, wraw, lsem.at[0]),
        pltpu.make_async_copy(adj_hbm, adj, lsem.at[1]),
        pltpu.make_async_copy(ct_hbm, ct, lsem.at[2]),
    ]
    emb = []
    for r in range(10):
        emb.append(pltpu.make_async_copy(tgt_hbm.at[r], tgt.at[pl.ds(r, 1)], lsem.at[3 + r]))
        emb.append(
            pltpu.make_async_copy(src_hbm.at[r, :, mine], src.at[pl.ds(r, 1)], lsem.at[13 + r])
        )
    for c in emb + loc:
        c.start()

    barrier = pltpu.get_barrier_semaphore()
    cross = dev((d + 15 + 2 * core) % 16)
    peers = [partner, cross] + chips + f_peers
    for p in peers:
        pl.semaphore_signal(barrier, inc=1, device_id=p, device_id_type=MESH)

    nvalid = valid[0]
    mask = (lax.broadcasted_iota(jnp.int32, (1, 2048), 1) < nvalid).astype(F32)
    masked32 = state[...].astype(F32) * mask
    myrows = pl.ds(pl.multiple_of(f * 64, 64), 64)
    own = pl.ds(128, 2048)
    mext[myrows, own] = masked32.astype(BF)
    base[...] = masked32
    row16 = lax.broadcasted_iota(jnp.int32, (16, 2048), 0)
    low = cluster[...] & 255
    high = cluster[...] >> 8
    ohlo[...] = (lax.broadcasted_iota(jnp.int32, (256, 2048), 0) == low).astype(F32).astype(BF)

    row8 = lax.broadcasted_iota(jnp.int32, (8, 2048), 0)
    row_high = (row8 & 1) * 8 + (row8 >> 1) * 2

    def pool_part(c, to_core):
        for xx in range(4):
            for yy in range(2):
                slot = xx * 2 + yy
                hit = high == (yy * 8 + xx * 2) + to_core
                pl_lhs[slot * 64:(slot + 1) * 64, :] = jnp.where(hit, base[...], 0.0).astype(BF)
        for i in range(2):
            res = dot(pl_lhs[i * 256:(i + 1) * 256, :], ohlo[...], ((1,), (1,))).astype(BF)
            for k in range(4):
                slot = i * 4 + k
                pool[c, slot // 2, slot % 2] = res[k * 64:(k + 1) * 64]
        lhs = jnp.where(high == row_high + to_core, mask, 0.0).astype(BF)
        pcnt[c] = dot(lhs, ohlo[...], ((1,), (1,)))

    pool_part(0, 1 - core)

    pl.semaphore_wait(barrier, len(peers))

    m_r1, m_c1 = Group(r1), Group(c1)
    m_r1.send(pool.at[0], r1, partner)
    m_c1.send(pcnt.at[0], c1, partner)
    mrow = lambda i: mext.at[pl.ds(pl.multiple_of(i * 64, 64), 64), own]
    mhalf = lambda i, h: mext.at[pl.ds(pl.multiple_of(i * 64 + h * 32, 32), 32), own]
    st_y = [Group(mext.at[0:32, own]) for h in range(2)]
    st_yz = [Group(mext.at[0:64, own]) for h in range(2)]
    st_z, st_far = Group(mext.at[0:128, own]), Group(mext.at[0:128, own])
    m_h = Group(halo.at[0])
    m_h.send(mext.at[myrows, pl.ds(128, 128)], halo.at[f, 1], dleft)
    m_h.send(mext.at[myrows, pl.ds(2048, 128)], halo.at[f, 0], dright)
    st_y[0].same(mhalf(f, 0), fdev(fy))
    st_z.same(mrow(f), fdev(fzp), fdev(fzm))
    pool_part(1, core)

    for c in emb:
        c.wait()
    t6[...] = jnp.zeros_like(t6)
    s6[...] = jnp.zeros_like(s6)
    ta, tb, tc = split3(tgt[0:10, :])
    sa, sb, sc = split3(src[0:10, :])
    for k, (t, s) in enumerate([(ta, sa), (ta, sb), (tb, sa), (ta, sc), (tb, sb), (tc, sa)]):
        t6[k * 16:k * 16 + 10, :] = t
        s6[k * 16:k * 16 + 10, :] = s

    def score_step(j, peak):
        cols = pl.ds(pl.multiple_of(j * 512, 512), 512)
        s = jnp.maximum(dot(t6[:, cols], s6[...], ((0,), (0,))), 0.0)
        scores[cols, :] = s
        return jnp.maximum(peak, jnp.max(s.reshape(64, 8, 256), axis=0))

    m_r1.recv()
    m_c1.recv()
    s1[...] = (pool[1].astype(F32) + r1[...].astype(F32)).astype(BF)
    s1cnt[...] = pcnt[1] + c1[...]
    m_rs, m_rc = Group(rs.at[0:7]), Group(rscnt.at[0:7])
    for k, (a, b) in enumerate(hops):
        xx, yy = (x + a) % 4, (yh + b) % 2
        m_rs.send(s1.at[xx, yy], rs.at[k], chips[k])
        m_rc.send(s1cnt.at[pl.ds(xx * 2 + yy, 1)], rscnt.at[k], chips[k])

    st_y[1].same(mhalf(f, 1), fdev(fy))
    peak = lax.fori_loop(0, 4, score_step, jnp.zeros((8, 256), F32))
    peak = lax.fori_loop(4, 8, score_step, peak)
    peak = jnp.max(peak, axis=0, keepdims=True)

    def exp_step(j, total):
        cols = pl.ds(pl.multiple_of(j * 512, 512), 512)
        e = jnp.exp(scores[cols, :] - peak)
        expo[cols, :] = e.astype(BF)
        return total + jnp.sum(e.reshape(64, 8, 256), axis=0)

    total = lax.fori_loop(0, 8, exp_step, jnp.zeros((8, 256), F32))
    inv = 1.0 / jnp.sum(total, axis=0, keepdims=True)

    st_y[0].recv()
    st_yz[0].same(mhalf(fy, 0), fdev(fzp), fdev(fzm))
    st_z.recv()
    st_far.same(mhalf(fzm, 0), fdev(fzp))
    st_far.same(mhalf(fzp, 1), fdev(fzm))
    m_h.recv()
    m_hs = Group(halo.at[0:7])
    m_hs.same(halo.at[f], *f_peers)
    m_rs.recv()
    m_rc.recv()
    sums, cnt = s1[x, yh].astype(F32), s1cnt[pl.ds(x * 2 + yh, 1), :]
    for k in range(7):
        sums = sums + rs[k].astype(F32)
        cnt = cnt + rscnt[k]
    pooled = sums / jnp.maximum(cnt, 1.0)
    pa, pb, pc = split3(pooled)
    wv = w_val[...]
    vals[d] = (dot(wv, pa) + dot(wv, pb) + dot(wv, pc)).astype(BF)

    near, far = Group(vals.at[0:4]), Group(vals.at[0:3])
    for k in range(7):
        (far if k < 3 else near).same(vals.at[d], chips[k])
    swap_near, swap_far = Group(vals.at[0:5]), Group(vals.at[0:3])
    swap_near.same(vals.at[d], partner)

    st_y[1].recv()
    st_yz[1].same(mhalf(fy, 1), fdev(fzp), fdev(fzm))
    loc[0].wait()
    for k in range(4):
        wg[k * 192:(k + 1) * 192, :] = wraw[:, k, :]

    def attend(total, slots):
        for i in slots:
            rows = pl.ds(pl.multiple_of(i * 256, 256), 256)
            total = total + dot(vals[i], expo[rows, :])
        return total

    st_yz[0].recv()
    st_far.same(mhalf(fi(zm, 1 - yl), 0), fdev(fzp))
    mine_of = lambda ks, c: [chip(*hops[k]) + c for k in ks]
    near.recv()
    for i in mine_of(range(3, 7), core):
        swap_near.same(vals.at[i], partner)
    att = attend(jnp.zeros((64, 256), F32), [d] + mine_of(range(3, 7), core))
    far.recv()
    for i in mine_of(range(3), core):
        swap_far.same(vals.at[i], partner)
    swap_near.recv()
    att = attend(att, mine_of(range(3), core) + [chip(0, 0) + 1 - core])
    att = attend(att, mine_of(range(3, 7), 1 - core))
    swap_far.recv()
    att = attend(att, mine_of(range(3), 1 - core))
    ca[f] = (pooled + att * inv).astype(BF)
    m_ca = Group(ca.at[0:7])
    m_ca.same(ca.at[f], *f_peers)
    st_yz[1].recv()
    st_far.same(mhalf(fi(zp, 1 - yl), 1), fdev(fzm))
    m_ca.recv()
    early = list(groups)
    gall = (gall0, gall1, gall2)
    slot = lambda g, i: gall[g].at[pl.ds(2 * i, 2)]
    several = lambda n: [Group(gall[g].at[0:2 * n]) for g in range(3)]
    g_x, g_p = several(7), several(8)
    for g in range(3):
        r = dot(wg[576 + g * 64:640 + g * 64, :], ca[...].reshape(512, 256)).astype(BF)
        gall[g][2 * d] = r[:, :128]
        gall[g][2 * d + 1] = r[:, 128:]
        g_x[g].same(slot(g, d), *chips)
        g_p[g].same(slot(g, d), partner)

    st_far.recv()
    m_hs.recv()
    for i in range(8):
        mext[i * 64:(i + 1) * 64, 0:128] = halo[i, 0]
        mext[i * 64:(i + 1) * 64, 2176:2304] = halo[i, 1]

    for c in range(9):
        cols = slice(c * 256, (c + 1) * 256)
        r = dot(wg[0:576, :], mext[:, cols])
        gsum[:, cols] = r[0:192]
        w1m[:, cols] = r[192:384]
        ubuf[:, cols] = r[384:576].astype(BF)

    loc[1].wait()

    def diffuse(buf, t):
        lo, mid, hi = (buf[:, (t + k) * 128:(t + k + 1) * 128] for k in range(3))

        def pick(k):
            c = jnp.full((1, 128), adj_cols[k, t], jnp.int32)
            wlo, wmid, whi = ((c == t + i).astype(F32).astype(BF) for i in range(3))
            return lo * wlo + mid * wmid + hi * whi

        lhs = jnp.concatenate([lo, pick(1), pick(2), hi], axis=1)
        r = dot(lhs, adj[t])
        pos = lax.broadcasted_iota(jnp.int32, (1, 128), 1) + t * 128
        return r * (pos < nvalid).astype(F32)

    def first(t):
        cols = slice((t + 1) * 128, (t + 2) * 128)
        vbuf[:, cols] = (w1m[:, cols] + diffuse(ubuf, t)).astype(BF)

    def second(t):
        cols = slice((t + 1) * 128, (t + 2) * 128)
        gsum[:, cols] = gsum[:, cols] + diffuse(vbuf, t)

    first(0)
    first(15)
    tile = lambda i: vbuf.at[:, pl.ds(i * 128, 128)]
    m_vh = Group(vbuf.at[:, 0:256])
    m_vh.send(tile(1), tile(17), dleft)
    m_vh.send(tile(16), tile(0), dright)
    for t in range(1, 15):
        first(t)
    for t in range(1, 15):
        second(t)
    def swap(g):
        g_x[g].recv()
        for i in mine_of(range(7), core):
            g_p[g].same(slot(g, i), partner)

    for m in early:
        m.sent()
    loc[2].wait()
    eye = lax.broadcasted_iota(jnp.int32, (64, 64), 0) == lax.broadcasted_iota(
        jnp.int32, (64, 64), 1
    )
    column = lambda row: jnp.sum(jnp.where(eye, row, 0.0), axis=1, keepdims=True)
    bcol = [column(bias[g:g + 1, :]) for g in range(3)]
    win = [w_in[g].astype(F32) for g in range(3)]
    wcol = [[column(win[g][i:i + 1]) for i in range(2)] for g in range(3)]

    def unpool(g):
        g_p[g].recv()
        for s in range(16):
            parts = []
            for t in (2 * s, 2 * s + 1):
                lhs = jnp.concatenate([gall[g][ccols[k, t]] for k in range(2)], axis=1)
                parts.append(gall[g][t].astype(F32) + dot(lhs, ct[t]))
            gmix[s] = jnp.concatenate(parts, axis=1).astype(BF)
        if g < 2:
            swap(g + 1)
        rows = slice(g * 64, (g + 1) * 64)
        for n in range(8):
            cols = slice(n * 256, (n + 1) * 256)
            ecols = slice(n * 256 + 128, (n + 1) * 256 + 128)
            hi_n = cluster[:, cols] >> 8
            r = dot(gmix[...].reshape(1024, 256), ohlo[:, cols])
            acc = r[0:64]
            for s in range(1, 16):
                acc = jnp.where(hi_n == s, r[s * 64:(s + 1) * 64], acc)
            pre = acc + gsum[rows, ecols]
            xi = xin[:, cols].astype(F32)
            terms = wcol[g][0] * xi[0:1] + wcol[g][1] * xi[1:2] + bcol[g]
            if g == 0:
                gsum[rows, ecols] = terms + pre
                continue
            if g == 1:
                gsum[0:64, ecols] = jax.nn.sigmoid(gsum[0:64, ecols])
                gsum[rows, ecols] = jax.nn.sigmoid(terms + pre)
                continue
            update, reset = gsum[0:64, ecols], gsum[64:128, ecols]
            cand = jnp.tanh(terms + reset * pre)
            mk = (lax.broadcasted_iota(jnp.int32, (1, 256), 1) + n * 256 < nvalid).astype(F32)
            ms = state[:, cols].astype(F32) * mk
            out[:, cols] = ((update * ms + (1.0 - update) * cand) * mk).astype(BF)
            cp = pltpu.make_async_copy(out.at[:, cols], out_hbm.at[:, cols], lsem.at[23])
            cp.start()

    swap(0)
    unpool(0)
    m_vh.recv()
    second(0)
    second(15)
    unpool(1)
    unpool(2)

    for m in groups[len(early):]:
        m.sent()
    pltpu.make_async_copy(out, out_hbm, lsem.at[23]).wait()
    assert len(groups) == N_MSG


def body(
    state, inputs, adj_tiles, adj_cols, valid_rows, cluster_of, w_gates, w_input, bias, w_value,
    source_emb, target_emb, coarse_tiles, coarse_cols,
):
    vm = pl.BlockSpec(memory_space=pltpu.VMEM)
    sm = pl.BlockSpec(memory_space=pltpu.SMEM)
    hb = pl.BlockSpec(memory_space=pl.ANY)
    V = pltpu.VMEM
    return pl.pallas_call(
        kernel,
        out_shape=jax.ShapeDtypeStruct(state.shape, BF),
        in_specs=[vm, vm, hb, sm, sm, vm, hb, vm, vm, vm, hb, hb, hb, sm],
        out_specs=hb,
        scratch_shapes=[
            V((512, 2304), BF),
            V((8, 2, 64, 128), BF),
            V((256, 2048), BF),
            V((64, 2048), F32),
            V((512, 2048), BF),
            V((2, 4, 2, 64, 256), BF),
            V((2, 8, 256), F32),
            V((4, 2, 64, 256), BF),
            V((8, 256), F32),
            V((4, 2, 64, 256), BF),
            V((8, 256), F32),
            V((7, 64, 256), BF),
            V((7, 1, 256), F32),
            V((16, 256), F32),
            V((16, 4096), F32),
            V((96, 4096), BF),
            V((96, 256), BF),
            V((4096, 256), F32),
            V((4096, 256), BF),
            V((16, 64, 256), BF),
            V((8, 64, 256), BF),
            V((32, 64, 128), BF),
            V((32, 64, 128), BF),
            V((32, 64, 128), BF),
            V((16, 64, 256), BF),
            V((192, 2304), BF),
            V((192, 2304), BF),
            V((192, 2304), F32),
            V((192, 2304), F32),
            V((64, 2048), BF),
            V((16, 512, 128), BF),
            V((192, 4, 512), BF),
            V((768, 512), BF),
            V((32, 256, 128), BF),
            pltpu.SemaphoreType.DMA((N_MSG,)),
            pltpu.SemaphoreType.DMA((N_MSG,)),
            pltpu.SemaphoreType.DMA((24,)),
        ],
        compiler_params=pltpu.CompilerParams(collective_id=0, has_side_effects=True),
    )(
        state, inputs, adj_tiles.reshape(16, 512, 128), adj_cols.T, valid_rows,
        cluster_of.reshape(1, 2048), w_gates.reshape(192, 4, 512),
        jnp.transpose(w_input, (0, 2, 1)), bias, w_value.reshape(64, 64),
        jnp.transpose(source_emb, (1, 0, 2)), jnp.transpose(target_emb, (1, 0, 2)),
        coarse_tiles.reshape(32, 256, 128), coarse_cols.T,
    )


def solution(mesh):
    return jax.shard_map(
        body,
        mesh=mesh,
        in_specs=(
            P("feat", "dom"),
            P(None, "dom"),
            P("dom", None, None, None),
            P("dom", None),
            P("dom"),
            P("dom"),
            P(None, "feat", None, None),
            P(None, "feat", None),
            P(None, "feat"),
            P("feat", None, None),
            P("feat", None, None),
            P("feat", None, None),
            P(),
            P(),
        ),
        out_specs=P("feat", "dom"),
        check_vma=False,
    )
```

```python
import jax
import jax.numpy as jnp
from jax import lax
from jax.experimental import pallas as pl
from jax.experimental.pallas import tpu as pltpu
from jax.sharding import PartitionSpec as P

MESH = pl.DeviceIdType.MESH
BF = jnp.bfloat16
F32 = jnp.float32
N_MSG = 25


def dot(a, b, dims=((1,), (0,))):
    return lax.dot_general(a, b, (dims, ((), ())), preferred_element_type=F32)


def split3(v):
    a = v.astype(BF)
    r = v - a.astype(F32)
    b = r.astype(BF)
    c = (r - b.astype(F32)).astype(BF)
    return a, b, c


def kernel(
    state, xin, adj_hbm, adj_cols, valid, cluster, wg_hbm, w_in, bias, w_val, src_hbm, tgt_hbm,
    ct_hbm, ccols, out_hbm,
    mext, halo, ohlo, base, pl_lhs, pool, pcnt, r1, c1, s1, s1cnt, rs, rscnt, src, tgt, t6, s6, scores, expo,
    vals, ca, gall0, gall1, gall2, gall3, gmix, gmix_half, ubuf, vbuf, w1m, gsum, out, adj, wraw, wg, ct,
    ssem, rsem, lsem,
):
    d = lax.axis_index("dom")
    f = lax.axis_index("feat")
    core, x, yh = d % 2, (d // 2) % 4, d // 8
    z, yl = f // 2, f % 2
    zp, zm = (z + 1) % 4, (z + 3) % 4
    dev = lambda i: (i, f)
    fdev = lambda i: (d, i)
    partner = dev(d + 1 - 2 * core)
    hops = [(2, 1), (1, 1), (3, 1), (2, 0), (0, 1), (1, 0), (3, 0)]
    chip = lambda a, b: ((yh + b) % 2) * 8 + ((x + a) % 4) * 2
    chips = [dev(chip(a, b) + core) for a, b in hops]
    dleft, dright = dev((d + 15) % 16), dev((d + 1) % 16)
    fi = lambda a, b: a * 2 + b
    fy, fzp, fzm = f + 1 - 2 * yl, fi(zp, yl), fi(zm, yl)
    f_peers = [fdev((f + k) % 8) for k in range(1, 8)]

    groups = []

    class Group:
        def __init__(self, whole):
            self.whole, self.sems = whole, (ssem.at[len(groups)], rsem.at[len(groups)])
            groups.append(self)

        def copy(self, src_ref, dst_ref, to):
            return pltpu.make_async_remote_copy(
                src_ref=src_ref, dst_ref=dst_ref, send_sem=self.sems[0], recv_sem=self.sems[1],
                device_id=to, device_id_type=MESH,
            )

        def send(self, src_ref, dst_ref, to):
            self.copy(src_ref, dst_ref, to).start()

        def same(self, ref, *to):
            for i in to:
                self.send(ref, ref, i)

        def recv(self):
            self.copy(self.whole, self.whole, partner).wait_recv()

        def sent(self):
            self.copy(self.whole, self.whole, partner).wait_send()

    mine = pl.ds(pl.multiple_of(d * 256, 256), 256)
    loc = [
        pltpu.make_async_copy(wg_hbm, wraw, lsem.at[0]),
        pltpu.make_async_copy(adj_hbm, adj, lsem.at[1]),
        pltpu.make_async_copy(ct_hbm, ct, lsem.at[2]),
    ]
    tgt_rows = [pltpu.make_async_copy(tgt_hbm.at[r], tgt.at[pl.ds(r, 1)], lsem.at[3]) for r in range(10)]
    src_rows = pltpu.make_async_copy(src_hbm.at[:, :, mine], src, lsem.at[4])
    for c in tgt_rows + [src_rows] + loc:
        c.start()

    barrier = pltpu.get_barrier_semaphore()
    cross = dev((d + 15 + 2 * core) % 16)
    peers = [partner, cross] + chips + f_peers
    for p in peers:
        pl.semaphore_signal(barrier, inc=1, device_id=p, device_id_type=MESH)

    nvalid = valid[0]
    mask = (lax.broadcasted_iota(jnp.int32, (1, 2048), 1) < nvalid).astype(F32)
    masked32 = state[...].astype(F32) * mask
    myrows = pl.ds(pl.multiple_of(f * 64, 64), 64)
    own = pl.ds(128, 2048)
    base[...] = masked32.astype(BF)
    mext[myrows, own] = base[...]
    low = cluster[...] & 255
    high = cluster[...] >> 8
    ohlo[...] = (lax.broadcasted_iota(jnp.int32, (256, 2048), 0) == low).astype(F32).astype(BF)

    row8 = lax.broadcasted_iota(jnp.int32, (8, 2048), 0)
    row_high = (row8 & 1) * 8 + (row8 >> 1) * 2

    def pool_part(c, to_core):
        for xx in range(4):
            for yy in range(2):
                slot = xx * 2 + yy
                hit = high == (yy * 8 + xx * 2) + to_core
                pl_lhs[slot * 64:(slot + 1) * 64, :] = base[...] * hit.astype(F32).astype(BF)
        for i in range(2):
            res = dot(pl_lhs[i * 256:(i + 1) * 256, :], ohlo[...], ((1,), (1,))).astype(BF)
            for k in range(4):
                slot = i * 4 + k
                pool[c, slot // 2, slot % 2] = res[k * 64:(k + 1) * 64]
        lhs = jnp.where(high == row_high + to_core, mask, 0.0).astype(BF)
        pcnt[c] = dot(lhs, ohlo[...], ((1,), (1,)))

    pool_part(0, 1 - core)

    pl.semaphore_wait(barrier, len(peers))

    m_r1, m_c1 = Group(r1), Group(c1)
    m_r1.send(pool.at[0], r1, partner)
    m_c1.send(pcnt.at[0], c1, partner)
    mrow = lambda i: mext.at[pl.ds(pl.multiple_of(i * 64, 64), 64), own]
    mhalf = lambda i, h: mext.at[pl.ds(pl.multiple_of(i * 64 + h * 32, 32), 32), own]
    st_y = [Group(expo.at[0:n]) for n in (256, 320)]
    st_yz = [Group(expo.at[0:n]) for n in (512, 640)]
    st_z, st_far = Group(expo.at[0:1152]), Group(expo.at[0:1152])
    m_h = Group(halo.at[0])
    m_h.send(mext.at[myrows, pl.ds(128, 128)], halo.at[f, 1], dleft)
    m_h.send(mext.at[myrows, pl.ds(2048, 128)], halo.at[f, 0], dright)
    st_y[0].same(mhalf(f, 0), fdev(fy))
    st_z.same(mrow(f), fdev(fzp), fdev(fzm))
    pool_part(1, core)

    pltpu.make_async_copy(expo.at[0:320], expo.at[0:320], lsem.at[3]).wait()
    src_rows.wait()
    t6[...] = jnp.zeros_like(t6)
    s6[...] = jnp.zeros_like(s6)
    ta, tb, tc = split3(tgt[0:10, :])
    sa, sb, sc = split3(jnp.concatenate([src[r] for r in range(10)], axis=0))
    for k, (t, s) in enumerate([(ta, sa), (ta, sb), (tb, sa), (ta, sc), (tb, sb), (tc, sa)]):
        t6[k * 16:k * 16 + 10, :] = t
        s6[k * 16:k * 16 + 10, :] = s

    def score_step(j, peak):
        cols = pl.ds(pl.multiple_of(j * 512, 512), 512)
        s = jnp.maximum(dot(t6[:, cols], s6[...], ((0,), (0,))), 0.0)
        scores[cols, :] = s
        return jnp.maximum(peak, jnp.max(s.reshape(64, 8, 256), axis=0))

    m_r1.recv()
    m_c1.recv()
    s1[...] = (pool[1].astype(F32) + r1[...].astype(F32)).astype(BF)
    s1cnt[...] = pcnt[1] + c1[...]
    m_rs, m_rc = Group(rs.at[0:7]), Group(rscnt.at[0:7])
    for k, (a, b) in enumerate(hops):
        xx, yy = (x + a) % 4, (yh + b) % 2
        m_rs.send(s1.at[xx, yy], rs.at[k], chips[k])
        m_rc.send(s1cnt.at[pl.ds(xx * 2 + yy, 1)], rscnt.at[k], chips[k])

    peak = lax.fori_loop(0, 4, score_step, jnp.zeros((8, 256), F32))
    m_h.recv()
    st_y[1].same(mhalf(f, 1), fdev(fy))
    st_y[1].same(halo.at[f], fdev(fy))
    st_z.same(halo.at[f], fdev(fzp), fdev(fzm))
    peak = lax.fori_loop(4, 8, score_step, peak)
    peak = jnp.max(peak, axis=0, keepdims=True)

    def exp_step(j, total):
        cols = pl.ds(pl.multiple_of(j * 512, 512), 512)
        e = jnp.exp(scores[cols, :] - peak)
        expo[cols, :] = e.astype(BF)
        return total + jnp.sum(e.reshape(64, 8, 256), axis=0)

    total = lax.fori_loop(0, 8, exp_step, jnp.zeros((8, 256), F32))
    inv = 1.0 / jnp.sum(total, axis=0, keepdims=True)

    st_y[0].recv()
    st_yz[0].same(mhalf(fy, 0), fdev(fzp), fdev(fzm))
    st_z.recv()
    st_far.same(mhalf(fzm, 0), fdev(fzp))
    st_far.same(mhalf(fzp, 1), fdev(fzm))
    st_far.same(halo.at[fzm, 0], fdev(fzp))
    st_far.same(halo.at[fzp, 1], fdev(fzm))
    m_rs.recv()
    m_rc.recv()
    sums, cnt = s1[x, yh].astype(F32), s1cnt[pl.ds(x * 2 + yh, 1), :]
    for k in range(7):
        sums = sums + rs[k].astype(F32)
        cnt = cnt + rscnt[k]
    pooled = sums / jnp.maximum(cnt, 1.0)
    pa, pb, pc = split3(pooled)
    wv = w_val[...]
    vals[d] = (dot(wv, pa) + dot(wv, pb) + dot(wv, pc)).astype(BF)

    near, far = Group(vals.at[0:4]), Group(vals.at[0:3])
    for k in range(7):
        (far if k < 3 else near).same(vals.at[d], chips[k])
    swap_near, swap_far = Group(vals.at[0:5]), Group(vals.at[0:3])
    swap_near.same(vals.at[d], partner)

    st_y[1].recv()
    st_yz[1].same(mhalf(fy, 1), fdev(fzp), fdev(fzm))
    st_yz[1].same(halo.at[fy], fdev(fzp), fdev(fzm))
    loc[0].wait()
    for k in range(4):
        wg[k * 192:(k + 1) * 192, :] = wraw[:, k, :]

    def attend(total, slots):
        for i in slots:
            rows = pl.ds(pl.multiple_of(i * 256, 256), 256)
            total = total + dot(vals[i], expo[rows, :])
        return total

    st_yz[0].recv()
    st_far.same(mhalf(fi(zm, 1 - yl), 0), fdev(fzp))
    mine_of = lambda ks, c: [chip(*hops[k]) + c for k in ks]
    near.recv()
    for i in mine_of(range(3, 7), core):
        swap_near.same(vals.at[i], partner)
    att = attend(jnp.zeros((64, 256), F32), [d] + mine_of(range(3, 7), core))
    far.recv()
    for i in mine_of(range(3), core):
        swap_far.same(vals.at[i], partner)
    swap_near.recv()
    att = attend(att, mine_of(range(3), core) + [chip(0, 0) + 1 - core])
    att = attend(att, mine_of(range(3, 7), 1 - core))
    swap_far.recv()
    att = attend(att, mine_of(range(3), 1 - core))
    ca[f] = (pooled + att * inv).astype(BF)
    m_ca = Group(ca.at[0:7])
    m_ca.same(ca.at[f], *f_peers)
    st_yz[1].recv()
    st_far.same(mhalf(fi(zp, 1 - yl), 1), fdev(fzm))
    st_far.same(halo.at[fi(zp, 1 - yl)], fdev(fzm))
    m_ca.recv()
    early = list(groups)
    gall = (gall0, gall1, gall2, gall3)
    pieces = ((0, 64), (64, 128), (128, 160), (160, 192))
    slot = lambda g, i: gall[g].at[pl.ds(2 * i, 2)]
    several = lambda n: [Group(gall[g].at[0:2 * n]) for g in range(4)]
    g_x, g_p = several(7), several(8)
    for g, (lo, hi) in enumerate(pieces):
        r = dot(wg[576 + lo:576 + hi, :], ca[...].reshape(512, 256)).astype(BF)
        gall[g][2 * d] = r[:, :128]
        gall[g][2 * d + 1] = r[:, 128:]
        g_x[g].same(slot(g, d), *chips)
        g_p[g].same(slot(g, d), partner)

    st_far.recv()
    for i in range(8):
        mext[i * 64:(i + 1) * 64, 0:128] = halo[i, 0]
        mext[i * 64:(i + 1) * 64, 2176:2304] = halo[i, 1]

    for c in range(9):
        cols = slice(c * 256, (c + 1) * 256)
        r = dot(wg[0:576, :], mext[:, cols])
        gsum[:, cols] = r[0:192]
        w1m[:, cols] = r[192:384]
        ubuf[:, cols] = r[384:576].astype(BF)

    loc[1].wait()

    def diffuse(buf, t):
        lo, mid, hi = (buf[:, (t + k) * 128:(t + k + 1) * 128] for k in range(3))

        def pick(k):
            c = jnp.full((1, 128), adj_cols[k, t], jnp.int32)
            wlo, wmid, whi = ((c == t + i).astype(F32).astype(BF) for i in range(3))
            return lo * wlo + mid * wmid + hi * whi

        lhs = jnp.concatenate([lo, pick(1), pick(2), hi], axis=1)
        r = dot(lhs, adj[t])
        pos = lax.broadcasted_iota(jnp.int32, (1, 128), 1) + t * 128
        return r * (pos < nvalid).astype(F32)

    def first(t):
        cols = slice((t + 1) * 128, (t + 2) * 128)
        vbuf[:, cols] = (w1m[:, cols] + diffuse(ubuf, t)).astype(BF)

    def second(t):
        cols = slice((t + 1) * 128, (t + 2) * 128)
        gsum[:, cols] = gsum[:, cols] + diffuse(vbuf, t)

    first(0)
    first(15)
    tile = lambda i: vbuf.at[:, pl.ds(i * 128, 128)]
    m_vh = Group(vbuf.at[:, 0:256])
    m_vh.send(tile(1), tile(17), dleft)
    m_vh.send(tile(16), tile(0), dright)
    for t in range(1, 15):
        first(t)
    for t in range(1, 15):
        second(t)
    def swap(g):
        g_x[g].recv()
        for i in mine_of(range(7), core):
            g_p[g].same(slot(g, i), partner)

    for m in early:
        m.sent()
    loc[2].wait()
    eye = lax.broadcasted_iota(jnp.int32, (64, 64), 0) == lax.broadcasted_iota(
        jnp.int32, (64, 64), 1
    )
    column = lambda row: jnp.sum(jnp.where(eye, row, 0.0), axis=1, keepdims=True)
    bcol = [column(bias[g:g + 1, :]) for g in range(3)]
    win = [w_in[g].astype(F32) for g in range(3)]
    wcol = [[column(win[g][i:i + 1]) for i in range(2)] for g in range(3)]

    def unpool(p):
        lo, hi = pieces[p]
        rows, count, g = slice(lo, hi), hi - lo, min(p, 2)
        part = slice(lo - 64 * g, hi - 64 * g)
        mixed = gmix if count == 64 else gmix_half
        g_p[p].recv()
        for s in range(16):
            tiles = []
            for t in (2 * s, 2 * s + 1):
                lhs = jnp.concatenate([gall[p][ccols[k, t]] for k in range(2)], axis=1)
                tiles.append(gall[p][t].astype(F32) + dot(lhs, ct[t]))
            mixed[s] = jnp.concatenate(tiles, axis=1).astype(BF)
        if p < 3:
            swap(p + 1)
        for n in range(8):
            cols = slice(n * 256, (n + 1) * 256)
            ecols = slice(n * 256 + 128, (n + 1) * 256 + 128)
            hi_n = cluster[:, cols] >> 8
            r = dot(mixed[...].reshape(16 * count, 256), ohlo[:, cols])
            acc = r[0:count]
            for s in range(1, 16):
                acc = jnp.where(hi_n == s, r[s * count:(s + 1) * count], acc)
            pre = acc + gsum[rows, ecols]
            xi = xin[:, cols].astype(F32)
            terms = wcol[g][0][part] * xi[0:1] + wcol[g][1][part] * xi[1:2] + bcol[g][part]
            if g == 0:
                gsum[rows, ecols] = terms + pre
                continue
            if g == 1:
                gsum[0:64, ecols] = jax.nn.sigmoid(gsum[0:64, ecols])
                gsum[rows, ecols] = jax.nn.sigmoid(terms + pre)
                continue
            update, reset = gsum[part, ecols], gsum[64 + lo - 128:64 + hi - 128, ecols]
            cand = jnp.tanh(terms + reset * pre)
            mk = (lax.broadcasted_iota(jnp.int32, (1, 256), 1) + n * 256 < nvalid).astype(F32)
            ms = state[part, cols].astype(F32) * mk
            out[part, cols] = ((update * ms + (1.0 - update) * cand) * mk).astype(BF)
            cp = pltpu.make_async_copy(out.at[part, cols], out_hbm.at[part, cols], lsem.at[5])
            cp.start()

    swap(0)
    unpool(0)
    m_vh.recv()
    second(0)
    second(15)
    unpool(1)
    unpool(2)
    unpool(3)

    for m in groups[len(early):]:
        m.sent()
    pltpu.make_async_copy(out, out_hbm, lsem.at[5]).wait()
    assert len(groups) == N_MSG


def body(
    state, inputs, adj_tiles, adj_cols, valid_rows, cluster_of, w_gates, w_input, bias, w_value,
    source_emb, target_emb, coarse_tiles, coarse_cols,
):
    vm = pl.BlockSpec(memory_space=pltpu.VMEM)
    sm = pl.BlockSpec(memory_space=pltpu.SMEM)
    hb = pl.BlockSpec(memory_space=pl.ANY)
    V = pltpu.VMEM
    return pl.pallas_call(
        kernel,
        out_shape=jax.ShapeDtypeStruct(state.shape, BF),
        in_specs=[vm, vm, hb, sm, sm, vm, hb, vm, vm, vm, hb, hb, hb, sm],
        out_specs=hb,
        scratch_shapes=[
            V((512, 2304), BF),
            V((8, 2, 64, 128), BF),
            V((256, 2048), BF),
            V((64, 2048), BF),
            V((512, 2048), BF),
            V((2, 4, 2, 64, 256), BF),
            V((2, 8, 256), F32),
            V((4, 2, 64, 256), BF),
            V((8, 256), F32),
            V((4, 2, 64, 256), BF),
            V((8, 256), F32),
            V((7, 64, 256), BF),
            V((7, 1, 256), F32),
            V((10, 1, 256), F32),
            V((16, 4096), F32),
            V((96, 4096), BF),
            V((96, 256), BF),
            V((4096, 256), F32),
            V((4096, 256), BF),
            V((16, 64, 256), BF),
            V((8, 64, 256), BF),
            V((32, 64, 128), BF),
            V((32, 64, 128), BF),
            V((32, 32, 128), BF),
            V((32, 32, 128), BF),
            V((16, 64, 256), BF),
            V((16, 32, 256), BF),
            V((192, 2304), BF),
            V((192, 2304), BF),
            V((192, 2304), F32),
            V((192, 2304), F32),
            V((64, 2048), BF),
            V((16, 512, 128), BF),
            V((192, 4, 512), BF),
            V((768, 512), BF),
            V((32, 256, 128), BF),
            pltpu.SemaphoreType.DMA((N_MSG,)),
            pltpu.SemaphoreType.DMA((N_MSG,)),
            pltpu.SemaphoreType.DMA((6,)),
        ],
        compiler_params=pltpu.CompilerParams(collective_id=0, has_side_effects=True),
    )(
        state, inputs, adj_tiles.reshape(16, 512, 128), adj_cols.T, valid_rows,
        cluster_of.reshape(1, 2048), w_gates.reshape(192, 4, 512),
        jnp.transpose(w_input, (0, 2, 1)), bias, w_value.reshape(64, 64),
        jnp.transpose(source_emb, (1, 0, 2)), jnp.transpose(target_emb, (1, 0, 2)),
        coarse_tiles.reshape(32, 256, 128), coarse_cols.T,
    )


def solution(mesh):
    return jax.shard_map(
        body,
        mesh=mesh,
        in_specs=(
            P("feat", "dom"),
            P(None, "dom"),
            P("dom", None, None, None),
            P("dom", None),
            P("dom"),
            P("dom"),
            P(None, "feat", None, None),
            P(None, "feat", None),
            P(None, "feat"),
            P("feat", None, None),
            P("feat", None, None),
            P("feat", None, None),
            P(),
            P(),
        ),
        out_specs=P("feat", "dom"),
        check_vma=False,
    )
```

```python
import jax
import jax.numpy as jnp
from jax import lax
from jax.experimental import pallas as pl
from jax.experimental.pallas import tpu as pltpu
from jax.sharding import PartitionSpec as P

MESH = pl.DeviceIdType.MESH
BF = jnp.bfloat16
F32 = jnp.float32
N_MSG = 26


def dot(a, b, dims=((1,), (0,))):
    return lax.dot_general(a, b, (dims, ((), ())), preferred_element_type=F32)


def split3(v):
    a = v.astype(BF)
    r = v - a.astype(F32)
    b = r.astype(BF)
    c = (r - b.astype(F32)).astype(BF)
    return a, b, c


def kernel(
    state, xin, adj_hbm, adj_cols, valid, cluster, wg_hbm, w_in, bias, w_val, src_hbm, tgt_hbm,
    ct_hbm, ccols, out_hbm,
    mext, halo, ohlo, base, pl_lhs, pool, pcnt, r1, c1, s1, s1cnt, rs, rscnt, src, tgt, t6, s6, scores, expo,
    vals, ca, gall0, gall1, gall2, gall3, gmix, gmix_half, ubuf, vbuf, w1m, gsum, out, adj, wraw, wg, ct,
    ssem, rsem, lsem,
):
    d = lax.axis_index("dom")
    f = lax.axis_index("feat")
    core, x, yh = d % 2, (d // 2) % 4, d // 8
    z, yl = f // 2, f % 2
    zp, zm = (z + 1) % 4, (z + 3) % 4
    dev = lambda i: (i, f)
    fdev = lambda i: (d, i)
    partner = dev(d + 1 - 2 * core)
    hops = [(2, 1), (1, 1), (3, 1), (2, 0), (0, 1), (1, 0), (3, 0)]
    chip = lambda a, b: ((yh + b) % 2) * 8 + ((x + a) % 4) * 2
    chips = [dev(chip(a, b) + core) for a, b in hops]
    dleft, dright = dev((d + 15) % 16), dev((d + 1) % 16)
    fi = lambda a, b: a * 2 + b
    fy, fzp, fzm = f + 1 - 2 * yl, fi(zp, yl), fi(zm, yl)
    f_peers = [fdev((f + k) % 8) for k in range(1, 8)]

    groups = []

    class Group:
        def __init__(self, whole):
            self.whole, self.sems = whole, (ssem.at[len(groups)], rsem.at[len(groups)])
            groups.append(self)

        def copy(self, src_ref, dst_ref, to):
            return pltpu.make_async_remote_copy(
                src_ref=src_ref, dst_ref=dst_ref, send_sem=self.sems[0], recv_sem=self.sems[1],
                device_id=to, device_id_type=MESH,
            )

        def send(self, src_ref, dst_ref, to):
            self.copy(src_ref, dst_ref, to).start()

        def same(self, ref, *to):
            for i in to:
                self.send(ref, ref, i)

        def recv(self):
            self.copy(self.whole, self.whole, partner).wait_recv()

        def sent(self):
            self.copy(self.whole, self.whole, partner).wait_send()

    mine = pl.ds(pl.multiple_of(d * 256, 256), 256)
    loc = [
        pltpu.make_async_copy(wg_hbm, wraw, lsem.at[0]),
        pltpu.make_async_copy(adj_hbm, adj, lsem.at[1]),
        pltpu.make_async_copy(ct_hbm, ct, lsem.at[2]),
    ]
    tgt_rows = [pltpu.make_async_copy(tgt_hbm.at[r], tgt.at[pl.ds(r, 1)], lsem.at[3]) for r in range(10)]
    src_rows = pltpu.make_async_copy(src_hbm.at[:, :, mine], src, lsem.at[4])
    for c in tgt_rows + [src_rows] + loc:
        c.start()

    barrier = pltpu.get_barrier_semaphore()
    cross = dev((d + 15 + 2 * core) % 16)
    peers = [partner, cross] + chips + f_peers
    for p in peers:
        pl.semaphore_signal(barrier, inc=1, device_id=p, device_id_type=MESH)

    nvalid = valid[0]
    mask = (lax.broadcasted_iota(jnp.int32, (1, 2048), 1) < nvalid).astype(F32)
    masked32 = state[...].astype(F32) * mask
    myrows = pl.ds(pl.multiple_of(f * 64, 64), 64)
    own = pl.ds(128, 2048)
    base[...] = masked32.astype(BF)
    mext[myrows, own] = base[...]
    low = cluster[...] & 511
    high = cluster[...] >> 9
    row8 = lax.broadcasted_iota(jnp.int32, (8, 2048), 0)
    cnt_lhs = jnp.where(high == (row8 & 1) * 4 + (row8 >> 1), mask, 0.0).astype(BF)

    def pool_part(c, to_core):
        rows = pl.ds(pl.multiple_of(to_core * 256, 256), 256)
        row = lax.broadcasted_iota(jnp.int32, (256, 2048), 0) + to_core * 256
        ohlo[rows, :] = (row == low).astype(F32).astype(BF)
        for i in range(2):
            if c == 0:
                for slot in range(i * 4, i * 4 + 4):
                    hit = high == (slot % 2) * 4 + slot // 2
                    pl_lhs[slot * 64:(slot + 1) * 64, :] = base[...] * hit.astype(F32).astype(BF)
            res = dot(pl_lhs[i * 256:(i + 1) * 256, :], ohlo[rows, :], ((1,), (1,))).astype(BF)
            for k in range(4):
                slot = i * 4 + k
                pool[c, slot // 2, slot % 2] = res[k * 64:(k + 1) * 64]
        pcnt[c] = dot(cnt_lhs, ohlo[rows, :], ((1,), (1,)))

    pool_part(0, 1 - core)

    pl.semaphore_wait(barrier, len(peers))

    m_r1, m_c1 = Group(r1), Group(c1)
    m_r1.send(pool.at[0], r1, partner)
    m_c1.send(pcnt.at[0], c1, partner)
    mrow = lambda i: mext.at[pl.ds(pl.multiple_of(i * 64, 64), 64), own]
    mhalf = lambda i, h: mext.at[pl.ds(pl.multiple_of(i * 64 + h * 32, 32), 32), own]
    st_y = [Group(expo.at[0:n]) for n in (256, 320)]
    st_yz = [Group(expo.at[0:n]) for n in (512, 640)]
    st_z, st_far = Group(expo.at[0:1152]), Group(expo.at[0:1152])
    m_h = Group(halo.at[0])
    m_h.send(mext.at[myrows, pl.ds(128, 128)], halo.at[f, 1], dleft)
    m_h.send(mext.at[myrows, pl.ds(2048, 128)], halo.at[f, 0], dright)
    st_y[0].same(mhalf(f, 0), fdev(fy))
    st_z.same(mrow(f), fdev(fzp), fdev(fzm))
    pool_part(1, core)

    pltpu.make_async_copy(expo.at[0:320], expo.at[0:320], lsem.at[3]).wait()
    src_rows.wait()
    t6[...] = jnp.zeros_like(t6)
    s6[...] = jnp.zeros_like(s6)
    ta, tb, tc = split3(tgt[0:10, :])
    sa, sb, sc = split3(jnp.concatenate([src[r] for r in range(10)], axis=0))
    for k, (t, s) in enumerate([(ta, sa), (ta, sb), (tb, sa), (ta, sc), (tb, sb), (tc, sa)]):
        t6[k * 16:k * 16 + 10, :] = t
        s6[k * 16:k * 16 + 10, :] = s

    def score_step(j, peak):
        cols = pl.ds(pl.multiple_of(j * 512, 512), 512)
        s = jnp.maximum(dot(t6[:, cols], s6[...], ((0,), (0,))), 0.0)
        scores[cols, :] = s
        return jnp.maximum(peak, jnp.max(s.reshape(64, 8, 256), axis=0))

    m_r1.recv()
    m_c1.recv()
    s1[...] = (pool[1].astype(F32) + r1[...].astype(F32)).astype(BF)
    s1cnt[...] = pcnt[1] + c1[...]
    m_rs, m_rc = Group(rs.at[0:7]), Group(rscnt.at[0:7])
    for k, (a, b) in enumerate(hops):
        xx, yy = (x + a) % 4, (yh + b) % 2
        m_rs.send(s1.at[xx, yy], rs.at[k], chips[k])
        m_rc.send(s1cnt.at[pl.ds(xx * 2 + yy, 1)], rscnt.at[k], chips[k])

    peak = lax.fori_loop(0, 4, score_step, jnp.zeros((8, 256), F32))
    m_h.recv()
    st_y[1].same(mhalf(f, 1), fdev(fy))
    st_y[1].same(halo.at[f], fdev(fy))
    st_z.same(halo.at[f], fdev(fzp), fdev(fzm))
    peak = lax.fori_loop(4, 8, score_step, peak)
    peak = jnp.max(peak, axis=0, keepdims=True)

    def exp_step(j, total):
        cols = pl.ds(pl.multiple_of(j * 512, 512), 512)
        e = jnp.exp(scores[cols, :] - peak)
        expo[cols, :] = e.astype(BF)
        return total + jnp.sum(e.reshape(64, 8, 256), axis=0)

    total = lax.fori_loop(0, 8, exp_step, jnp.zeros((8, 256), F32))
    inv = 1.0 / jnp.sum(total, axis=0, keepdims=True)

    st_y[0].recv()
    st_yz[0].same(mhalf(fy, 0), fdev(fzp), fdev(fzm))
    st_z.recv()
    st_far.same(mhalf(fzm, 0), fdev(fzp))
    st_far.same(mhalf(fzp, 1), fdev(fzm))
    st_far.same(halo.at[fzm, 0], fdev(fzp))
    st_far.same(halo.at[fzp, 1], fdev(fzm))
    m_rs.recv()
    m_rc.recv()
    sums, cnt = s1[x, yh].astype(F32), s1cnt[pl.ds(x * 2 + yh, 1), :]
    for k in range(7):
        sums = sums + rs[k].astype(F32)
        cnt = cnt + rscnt[k]
    pooled = sums / jnp.maximum(cnt, 1.0)
    pa, pb, pc = split3(pooled)
    wv = w_val[...]
    vals[d] = (dot(wv, pa) + dot(wv, pb) + dot(wv, pc)).astype(BF)

    near, far = Group(vals.at[0:4]), Group(vals.at[0:3])
    for k in range(7):
        (far if k < 3 else near).same(vals.at[d], chips[k])
    swap_near, swap_far = Group(vals.at[0:5]), Group(vals.at[0:3])
    swap_near.same(vals.at[d], partner)

    st_y[1].recv()
    st_yz[1].same(mhalf(fy, 1), fdev(fzp), fdev(fzm))
    st_yz[1].same(halo.at[fy], fdev(fzp), fdev(fzm))
    loc[0].wait()
    for k in range(4):
        wg[k * 192:(k + 1) * 192, :] = wraw[:, k, :]

    def attend(total, slots):
        for i in slots:
            rows = pl.ds(pl.multiple_of(i * 256, 256), 256)
            total = total + dot(vals[i], expo[rows, :])
        return total

    st_yz[0].recv()
    st_far.same(mhalf(fi(zm, 1 - yl), 0), fdev(fzp))
    mine_of = lambda ks, c: [chip(*hops[k]) + c for k in ks]
    near.recv()
    for i in mine_of(range(3, 7), core):
        swap_near.same(vals.at[i], partner)
    att = attend(jnp.zeros((64, 256), F32), [d] + mine_of(range(3, 7), core))
    far.recv()
    for i in mine_of(range(3), core):
        swap_far.same(vals.at[i], partner)
    swap_near.recv()
    att = attend(att, mine_of(range(3), core) + [chip(0, 0) + 1 - core])
    att = attend(att, mine_of(range(3, 7), 1 - core))
    swap_far.recv()
    att = attend(att, mine_of(range(3), 1 - core))
    attn = (pooled + att * inv).astype(BF)
    m_ca = [Group(ca.at[0, 0:7]) for h in range(2)]
    for h in range(2):
        ca[h, f] = attn[:, h * 128:(h + 1) * 128]
    for h in range(2):
        m_ca[h].same(ca.at[h, f], *f_peers)
    st_yz[1].recv()
    st_far.same(mhalf(fi(zp, 1 - yl), 1), fdev(fzm))
    st_far.same(halo.at[fi(zp, 1 - yl)], fdev(fzm))
    early = list(groups)
    gall = (gall0, gall1, gall2, gall3)
    pieces = ((0, 64), (64, 128), (128, 160), (160, 192))
    slot = lambda g, i: gall[g].at[pl.ds(2 * i, 2)]
    several = lambda n: [Group(gall[g].at[0:2 * n]) for g in range(4)]
    g_x, g_p = several(7), several(8)

    def g_send(g, h):
        g_x[g].same(gall[g].at[2 * d + h], *chips)
        g_p[g].same(gall[g].at[2 * d + h], partner)

    for h in range(2):
        m_ca[h].recv()
        for g, (lo, hi) in enumerate(pieces):
            gall[g][2 * d + h] = dot(wg[576 + lo:576 + hi, :], ca[h].reshape(512, 128)).astype(BF)
            if g == 0 or g == 1 and h == 1:
                g_send(g, h)
        if h == 0:
            g_send(1, 0)
    for g in (2, 3):
        for h in range(2):
            g_send(g, h)

    st_far.recv()
    for i in range(8):
        mext[i * 64:(i + 1) * 64, 0:128] = halo[i, 0]
        mext[i * 64:(i + 1) * 64, 2176:2304] = halo[i, 1]

    for c in range(9):
        cols = slice(c * 256, (c + 1) * 256)
        r = dot(wg[0:576, :], mext[:, cols])
        gsum[:, cols] = r[0:192]
        w1m[:, cols] = r[192:384]
        ubuf[:, cols] = r[384:576].astype(BF)

    loc[1].wait()

    def diffuse(buf, t):
        lo, mid, hi = (buf[:, (t + k) * 128:(t + k + 1) * 128] for k in range(3))

        def pick(k):
            c = jnp.full((1, 128), adj_cols[k, t], jnp.int32)
            wlo, wmid, whi = ((c == t + i).astype(F32).astype(BF) for i in range(3))
            return lo * wlo + mid * wmid + hi * whi

        lhs = jnp.concatenate([lo, pick(1), pick(2), hi], axis=1)
        r = dot(lhs, adj[t])
        pos = lax.broadcasted_iota(jnp.int32, (1, 128), 1) + t * 128
        return r * (pos < nvalid).astype(F32)

    def first(t):
        cols = slice((t + 1) * 128, (t + 2) * 128)
        vbuf[:, cols] = (w1m[:, cols] + diffuse(ubuf, t)).astype(BF)

    def second(t):
        cols = slice((t + 1) * 128, (t + 2) * 128)
        gsum[:, cols] = gsum[:, cols] + diffuse(vbuf, t)

    first(0)
    first(15)
    tile = lambda i: vbuf.at[:, pl.ds(i * 128, 128)]
    m_vh = Group(vbuf.at[:, 0:256])
    m_vh.send(tile(1), tile(17), dleft)
    m_vh.send(tile(16), tile(0), dright)
    for t in range(1, 15):
        first(t)
    for t in range(1, 15):
        second(t)
    def swap(g):
        g_x[g].recv()
        for i in mine_of(range(7), core):
            g_p[g].same(slot(g, i), partner)

    for m in early:
        m.sent()
    loc[2].wait()
    eye = lax.broadcasted_iota(jnp.int32, (64, 64), 0) == lax.broadcasted_iota(
        jnp.int32, (64, 64), 1
    )
    column = lambda row: jnp.sum(jnp.where(eye, row, 0.0), axis=1, keepdims=True)
    bcol = [column(bias[g:g + 1, :]) for g in range(3)]
    win = [w_in[g].astype(F32) for g in range(3)]
    wcol = [[column(win[g][i:i + 1]) for i in range(2)] for g in range(3)]

    def unpool(p):
        lo, hi = pieces[p]
        rows, count, g = slice(lo, hi), hi - lo, min(p, 2)
        part = slice(lo - 64 * g, hi - 64 * g)
        mixed = gmix if count == 64 else gmix_half
        g_p[p].recv()
        for s in range(8):
            tiles = []
            for t in range(4 * s, 4 * s + 4):
                lhs = jnp.concatenate([gall[p][ccols[k, t]] for k in range(2)], axis=1)
                tiles.append(gall[p][t].astype(F32) + dot(lhs, ct[t]))
            mixed[s] = jnp.concatenate(tiles, axis=1).astype(BF)
        if p < 3:
            swap(p + 1)
        for n in range(8):
            cols = slice(n * 256, (n + 1) * 256)
            ecols = slice(n * 256 + 128, (n + 1) * 256 + 128)
            hi_n = cluster[:, cols] >> 9
            r = dot(mixed[...].reshape(8 * count, 512), ohlo[:, cols])
            acc = r[0:count]
            for s in range(1, 8):
                acc = jnp.where(hi_n == s, r[s * count:(s + 1) * count], acc)
            pre = acc + gsum[rows, ecols]
            xi = xin[:, cols].astype(F32)
            terms = wcol[g][0][part] * xi[0:1] + wcol[g][1][part] * xi[1:2] + bcol[g][part]
            if g == 0:
                gsum[rows, ecols] = terms + pre
                continue
            if g == 1:
                gsum[0:64, ecols] = jax.nn.sigmoid(gsum[0:64, ecols])
                gsum[rows, ecols] = jax.nn.sigmoid(terms + pre)
                continue
            update, reset = gsum[part, ecols], gsum[64 + lo - 128:64 + hi - 128, ecols]
            cand = jnp.tanh(terms + reset * pre)
            mk = (lax.broadcasted_iota(jnp.int32, (1, 256), 1) + n * 256 < nvalid).astype(F32)
            ms = state[part, cols].astype(F32) * mk
            out[part, cols] = ((update * ms + (1.0 - update) * cand) * mk).astype(BF)
            cp = pltpu.make_async_copy(out.at[part, cols], out_hbm.at[part, cols], lsem.at[5])
            cp.start()

    swap(0)
    unpool(0)
    m_vh.recv()
    second(0)
    second(15)
    unpool(1)
    unpool(2)
    unpool(3)

    for m in groups[len(early):]:
        m.sent()
    pltpu.make_async_copy(out, out_hbm, lsem.at[5]).wait()
    assert len(groups) == N_MSG


def body(
    state, inputs, adj_tiles, adj_cols, valid_rows, cluster_of, w_gates, w_input, bias, w_value,
    source_emb, target_emb, coarse_tiles, coarse_cols,
):
    vm = pl.BlockSpec(memory_space=pltpu.VMEM)
    sm = pl.BlockSpec(memory_space=pltpu.SMEM)
    hb = pl.BlockSpec(memory_space=pl.ANY)
    V = pltpu.VMEM
    return pl.pallas_call(
        kernel,
        out_shape=jax.ShapeDtypeStruct(state.shape, BF),
        in_specs=[vm, vm, hb, sm, sm, vm, hb, vm, vm, vm, hb, hb, hb, sm],
        out_specs=hb,
        scratch_shapes=[
            V((512, 2304), BF),
            V((8, 2, 64, 128), BF),
            V((512, 2048), BF),
            V((64, 2048), BF),
            V((512, 2048), BF),
            V((2, 4, 2, 64, 256), BF),
            V((2, 8, 256), F32),
            V((4, 2, 64, 256), BF),
            V((8, 256), F32),
            V((4, 2, 64, 256), BF),
            V((8, 256), F32),
            V((7, 64, 256), BF),
            V((7, 1, 256), F32),
            V((10, 1, 256), F32),
            V((16, 4096), F32),
            V((96, 4096), BF),
            V((96, 256), BF),
            V((4096, 256), F32),
            V((4096, 256), BF),
            V((16, 64, 256), BF),
            V((2, 8, 64, 128), BF),
            V((32, 64, 128), BF),
            V((32, 64, 128), BF),
            V((32, 32, 128), BF),
            V((32, 32, 128), BF),
            V((8, 64, 512), BF),
            V((8, 32, 512), BF),
            V((192, 2304), BF),
            V((192, 2304), BF),
            V((192, 2304), F32),
            V((192, 2304), F32),
            V((64, 2048), BF),
            V((16, 512, 128), BF),
            V((192, 4, 512), BF),
            V((768, 512), BF),
            V((32, 256, 128), BF),
            pltpu.SemaphoreType.DMA((N_MSG,)),
            pltpu.SemaphoreType.DMA((N_MSG,)),
            pltpu.SemaphoreType.DMA((6,)),
        ],
        compiler_params=pltpu.CompilerParams(collective_id=0, has_side_effects=True),
    )(
        state, inputs, adj_tiles.reshape(16, 512, 128), adj_cols.T, valid_rows,
        cluster_of.reshape(1, 2048), w_gates.reshape(192, 4, 512),
        jnp.transpose(w_input, (0, 2, 1)), bias, w_value.reshape(64, 64),
        jnp.transpose(source_emb, (1, 0, 2)), jnp.transpose(target_emb, (1, 0, 2)),
        coarse_tiles.reshape(32, 256, 128), coarse_cols.T,
    )


def solution(mesh):
    return jax.shard_map(
        body,
        mesh=mesh,
        in_specs=(
            P("feat", "dom"),
            P(None, "dom"),
            P("dom", None, None, None),
            P("dom", None),
            P("dom"),
            P("dom"),
            P(None, "feat", None, None),
            P(None, "feat", None),
            P(None, "feat"),
            P("feat", None, None),
            P("feat", None, None),
            P("feat", None, None),
            P(),
            P(),
        ),
        out_specs=P("feat", "dom"),
        check_vma=False,
    )
```

```python
import jax
import jax.numpy as jnp
from jax import lax
from jax.experimental import pallas as pl
from jax.experimental.pallas import tpu as pltpu
from jax.sharding import PartitionSpec as P

MESH = pl.DeviceIdType.MESH
BF = jnp.bfloat16
F32 = jnp.float32
N_MSG = 24


def dot(a, b, dims=((1,), (0,))):
    return lax.dot_general(a, b, (dims, ((), ())), preferred_element_type=F32)


def split3(v):
    a = v.astype(BF)
    r = v - a.astype(F32)
    b = r.astype(BF)
    c = (r - b.astype(F32)).astype(BF)
    return a, b, c


def kernel(
    state, xin, adj_hbm, adj_cols, valid, cluster, wg_hbm, w_in, bias, w_val, src_hbm, tgt_hbm,
    ct_hbm, ccols, out,
    mext, halo, ohlo, base, pl_lhs, pool, pcnt, r1, c1, s1, s1cnt, rs, rscnt, src, tgt, t6, s6, scores, expo,
    vals, ca, gall0, gall1, gall2, gmix, ubuf, vbuf, w1m, gsum, adj, wraw, wg, ct,
    ssem, rsem, lsem,
):
    d = lax.axis_index("dom")
    f = lax.axis_index("feat")
    core, x, yh = d % 2, (d // 2) % 4, d // 8
    z, yl = f // 2, f % 2
    zp, zm = (z + 1) % 4, (z + 3) % 4
    dev = lambda i: (i, f)
    fdev = lambda i: (d, i)
    partner = dev(d + 1 - 2 * core)
    hops = [(2, 1), (1, 1), (3, 1), (2, 0), (0, 1), (1, 0), (3, 0)]
    chip = lambda a, b: ((yh + b) % 2) * 8 + ((x + a) % 4) * 2
    chips = [dev(chip(a, b) + core) for a, b in hops]
    dleft, dright = dev((d + 15) % 16), dev((d + 1) % 16)
    fi = lambda a, b: a * 2 + b
    fy, fzp, fzm = f + 1 - 2 * yl, fi(zp, yl), fi(zm, yl)
    f_peers = [fdev((f + k) % 8) for k in range(1, 8)]

    groups = []

    class Group:
        def __init__(self, whole):
            self.whole, self.sems = whole, (ssem.at[len(groups)], rsem.at[len(groups)])
            groups.append(self)

        def copy(self, src_ref, dst_ref, to):
            return pltpu.make_async_remote_copy(
                src_ref=src_ref, dst_ref=dst_ref, send_sem=self.sems[0], recv_sem=self.sems[1],
                device_id=to, device_id_type=MESH,
            )

        def send(self, src_ref, dst_ref, to):
            self.copy(src_ref, dst_ref, to).start()

        def same(self, ref, *to):
            for i in to:
                self.send(ref, ref, i)

        def recv(self):
            self.copy(self.whole, self.whole, partner).wait_recv()

        def sent(self):
            self.copy(self.whole, self.whole, partner).wait_send()

    mine = pl.ds(pl.multiple_of(d * 256, 256), 256)
    loc = [
        pltpu.make_async_copy(wg_hbm, wraw, lsem.at[0]),
        pltpu.make_async_copy(adj_hbm, adj, lsem.at[1]),
        pltpu.make_async_copy(ct_hbm, ct, lsem.at[2]),
    ]
    tgt_rows = [pltpu.make_async_copy(tgt_hbm.at[r], tgt.at[pl.ds(r, 1)], lsem.at[3]) for r in range(10)]
    src_rows = pltpu.make_async_copy(src_hbm.at[:, :, mine], src, lsem.at[4])
    for c in tgt_rows + [src_rows] + loc:
        c.start()

    barrier = pltpu.get_barrier_semaphore()
    cross = dev((d + 15 + 2 * core) % 16)
    peers = [partner, cross] + chips + f_peers
    for p in peers:
        pl.semaphore_signal(barrier, inc=1, device_id=p, device_id_type=MESH)

    nvalid = valid[0]
    mask = (lax.broadcasted_iota(jnp.int32, (1, 2048), 1) < nvalid).astype(F32)
    masked32 = state[...].astype(F32) * mask
    myrows = pl.ds(pl.multiple_of(f * 64, 64), 64)
    own = pl.ds(128, 2048)
    base[...] = masked32.astype(BF)
    mext[myrows, own] = base[...]
    low = cluster[...] & 511
    high = cluster[...] >> 9
    row8 = lax.broadcasted_iota(jnp.int32, (8, 2048), 0)
    cnt_lhs = jnp.where(high == (row8 & 1) * 4 + (row8 >> 1), mask, 0.0).astype(BF)

    def pool_part(c, to_core):
        rows = pl.ds(pl.multiple_of(to_core * 256, 256), 256)
        row = lax.broadcasted_iota(jnp.int32, (256, 2048), 0) + to_core * 256
        ohlo[rows, :] = (row == low).astype(F32).astype(BF)
        for i in range(2):
            if c == 0:
                for slot in range(i * 4, i * 4 + 4):
                    hit = high == (slot % 2) * 4 + slot // 2
                    pl_lhs[slot * 64:(slot + 1) * 64, :] = base[...] * hit.astype(F32).astype(BF)
            res = dot(pl_lhs[i * 256:(i + 1) * 256, :], ohlo[rows, :], ((1,), (1,))).astype(BF)
            for k in range(4):
                slot = i * 4 + k
                pool[c, slot // 2, slot % 2] = res[k * 64:(k + 1) * 64]
        pcnt[c] = dot(cnt_lhs, ohlo[rows, :], ((1,), (1,)))

    pool_part(0, 1 - core)

    pl.semaphore_wait(barrier, len(peers))

    m_r1, m_c1 = Group(r1), Group(c1)
    m_r1.send(pool.at[0], r1, partner)
    m_c1.send(pcnt.at[0], c1, partner)
    mrow = lambda i: mext.at[pl.ds(pl.multiple_of(i * 64, 64), 64), own]
    mhalf = lambda i, h: mext.at[pl.ds(pl.multiple_of(i * 64 + h * 32, 32), 32), own]
    st_y = [Group(expo.at[0:n]) for n in (256, 320)]
    st_yz = [Group(expo.at[0:n]) for n in (512, 640)]
    st_z, st_far = Group(expo.at[0:1152]), Group(expo.at[0:1152])
    m_h = Group(halo.at[0])
    m_h.send(mext.at[myrows, pl.ds(128, 128)], halo.at[f, 1], dleft)
    m_h.send(mext.at[myrows, pl.ds(2048, 128)], halo.at[f, 0], dright)
    st_y[0].same(mhalf(f, 0), fdev(fy))
    st_z.same(mrow(f), fdev(fzp), fdev(fzm))
    pool_part(1, core)

    pltpu.make_async_copy(expo.at[0:320], expo.at[0:320], lsem.at[3]).wait()
    src_rows.wait()
    t6[...] = jnp.zeros_like(t6)
    s6[...] = jnp.zeros_like(s6)
    ta, tb, tc = split3(tgt[0:10, :])
    sa, sb, sc = split3(jnp.concatenate([src[r] for r in range(10)], axis=0))
    for k, (t, s) in enumerate([(ta, sa), (ta, sb), (tb, sa), (ta, sc), (tb, sb), (tc, sa)]):
        t6[k * 16:k * 16 + 10, :] = t
        s6[k * 16:k * 16 + 10, :] = s

    def score_step(j, peak):
        cols = pl.ds(pl.multiple_of(j * 512, 512), 512)
        s = jnp.maximum(dot(t6[:, cols], s6[...], ((0,), (0,))), 0.0)
        scores[cols, :] = s
        return jnp.maximum(peak, jnp.max(s.reshape(64, 8, 256), axis=0))

    m_r1.recv()
    m_c1.recv()
    s1[...] = (pool[1].astype(F32) + r1[...].astype(F32)).astype(BF)
    s1cnt[...] = pcnt[1] + c1[...]
    m_rs, m_rc = Group(rs.at[0:7]), Group(rscnt.at[0:7])
    for k, (a, b) in enumerate(hops):
        xx, yy = (x + a) % 4, (yh + b) % 2
        m_rs.send(s1.at[xx, yy], rs.at[k], chips[k])
        m_rc.send(s1cnt.at[pl.ds(xx * 2 + yy, 1)], rscnt.at[k], chips[k])

    peak = lax.fori_loop(0, 4, score_step, jnp.zeros((8, 256), F32))
    m_h.recv()
    st_y[1].same(mhalf(f, 1), fdev(fy))
    st_y[1].same(halo.at[f], fdev(fy))
    st_z.same(halo.at[f], fdev(fzp), fdev(fzm))
    peak = lax.fori_loop(4, 8, score_step, peak)
    peak = jnp.max(peak, axis=0, keepdims=True)

    def exp_step(j, total):
        cols = pl.ds(pl.multiple_of(j * 512, 512), 512)
        e = jnp.exp(scores[cols, :] - peak)
        expo[cols, :] = e.astype(BF)
        return total + jnp.sum(e.reshape(64, 8, 256), axis=0)

    total = lax.fori_loop(0, 8, exp_step, jnp.zeros((8, 256), F32))
    inv = 1.0 / jnp.sum(total, axis=0, keepdims=True)

    st_y[0].recv()
    st_yz[0].same(mhalf(fy, 0), fdev(fzp), fdev(fzm))
    st_z.recv()
    st_far.same(mhalf(fzm, 0), fdev(fzp))
    st_far.same(mhalf(fzp, 1), fdev(fzm))
    st_far.same(halo.at[fzm, 0], fdev(fzp))
    st_far.same(halo.at[fzp, 1], fdev(fzm))
    m_rs.recv()
    m_rc.recv()
    sums, cnt = s1[x, yh].astype(F32), s1cnt[pl.ds(x * 2 + yh, 1), :]
    for k in range(7):
        sums = sums + rs[k].astype(F32)
        cnt = cnt + rscnt[k]
    pooled = sums / jnp.maximum(cnt, 1.0)
    pa, pb, pc = split3(pooled)
    wv = w_val[...]
    vals[d] = (dot(wv, pa) + dot(wv, pb) + dot(wv, pc)).astype(BF)

    near, far = Group(vals.at[0:4]), Group(vals.at[0:3])
    for k in range(7):
        (far if k < 3 else near).same(vals.at[d], chips[k])
    swap_near, swap_far = Group(vals.at[0:5]), Group(vals.at[0:3])
    swap_near.same(vals.at[d], partner)

    st_y[1].recv()
    st_yz[1].same(mhalf(fy, 1), fdev(fzp), fdev(fzm))
    st_yz[1].same(halo.at[fy], fdev(fzp), fdev(fzm))
    loc[0].wait()
    for k in range(4):
        wg[k * 192:(k + 1) * 192, :] = wraw[:, k, :]

    def attend(total, slots):
        for i in slots:
            rows = pl.ds(pl.multiple_of(i * 256, 256), 256)
            total = total + dot(vals[i], expo[rows, :])
        return total

    st_yz[0].recv()
    st_far.same(mhalf(fi(zm, 1 - yl), 0), fdev(fzp))
    mine_of = lambda ks, c: [chip(*hops[k]) + c for k in ks]
    near.recv()
    for i in mine_of(range(3, 7), core):
        swap_near.same(vals.at[i], partner)
    att = attend(jnp.zeros((64, 256), F32), [d] + mine_of(range(3, 7), core))
    far.recv()
    for i in mine_of(range(3), core):
        swap_far.same(vals.at[i], partner)
    swap_near.recv()
    att = attend(att, mine_of(range(3), core) + [chip(0, 0) + 1 - core])
    att = attend(att, mine_of(range(3, 7), 1 - core))
    swap_far.recv()
    att = attend(att, mine_of(range(3), 1 - core))
    attn = (pooled + att * inv).astype(BF)
    m_ca = [Group(ca.at[0, 0:7]) for h in range(2)]
    for h in range(2):
        ca[h, f] = attn[:, h * 128:(h + 1) * 128]
    for h in range(2):
        m_ca[h].same(ca.at[h, f], *f_peers)
    st_yz[1].recv()
    st_far.same(mhalf(fi(zp, 1 - yl), 1), fdev(fzm))
    st_far.same(halo.at[fi(zp, 1 - yl)], fdev(fzm))
    early = list(groups)
    gall = (gall0, gall1, gall2)
    pieces = ((0, 64), (64, 128), (128, 192))
    slot = lambda g, i: gall[g].at[pl.ds(2 * i, 2)]
    several = lambda n: [Group(gall[g].at[0:2 * n]) for g in range(3)]
    g_x, g_p = several(7), several(8)

    def g_send(g, h):
        g_x[g].same(gall[g].at[2 * d + h], *chips)
        g_p[g].same(gall[g].at[2 * d + h], partner)

    for h in range(2):
        m_ca[h].recv()
        for g, (lo, hi) in enumerate(pieces):
            gall[g][2 * d + h] = dot(wg[576 + lo:576 + hi, :], ca[h].reshape(512, 128)).astype(BF)
            if g == 0 or g == 1 and h == 1:
                g_send(g, h)
        if h == 0:
            g_send(1, 0)
    for h in range(2):
        g_send(2, h)

    st_far.recv()
    for i in range(8):
        mext[i * 64:(i + 1) * 64, 0:128] = halo[i, 0]
        mext[i * 64:(i + 1) * 64, 2176:2304] = halo[i, 1]

    for c in range(9):
        cols = slice(c * 256, (c + 1) * 256)
        r = dot(wg[0:576, :], mext[:, cols])
        gsum[:, cols] = r[0:192]
        w1m[:, cols] = r[192:384]
        ubuf[:, cols] = r[384:576].astype(BF)

    loc[1].wait()

    def diffuse(buf, t):
        lo, mid, hi = (buf[:, (t + k) * 128:(t + k + 1) * 128] for k in range(3))

        def pick(k):
            c = jnp.full((1, 128), adj_cols[k, t], jnp.int32)
            wlo, wmid, whi = ((c == t + i).astype(F32).astype(BF) for i in range(3))
            return lo * wlo + mid * wmid + hi * whi

        lhs = jnp.concatenate([lo, pick(1), pick(2), hi], axis=1)
        r = dot(lhs, adj[t])
        pos = lax.broadcasted_iota(jnp.int32, (1, 128), 1) + t * 128
        return r * (pos < nvalid).astype(F32)

    def first(t):
        cols = slice((t + 1) * 128, (t + 2) * 128)
        vbuf[:, cols] = (w1m[:, cols] + diffuse(ubuf, t)).astype(BF)

    def second(t):
        cols = slice((t + 1) * 128, (t + 2) * 128)
        gsum[:, cols] = gsum[:, cols] + diffuse(vbuf, t)

    first(0)
    first(15)
    tile = lambda i: vbuf.at[:, pl.ds(i * 128, 128)]
    m_vh = Group(vbuf.at[:, 0:256])
    m_vh.send(tile(1), tile(17), dleft)
    m_vh.send(tile(16), tile(0), dright)
    for t in range(1, 15):
        first(t)
    for t in range(1, 15):
        second(t)
    def swap(g):
        g_x[g].recv()
        for i in mine_of(range(7), core):
            g_p[g].same(slot(g, i), partner)

    for m in early:
        m.sent()
    loc[2].wait()
    eye = lax.broadcasted_iota(jnp.int32, (64, 64), 0) == lax.broadcasted_iota(
        jnp.int32, (64, 64), 1
    )
    column = lambda row: jnp.sum(jnp.where(eye, row, 0.0), axis=1, keepdims=True)
    bcol = [column(bias[g:g + 1, :]) for g in range(3)]
    win = [w_in[g].astype(F32) for g in range(3)]
    wcol = [[column(win[g][i:i + 1]) for i in range(2)] for g in range(3)]

    def unpool(p):
        lo, hi = pieces[p]
        rows, count, g = slice(lo, hi), hi - lo, min(p, 2)
        part = slice(lo - 64 * g, hi - 64 * g)
        g_p[p].recv()
        for s in range(8):
            tiles = []
            for t in range(4 * s, 4 * s + 4):
                lhs = jnp.concatenate([gall[p][ccols[k, t]] for k in range(2)], axis=1)
                tiles.append(gall[p][t].astype(F32) + dot(lhs, ct[t]))
            gmix[s] = jnp.concatenate(tiles, axis=1).astype(BF)
        if p < 2:
            swap(p + 1)
        for n in range(8):
            cols = slice(n * 256, (n + 1) * 256)
            ecols = slice(n * 256 + 128, (n + 1) * 256 + 128)
            hi_n = cluster[:, cols] >> 9
            r = dot(gmix[...].reshape(8 * count, 512), ohlo[:, cols])
            acc = r[0:count]
            for s in range(1, 8):
                acc = jnp.where(hi_n == s, r[s * count:(s + 1) * count], acc)
            pre = acc + gsum[rows, ecols]
            xi = xin[:, cols].astype(F32)
            terms = wcol[g][0][part] * xi[0:1] + wcol[g][1][part] * xi[1:2] + bcol[g][part]
            if g == 0:
                gsum[rows, ecols] = terms + pre
                continue
            if g == 1:
                gsum[0:64, ecols] = jax.nn.sigmoid(gsum[0:64, ecols])
                gsum[rows, ecols] = jax.nn.sigmoid(terms + pre)
                continue
            update, reset = gsum[part, ecols], gsum[64 + lo - 128:64 + hi - 128, ecols]
            cand = jnp.tanh(terms + reset * pre)
            mk = (lax.broadcasted_iota(jnp.int32, (1, 256), 1) + n * 256 < nvalid).astype(F32)
            ms = state[part, cols].astype(F32) * mk
            out[part, cols] = ((update * ms + (1.0 - update) * cand) * mk).astype(BF)

    swap(0)
    unpool(0)
    m_vh.recv()
    second(0)
    second(15)
    unpool(1)
    unpool(2)

    for m in groups[len(early):]:
        m.sent()
    assert len(groups) == N_MSG


def body(
    state, inputs, adj_tiles, adj_cols, valid_rows, cluster_of, w_gates, w_input, bias, w_value,
    source_emb, target_emb, coarse_tiles, coarse_cols,
):
    vm = pl.BlockSpec(memory_space=pltpu.VMEM)
    sm = pl.BlockSpec(memory_space=pltpu.SMEM)
    hb = pl.BlockSpec(memory_space=pl.ANY)
    V = pltpu.VMEM
    return pl.pallas_call(
        kernel,
        out_shape=pltpu.VMEM(state.shape, BF),
        in_specs=[vm, vm, hb, sm, sm, vm, hb, vm, vm, vm, hb, hb, hb, sm],
        out_specs=vm,
        scratch_shapes=[
            V((512, 2304), BF),
            V((8, 2, 64, 128), BF),
            V((512, 2048), BF),
            V((64, 2048), BF),
            V((512, 2048), BF),
            V((2, 4, 2, 64, 256), BF),
            V((2, 8, 256), F32),
            V((4, 2, 64, 256), BF),
            V((8, 256), F32),
            V((4, 2, 64, 256), BF),
            V((8, 256), F32),
            V((7, 64, 256), BF),
            V((7, 1, 256), F32),
            V((10, 1, 256), F32),
            V((16, 4096), F32),
            V((96, 4096), BF),
            V((96, 256), BF),
            V((4096, 256), F32),
            V((4096, 256), BF),
            V((16, 64, 256), BF),
            V((2, 8, 64, 128), BF),
            V((32, 64, 128), BF),
            V((32, 64, 128), BF),
            V((32, 64, 128), BF),
            V((8, 64, 512), BF),
            V((192, 2304), BF),
            V((192, 2304), BF),
            V((192, 2304), F32),
            V((192, 2304), F32),
            V((16, 512, 128), BF),
            V((192, 4, 512), BF),
            V((768, 512), BF),
            V((32, 256, 128), BF),
            pltpu.SemaphoreType.DMA((N_MSG,)),
            pltpu.SemaphoreType.DMA((N_MSG,)),
            pltpu.SemaphoreType.DMA((5,)),
        ],
        compiler_params=pltpu.CompilerParams(collective_id=0, has_side_effects=True),
    )(
        state, inputs, adj_tiles.reshape(16, 512, 128), adj_cols.T, valid_rows,
        cluster_of.reshape(1, 2048), w_gates.reshape(192, 4, 512),
        jnp.transpose(w_input, (0, 2, 1)), bias, w_value.reshape(64, 64),
        jnp.transpose(source_emb, (1, 0, 2)), jnp.transpose(target_emb, (1, 0, 2)),
        coarse_tiles.reshape(32, 256, 128), coarse_cols.T,
    )


def solution(mesh):
    return jax.shard_map(
        body,
        mesh=mesh,
        in_specs=(
            P("feat", "dom"),
            P(None, "dom"),
            P("dom", None, None, None),
            P("dom", None),
            P("dom"),
            P("dom"),
            P(None, "feat", None, None),
            P(None, "feat", None),
            P(None, "feat"),
            P("feat", None, None),
            P("feat", None, None),
            P("feat", None, None),
            P(),
            P(),
        ),
        out_specs=P("feat", "dom"),
        check_vma=False,
    )
```

```python
import jax
import jax.numpy as jnp
from jax import lax
from jax.experimental import pallas as pl
from jax.experimental.pallas import tpu as pltpu
from jax.sharding import PartitionSpec as P

MESH = pl.DeviceIdType.MESH
BF = jnp.bfloat16
F32 = jnp.float32
N_MSG = 27


def dot(a, b, dims=((1,), (0,))):
    return lax.dot_general(a, b, (dims, ((), ())), preferred_element_type=F32)


def split3(v):
    a = v.astype(BF)
    r = v - a.astype(F32)
    b = r.astype(BF)
    c = (r - b.astype(F32)).astype(BF)
    return a, b, c


def kernel(
    state, xin, adj_hbm, adj_cols, valid, cluster, wg_hbm, w_in, bias, w_val, src_hbm, tgt_hbm,
    ct_hbm, ccols, out,
    mext, halo, ohlo, base, pl_lhs, pool, pcnt, r1, c1, s1, s1cnt, rs, rscnt, src, tgt, t6, s6, scores, expo, stat, stat_in, part, part_in,
    vals, ca, gall0, gall1, gall2, gmix, ubuf, vbuf, w1m, gsum, adj, wraw, wg, ct,
    ssem, rsem, lsem,
):
    d = lax.axis_index("dom")
    f = lax.axis_index("feat")
    core, x, yh = d % 2, (d // 2) % 4, d // 8
    z, yl = f // 2, f % 2
    zp, zm = (z + 1) % 4, (z + 3) % 4
    dev = lambda i: (i, f)
    fdev = lambda i: (d, i)
    partner = dev(d + 1 - 2 * core)
    hops = [(2, 1), (1, 1), (3, 1), (2, 0), (0, 1), (1, 0), (3, 0)]
    chip = lambda a, b: ((yh + b) % 2) * 8 + ((x + a) % 4) * 2
    chips = [dev(chip(a, b) + core) for a, b in hops]
    dleft, dright = dev((d + 15) % 16), dev((d + 1) % 16)
    fi = lambda a, b: a * 2 + b
    fy, fzp, fzm = f + 1 - 2 * yl, fi(zp, yl), fi(zm, yl)
    z2 = (z + 2) % 4
    f_peers = [fdev(fi(*i)) for i in ((z2, 1 - yl), (z2, yl), (zp, 1 - yl), (zm, 1 - yl))]
    f_peers += [fdev(fzp), fdev(fzm), fdev(fy)]

    groups = []

    class Group:
        def __init__(self, whole):
            self.whole, self.sems = whole, (ssem.at[len(groups)], rsem.at[len(groups)])
            groups.append(self)

        def copy(self, src_ref, dst_ref, to):
            return pltpu.make_async_remote_copy(
                src_ref=src_ref, dst_ref=dst_ref, send_sem=self.sems[0], recv_sem=self.sems[1],
                device_id=to, device_id_type=MESH,
            )

        def send(self, src_ref, dst_ref, to):
            self.copy(src_ref, dst_ref, to).start()

        def same(self, ref, *to):
            for i in to:
                self.send(ref, ref, i)

        def recv(self):
            self.copy(self.whole, self.whole, partner).wait_recv()

        def sent(self):
            self.copy(self.whole, self.whole, partner).wait_send()

    mine = pl.ds(pl.multiple_of((yh * 4 + x) * 512, 512), 512)
    loc = [
        pltpu.make_async_copy(wg_hbm, wraw, lsem.at[0]),
        pltpu.make_async_copy(adj_hbm, adj, lsem.at[1]),
        pltpu.make_async_copy(ct_hbm, ct, lsem.at[2]),
    ]
    tgt_rows = [pltpu.make_async_copy(tgt_hbm.at[r], tgt.at[pl.ds(r, 1)], lsem.at[3]) for r in range(10)]
    src_rows = pltpu.make_async_copy(src_hbm.at[:, :, mine], src, lsem.at[4])
    for c in tgt_rows + [src_rows] + loc:
        c.start()

    barrier = pltpu.get_barrier_semaphore()
    cross = dev((d + 15 + 2 * core) % 16)
    peers = [partner, cross] + chips + f_peers
    for p in peers:
        pl.semaphore_signal(barrier, inc=1, device_id=p, device_id_type=MESH)

    nvalid = valid[0]
    mask = (lax.broadcasted_iota(jnp.int32, (1, 2048), 1) < nvalid).astype(F32)
    masked32 = state[...].astype(F32) * mask
    myrows = pl.ds(pl.multiple_of(f * 64, 64), 64)
    own = pl.ds(128, 2048)
    base[...] = masked32.astype(BF)
    mext[myrows, own] = base[...]
    low = cluster[...] & 511
    high = cluster[...] >> 9
    row8 = lax.broadcasted_iota(jnp.int32, (8, 2048), 0)
    cnt_lhs = jnp.where(high == (row8 & 1) * 4 + (row8 >> 1), mask, 0.0).astype(BF)

    def pool_part(c, to_core):
        rows = pl.ds(pl.multiple_of(to_core * 256, 256), 256)
        row = lax.broadcasted_iota(jnp.int32, (256, 2048), 0) + to_core * 256
        ohlo[rows, :] = (row == low).astype(F32).astype(BF)
        for i in range(2):
            if c == 0:
                for slot in range(i * 4, i * 4 + 4):
                    hit = high == (slot % 2) * 4 + slot // 2
                    pl_lhs[slot * 64:(slot + 1) * 64, :] = base[...] * hit.astype(F32).astype(BF)
            res = dot(pl_lhs[i * 256:(i + 1) * 256, :], ohlo[rows, :], ((1,), (1,))).astype(BF)
            for k in range(4):
                slot = i * 4 + k
                pool[c, slot // 2, slot % 2] = res[k * 64:(k + 1) * 64]
        pcnt[c] = dot(cnt_lhs, ohlo[rows, :], ((1,), (1,)))

    pool_part(0, 1 - core)

    pl.semaphore_wait(barrier, len(peers))

    m_r1, m_c1 = Group(r1), Group(c1)
    m_r1.send(pool.at[0], r1, partner)
    m_c1.send(pcnt.at[0], c1, partner)
    mrow = lambda i: mext.at[pl.ds(pl.multiple_of(i * 64, 64), 64), own]
    mhalf = lambda i, h: mext.at[pl.ds(pl.multiple_of(i * 64 + h * 32, 32), 32), own]
    st_y = [Group(expo.at[0:n]) for n in (128, 160)]
    st_yz = [Group(expo.at[0:n]) for n in (256, 320)]
    st_z, st_far = Group(expo.at[0:576]), Group(expo.at[0:576])
    m_h = Group(halo.at[0])
    m_h.send(mext.at[myrows, pl.ds(128, 128)], halo.at[f, 1], dleft)
    m_h.send(mext.at[myrows, pl.ds(2048, 128)], halo.at[f, 0], dright)
    st_y[0].same(mhalf(f, 0), fdev(fy))
    st_z.same(mrow(f), fdev(fzp), fdev(fzm))
    pool_part(1, core)

    pltpu.make_async_copy(expo.at[0:160], expo.at[0:160], lsem.at[3]).wait()
    src_rows.wait()
    t6[...] = jnp.zeros_like(t6)
    s6[...] = jnp.zeros_like(s6)
    ta, tb, tc = split3(tgt[0:10, :])
    sa, sb, sc = split3(jnp.concatenate([src[r] for r in range(10)], axis=0))
    for k, (t, s) in enumerate([(ta, sa), (ta, sb), (tb, sa), (ta, sc), (tb, sb), (tc, sa)]):
        t6[k * 16:k * 16 + 10, :] = t
        s6[k * 16:k * 16 + 10, :] = s

    def score_step(j, peak):
        cols = pl.ds(pl.multiple_of((j * 2 + core) * 256, 256), 256)
        s = jnp.maximum(dot(t6[:, cols], s6[...], ((0,), (0,))), 0.0)
        scores[pl.ds(pl.multiple_of(j * 256, 256), 256), :] = s
        return jnp.maximum(peak, jnp.max(s.reshape(32, 8, 512), axis=0))

    m_r1.recv()
    m_c1.recv()
    s1[...] = (pool[1].astype(F32) + r1[...].astype(F32)).astype(BF)
    s1cnt[...] = pcnt[1] + c1[...]
    m_rs, m_rc = Group(rs.at[0:7]), Group(rscnt.at[0:7])
    for k, (a, b) in enumerate(hops):
        xx, yy = (x + a) % 4, (yh + b) % 2
        m_rs.send(s1.at[xx, yy], rs.at[k], chips[k])
        m_rc.send(s1cnt.at[pl.ds(xx * 2 + yy, 1)], rscnt.at[k], chips[k])

    peak = lax.fori_loop(0, 4, score_step, jnp.zeros((8, 512), F32))
    m_h.recv()
    st_y[1].same(mhalf(f, 1), fdev(fy))
    st_y[1].same(halo.at[f], fdev(fy))
    st_z.same(halo.at[f], fdev(fzp), fdev(fzm))
    peak = lax.fori_loop(4, 8, score_step, peak)
    peak = jnp.max(peak, axis=0, keepdims=True)

    def exp_step(j, total):
        rows = pl.ds(pl.multiple_of(j * 256, 256), 256)
        e = jnp.exp(scores[rows, :] - peak)
        expo[rows, :] = e.astype(BF)
        return total + jnp.sum(e.reshape(32, 8, 512), axis=0)

    total = lax.fori_loop(0, 8, exp_step, jnp.zeros((8, 512), F32))
    total = jnp.sum(total, axis=0, keepdims=True)
    both = jnp.concatenate([peak, total], axis=0)
    for h in range(2):
        stat[h] = both[:, h * 256:(h + 1) * 256]
    m_stat = Group(stat_in)
    m_stat.send(stat.at[1 - core], stat_in, partner)

    st_y[0].recv()
    st_yz[0].same(mhalf(fy, 0), fdev(fzp), fdev(fzm))
    st_z.recv()
    st_far.same(mhalf(fzm, 0), fdev(fzp))
    st_far.same(mhalf(fzp, 1), fdev(fzm))
    st_far.same(halo.at[fzm, 0], fdev(fzp))
    st_far.same(halo.at[fzp, 1], fdev(fzm))
    m_rs.recv()
    m_rc.recv()
    sums, cnt = s1[x, yh].astype(F32), s1cnt[pl.ds(x * 2 + yh, 1), :]
    for k in range(7):
        sums = sums + rs[k].astype(F32)
        cnt = cnt + rscnt[k]
    pooled = sums / jnp.maximum(cnt, 1.0)
    pa, pb, pc = split3(pooled)
    wv = w_val[...]
    vals[d] = (dot(wv, pa) + dot(wv, pb) + dot(wv, pc)).astype(BF)

    near, far = Group(vals.at[0:4]), Group(vals.at[0:3])
    for k in range(7):
        (far if k < 3 else near).same(vals.at[d], chips[k])
    st_y[1].recv()
    st_yz[1].same(mhalf(fy, 1), fdev(fzp), fdev(fzm))
    st_yz[1].same(halo.at[fy], fdev(fzp), fdev(fzm))
    loc[0].wait()
    for k in range(4):
        wg[k * 192:(k + 1) * 192, :] = wraw[:, k, :]

    def attend(total, chips_at):
        for i in chips_at:
            rows = pl.ds(pl.multiple_of(i * 128, 256), 256)
            total = total + dot(vals[i + core], expo[rows, :])
        return total

    st_yz[0].recv()
    st_far.same(mhalf(fi(zm, 1 - yl), 0), fdev(fzp))
    mine_of = lambda ks, c: [chip(*hops[k]) + c for k in ks]
    at = lambda ks: [chip(*hops[k]) for k in ks]
    near.recv()
    att = attend(jnp.zeros((64, 512), F32), [chip(0, 0)] + at(range(3, 7)))
    far.recv()
    att = attend(att, at(range(3)))
    for h in range(2):
        part[h] = att[:, h * 256:(h + 1) * 256]
    m_part = Group(part_in)
    m_part.send(part.at[1 - core], part_in, partner)
    m_stat.recv()
    peaks = stat[core, 0:1, :], stat_in[0:1, :]
    top = jnp.maximum(*peaks)
    wa, wb = (jnp.exp(i - top) for i in peaks)
    inv = 1.0 / (stat[core, 1:2, :] * wa + stat_in[1:2, :] * wb)
    m_part.recv()
    attn = (pooled + part[core] * (wa * inv) + part_in[...] * (wb * inv)).astype(BF)
    m_ca = [Group(ca.at[0, 0:7]) for h in range(2)]
    for h in range(2):
        ca[h, f] = attn[:, h * 128:(h + 1) * 128]
    for h in range(2):
        m_ca[h].same(ca.at[h, f], *f_peers)
    st_yz[1].recv()
    st_far.same(mhalf(fi(zp, 1 - yl), 1), fdev(fzm))
    st_far.same(halo.at[fi(zp, 1 - yl)], fdev(fzm))
    early = list(groups)
    gall = (gall0, gall1, gall2)
    pieces = ((0, 64), (64, 128), (128, 192))
    slot = lambda g, i: gall[g].at[pl.ds(2 * i, 2)]
    several = lambda n: [Group(gall[g].at[0:2 * n]) for g in range(3)]
    g_far, g_near, g_p = several(3), several(4), several(8)

    def g_send(g, h):
        g_far[g].same(gall[g].at[2 * d + h], *chips[:3])
        g_near[g].same(gall[g].at[2 * d + h], *chips[3:])
        g_p[g].same(gall[g].at[2 * d + h], partner)

    for h in range(2):
        m_ca[h].recv()
        for g, (lo, hi) in enumerate(pieces):
            gall[g][2 * d + h] = dot(wg[576 + lo:576 + hi, :], ca[h].reshape(512, 128)).astype(BF)
            if g == 0 or g == 1 and h == 1:
                g_send(g, h)
        if h == 0:
            g_send(1, 0)
    for h in range(2):
        g_send(2, h)

    st_far.recv()
    for i in range(8):
        mext[i * 64:(i + 1) * 64, 0:128] = halo[i, 0]
        mext[i * 64:(i + 1) * 64, 2176:2304] = halo[i, 1]

    for c in range(9):
        cols = slice(c * 256, (c + 1) * 256)
        r = dot(wg[0:576, :], mext[:, cols])
        gsum[:, cols] = r[0:192]
        w1m[:, cols] = r[192:384]
        ubuf[:, cols] = r[384:576].astype(BF)

    loc[1].wait()

    def diffuse(buf, t):
        lo, mid, hi = (buf[:, (t + k) * 128:(t + k + 1) * 128] for k in range(3))

        def pick(k):
            c = jnp.full((1, 128), adj_cols[k, t], jnp.int32)
            wlo, wmid, whi = ((c == t + i).astype(F32).astype(BF) for i in range(3))
            return lo * wlo + mid * wmid + hi * whi

        lhs = jnp.concatenate([lo, pick(1), pick(2), hi], axis=1)
        r = dot(lhs, adj[t])
        pos = lax.broadcasted_iota(jnp.int32, (1, 128), 1) + t * 128
        return r * (pos < nvalid).astype(F32)

    def first(t):
        cols = slice((t + 1) * 128, (t + 2) * 128)
        vbuf[:, cols] = (w1m[:, cols] + diffuse(ubuf, t)).astype(BF)

    def second(t):
        cols = slice((t + 1) * 128, (t + 2) * 128)
        gsum[:, cols] = gsum[:, cols] + diffuse(vbuf, t)

    first(0)
    first(15)
    tile = lambda i: vbuf.at[:, pl.ds(i * 128, 128)]
    m_vh = Group(vbuf.at[:, 0:256])
    m_vh.send(tile(1), tile(17), dleft)
    m_vh.send(tile(16), tile(0), dright)
    for t in range(1, 15):
        first(t)
    for t in range(1, 15):
        second(t)
    def swap(g):
        for group, ks in ((g_near, range(3, 7)), (g_far, range(3))):
            group[g].recv()
            for i in mine_of(ks, core):
                g_p[g].same(slot(g, i), partner)

    for m in early:
        m.sent()
    loc[2].wait()
    eye = lax.broadcasted_iota(jnp.int32, (64, 64), 0) == lax.broadcasted_iota(
        jnp.int32, (64, 64), 1
    )
    column = lambda row: jnp.sum(jnp.where(eye, row, 0.0), axis=1, keepdims=True)
    bcol = [column(bias[g:g + 1, :]) for g in range(3)]
    win = [w_in[g].astype(F32) for g in range(3)]
    wcol = [[column(win[g][i:i + 1]) for i in range(2)] for g in range(3)]

    def unpool(p):
        lo, hi = pieces[p]
        rows, count, g = slice(lo, hi), hi - lo, min(p, 2)
        part = slice(lo - 64 * g, hi - 64 * g)
        g_p[p].recv()
        for s in range(8):
            tiles = []
            for t in range(4 * s, 4 * s + 4):
                lhs = jnp.concatenate([gall[p][ccols[k, t]] for k in range(2)], axis=1)
                tiles.append(gall[p][t].astype(F32) + dot(lhs, ct[t]))
            gmix[s] = jnp.concatenate(tiles, axis=1).astype(BF)
        if p < 2:
            swap(p + 1)
        for n in range(8):
            cols = slice(n * 256, (n + 1) * 256)
            ecols = slice(n * 256 + 128, (n + 1) * 256 + 128)
            hi_n = cluster[:, cols] >> 9
            r = dot(gmix[...].reshape(8 * count, 512), ohlo[:, cols])
            acc = r[0:count]
            for s in range(1, 8):
                acc = jnp.where(hi_n == s, r[s * count:(s + 1) * count], acc)
            pre = acc + gsum[rows, ecols]
            xi = xin[:, cols].astype(F32)
            terms = wcol[g][0][part] * xi[0:1] + wcol[g][1][part] * xi[1:2] + bcol[g][part]
            if g == 0:
                gsum[rows, ecols] = terms + pre
                continue
            if g == 1:
                gsum[0:64, ecols] = jax.nn.sigmoid(gsum[0:64, ecols])
                gsum[rows, ecols] = jax.nn.sigmoid(terms + pre)
                continue
            update, reset = gsum[part, ecols], gsum[64 + lo - 128:64 + hi - 128, ecols]
            cand = jnp.tanh(terms + reset * pre)
            mk = (lax.broadcasted_iota(jnp.int32, (1, 256), 1) + n * 256 < nvalid).astype(F32)
            ms = state[part, cols].astype(F32) * mk
            out[part, cols] = ((update * ms + (1.0 - update) * cand) * mk).astype(BF)

    swap(0)
    unpool(0)
    m_vh.recv()
    second(0)
    second(15)
    unpool(1)
    unpool(2)

    for m in groups[len(early):]:
        m.sent()
    assert len(groups) == N_MSG


def body(
    state, inputs, adj_tiles, adj_cols, valid_rows, cluster_of, w_gates, w_input, bias, w_value,
    source_emb, target_emb, coarse_tiles, coarse_cols,
):
    vm = pl.BlockSpec(memory_space=pltpu.VMEM)
    sm = pl.BlockSpec(memory_space=pltpu.SMEM)
    hb = pl.BlockSpec(memory_space=pl.ANY)
    V = pltpu.VMEM
    return pl.pallas_call(
        kernel,
        out_shape=pltpu.VMEM(state.shape, BF),
        in_specs=[vm, vm, hb, sm, sm, vm, hb, vm, vm, vm, hb, hb, hb, sm],
        out_specs=vm,
        scratch_shapes=[
            V((512, 2304), BF),
            V((8, 2, 64, 128), BF),
            V((512, 2048), BF),
            V((64, 2048), BF),
            V((512, 2048), BF),
            V((2, 4, 2, 64, 256), BF),
            V((2, 8, 256), F32),
            V((4, 2, 64, 256), BF),
            V((8, 256), F32),
            V((4, 2, 64, 256), BF),
            V((8, 256), F32),
            V((7, 64, 256), BF),
            V((7, 1, 256), F32),
            V((10, 1, 512), F32),
            V((16, 4096), F32),
            V((96, 4096), BF),
            V((96, 512), BF),
            V((2048, 512), F32),
            V((2048, 512), BF),
            V((2, 2, 256), F32),
            V((2, 256), F32),
            V((2, 64, 256), F32),
            V((64, 256), F32),
            V((16, 64, 256), BF),
            V((2, 8, 64, 128), BF),
            V((32, 64, 128), BF),
            V((32, 64, 128), BF),
            V((32, 64, 128), BF),
            V((8, 64, 512), BF),
            V((192, 2304), BF),
            V((192, 2304), BF),
            V((192, 2304), F32),
            V((192, 2304), F32),
            V((16, 512, 128), BF),
            V((192, 4, 512), BF),
            V((768, 512), BF),
            V((32, 256, 128), BF),
            pltpu.SemaphoreType.DMA((N_MSG,)),
            pltpu.SemaphoreType.DMA((N_MSG,)),
            pltpu.SemaphoreType.DMA((5,)),
        ],
        compiler_params=pltpu.CompilerParams(collective_id=0, has_side_effects=True),
    )(
        state, inputs, adj_tiles.reshape(16, 512, 128), adj_cols.T, valid_rows,
        cluster_of.reshape(1, 2048), w_gates.reshape(192, 4, 512),
        jnp.transpose(w_input, (0, 2, 1)), bias, w_value.reshape(64, 64),
        jnp.transpose(source_emb, (1, 0, 2)), jnp.transpose(target_emb, (1, 0, 2)),
        coarse_tiles.reshape(32, 256, 128), coarse_cols.T,
    )


def solution(mesh):
    return jax.shard_map(
        body,
        mesh=mesh,
        in_specs=(
            P("feat", "dom"),
            P(None, "dom"),
            P("dom", None, None, None),
            P("dom", None),
            P("dom"),
            P("dom"),
            P(None, "feat", None, None),
            P(None, "feat", None),
            P(None, "feat"),
            P("feat", None, None),
            P("feat", None, None),
            P("feat", None, None),
            P(),
            P(),
        ),
        out_specs=P("feat", "dom"),
        check_vma=False,
    )
```

```python
import jax
import jax.numpy as jnp
from jax import lax
from jax.experimental import pallas as pl
from jax.experimental.pallas import tpu as pltpu
from jax.sharding import PartitionSpec as P

MESH = pl.DeviceIdType.MESH
BF = jnp.bfloat16
F32 = jnp.float32
N_MSG = 27


def dot(a, b, dims=((1,), (0,))):
    return lax.dot_general(a, b, (dims, ((), ())), preferred_element_type=F32)


def split3(v):
    a = v.astype(BF)
    r = v - a.astype(F32)
    b = r.astype(BF)
    c = (r - b.astype(F32)).astype(BF)
    return a, b, c


def kernel(
    state, xin, adj_hbm, adj_cols, valid, cluster, wg_hbm, w_in, bias, w_val, src_hbm, tgt_hbm,
    ct_hbm, ccols, out,
    mext, halo, ohlo, base, pl_lhs, pool, pcnt, r1, c1, s1, s1cnt, rs, rscnt, src, tgt, t6, s6, scores, expo, stat, stat_in, part, part_in,
    vals, ca, gall0, gall1, gall2, gmix, ubuf, vbuf, w1m, gsum, adj, wraw, wg, ct,
    ssem, rsem, lsem,
):
    d = lax.axis_index("dom")
    f = lax.axis_index("feat")
    core, x, yh = d % 2, (d // 2) % 4, d // 8
    z, yl = f // 2, f % 2
    zp, zm = (z + 1) % 4, (z + 3) % 4
    dev = lambda i: (i, f)
    fdev = lambda i: (d, i)
    partner = dev(d + 1 - 2 * core)
    hops = [(2, 1), (1, 1), (3, 1), (2, 0), (0, 1), (1, 0), (3, 0)]
    chip = lambda a, b: ((yh + b) % 2) * 8 + ((x + a) % 4) * 2
    chips = [dev(chip(a, b) + core) for a, b in hops]
    dleft, dright = dev((d + 15) % 16), dev((d + 1) % 16)
    fi = lambda a, b: a * 2 + b
    fy, fzp, fzm = f + 1 - 2 * yl, fi(zp, yl), fi(zm, yl)
    z2 = (z + 2) % 4
    f_peers = [fdev(fi(*i)) for i in ((z2, 1 - yl), (z2, yl), (zp, 1 - yl), (zm, 1 - yl))]
    f_peers += [fdev(fzp), fdev(fzm), fdev(fy)]

    groups = []

    class Group:
        def __init__(self, whole):
            self.whole, self.sems = whole, (ssem.at[len(groups)], rsem.at[len(groups)])
            groups.append(self)

        def copy(self, src_ref, dst_ref, to):
            return pltpu.make_async_remote_copy(
                src_ref=src_ref, dst_ref=dst_ref, send_sem=self.sems[0], recv_sem=self.sems[1],
                device_id=to, device_id_type=MESH,
            )

        def send(self, src_ref, dst_ref, to):
            self.copy(src_ref, dst_ref, to).start()

        def same(self, ref, *to):
            for i in to:
                self.send(ref, ref, i)

        def recv(self):
            self.copy(self.whole, self.whole, partner).wait_recv()

        def sent(self):
            self.copy(self.whole, self.whole, partner).wait_send()

    mine = pl.ds(pl.multiple_of((yh * 4 + x) * 512, 512), 512)
    loc = [
        pltpu.make_async_copy(wg_hbm, wraw, lsem.at[0]),
        pltpu.make_async_copy(adj_hbm, adj, lsem.at[1]),
        pltpu.make_async_copy(ct_hbm, ct, lsem.at[2]),
    ]
    tgt_rows = [pltpu.make_async_copy(tgt_hbm.at[r], tgt.at[pl.ds(r, 1)], lsem.at[3]) for r in range(10)]
    src_rows = pltpu.make_async_copy(src_hbm.at[:, :, mine], src, lsem.at[4])
    for c in tgt_rows + [src_rows] + loc:
        c.start()

    barrier = pltpu.get_barrier_semaphore()
    cross = dev((d + 15 + 2 * core) % 16)
    peers = [partner, cross] + chips + f_peers
    for p in peers:
        pl.semaphore_signal(barrier, inc=1, device_id=p, device_id_type=MESH)

    nvalid = valid[0]
    mask = (lax.broadcasted_iota(jnp.int32, (1, 2048), 1) < nvalid).astype(F32)
    masked32 = state[...].astype(F32) * mask
    myrows = pl.ds(pl.multiple_of(f * 64, 64), 64)
    own = pl.ds(128, 2048)
    base[...] = masked32.astype(BF)
    mext[myrows, own] = base[...]
    low = cluster[...] & 511
    high = cluster[...] >> 9
    row8 = lax.broadcasted_iota(jnp.int32, (8, 2048), 0)
    cnt_lhs = jnp.where(high == (row8 & 1) * 4 + (row8 >> 1), mask, 0.0).astype(BF)

    def pool_part(c, to_core):
        rows = pl.ds(pl.multiple_of(to_core * 256, 256), 256)
        row = lax.broadcasted_iota(jnp.int32, (256, 2048), 0) + to_core * 256
        ohlo[rows, :] = (row == low).astype(F32).astype(BF)
        for i in range(2):
            if c == 0:
                for slot in range(i * 4, i * 4 + 4):
                    hit = high == (slot % 2) * 4 + slot // 2
                    pl_lhs[slot * 64:(slot + 1) * 64, :] = base[...] * hit.astype(F32).astype(BF)
            res = dot(pl_lhs[i * 256:(i + 1) * 256, :], ohlo[rows, :], ((1,), (1,))).astype(BF)
            for k in range(4):
                slot = i * 4 + k
                pool[c, slot // 2, slot % 2] = res[k * 64:(k + 1) * 64]
        pcnt[c] = dot(cnt_lhs, ohlo[rows, :], ((1,), (1,)))

    pool_part(0, 1 - core)

    pl.semaphore_wait(barrier, len(peers))

    m_r1, m_c1 = Group(r1), Group(c1)
    m_r1.send(pool.at[0], r1, partner)
    m_c1.send(pcnt.at[0], c1, partner)
    mrow = lambda i: mext.at[pl.ds(pl.multiple_of(i * 64, 64), 64), own]
    mhalf = lambda i, h: mext.at[pl.ds(pl.multiple_of(i * 64 + h * 32, 32), 32), own]
    st_y = [Group(expo.at[0:n]) for n in (128, 160)]
    st_yz = [Group(expo.at[0:n]) for n in (256, 320)]
    st_z, st_far = Group(expo.at[0:576]), Group(expo.at[0:576])
    m_h = Group(halo.at[0])
    m_h.send(mext.at[myrows, pl.ds(128, 128)], halo.at[f, 1], dleft)
    m_h.send(mext.at[myrows, pl.ds(2048, 128)], halo.at[f, 0], dright)
    st_y[0].same(mhalf(f, 0), fdev(fy))
    st_z.same(mrow(f), fdev(fzp), fdev(fzm))
    pool_part(1, core)

    pltpu.make_async_copy(expo.at[0:160], expo.at[0:160], lsem.at[3]).wait()
    src_rows.wait()
    t6[...] = jnp.zeros_like(t6)
    s6[...] = jnp.zeros_like(s6)
    ta, tb, tc = split3(tgt[0:10, :])
    sa, sb, sc = split3(jnp.concatenate([src[r] for r in range(10)], axis=0))
    for k, (t, s) in enumerate([(ta, sa), (ta, sb), (tb, sa), (ta, sc), (tb, sb), (tc, sa)]):
        t6[k * 16:k * 16 + 10, :] = t
        s6[k * 16:k * 16 + 10, :] = s

    def score_step(j, peak):
        cols = pl.ds(pl.multiple_of((j * 2 + core) * 256, 256), 256)
        s = jnp.maximum(dot(t6[:, cols], s6[...], ((0,), (0,))), 0.0)
        scores[pl.ds(pl.multiple_of(j * 256, 256), 256), :] = s
        return jnp.maximum(peak, jnp.max(s.reshape(32, 8, 512), axis=0))

    m_r1.recv()
    m_c1.recv()
    s1[...] = (pool[1].astype(F32) + r1[...].astype(F32)).astype(BF)
    s1cnt[...] = pcnt[1] + c1[...]
    m_rs, m_rc = Group(rs.at[0:7]), Group(rscnt.at[0:7])
    for k, (a, b) in enumerate(hops):
        xx, yy = (x + a) % 4, (yh + b) % 2
        m_rs.send(s1.at[xx, yy], rs.at[k], chips[k])
        m_rc.send(s1cnt.at[pl.ds(xx * 2 + yy, 1)], rscnt.at[k], chips[k])

    peak = lax.fori_loop(0, 4, score_step, jnp.zeros((8, 512), F32))
    m_h.recv()
    st_y[1].same(mhalf(f, 1), fdev(fy))
    st_y[1].same(halo.at[f], fdev(fy))
    st_z.same(halo.at[f], fdev(fzp), fdev(fzm))
    peak = lax.fori_loop(4, 8, score_step, peak)
    peak = jnp.max(peak, axis=0, keepdims=True)

    def exp_step(j, total):
        rows = pl.ds(pl.multiple_of(j * 256, 256), 256)
        e = jnp.exp(scores[rows, :] - peak)
        expo[rows, :] = e.astype(BF)
        return total + jnp.sum(e.reshape(32, 8, 512), axis=0)

    total = lax.fori_loop(0, 8, exp_step, jnp.zeros((8, 512), F32))
    total = jnp.sum(total, axis=0, keepdims=True)
    both = jnp.concatenate([peak, total], axis=0)
    for h in range(2):
        stat[h] = both[:, h * 256:(h + 1) * 256]
    m_stat = Group(stat_in)
    m_stat.send(stat.at[1 - core], stat_in, partner)

    st_y[0].recv()
    st_yz[0].same(mhalf(fy, 0), fdev(fzp), fdev(fzm))
    st_z.recv()
    st_far.same(mhalf(fzm, 0), fdev(fzp))
    st_far.same(mhalf(fzp, 1), fdev(fzm))
    st_far.same(halo.at[fzm, 0], fdev(fzp))
    st_far.same(halo.at[fzp, 1], fdev(fzm))
    m_rs.recv()
    m_rc.recv()
    sums, cnt = s1[x, yh].astype(F32), s1cnt[pl.ds(x * 2 + yh, 1), :]
    for k in range(7):
        sums = sums + rs[k].astype(F32)
        cnt = cnt + rscnt[k]
    pooled = sums / jnp.maximum(cnt, 1.0)
    pa, pb, pc = split3(pooled)
    wv = w_val[...]
    vals[d] = (dot(wv, pa) + dot(wv, pb) + dot(wv, pc)).astype(BF)

    near, far = Group(vals.at[0:4]), Group(vals.at[0:3])
    for k in range(7):
        (far if k < 3 else near).same(vals.at[d], chips[k])
    st_y[1].recv()
    st_yz[1].same(mhalf(fy, 1), fdev(fzp), fdev(fzm))
    st_yz[1].same(halo.at[fy], fdev(fzp), fdev(fzm))
    loc[0].wait()
    for k in range(4):
        wg[k * 192:(k + 1) * 192, :] = wraw[:, k, :]

    def attend(total, chips_at):
        for i in chips_at:
            rows = pl.ds(pl.multiple_of(i * 128, 256), 256)
            total = total + dot(vals[i + core], expo[rows, :])
        return total

    mine_of = lambda ks, c: [chip(*hops[k]) + c for k in ks]
    at = lambda ks: [chip(*hops[k]) for k in ks]
    near.recv()
    att = attend(jnp.zeros((64, 512), F32), [chip(0, 0)] + at(range(3, 7)))
    far.recv()
    att = attend(att, at(range(3)))
    for h in range(2):
        part[h] = att[:, h * 256:(h + 1) * 256]
    m_part = Group(part_in)
    m_part.send(part.at[1 - core], part_in, partner)
    m_stat.recv()
    peaks = stat[core, 0:1, :], stat_in[0:1, :]
    top = jnp.maximum(*peaks)
    wa, wb = (jnp.exp(i - top) for i in peaks)
    inv = 1.0 / (stat[core, 1:2, :] * wa + stat_in[1:2, :] * wb)
    m_part.recv()
    attn = (pooled + part[core] * (wa * inv) + part_in[...] * (wb * inv)).astype(BF)
    m_ca = [Group(ca.at[0, 0:7]) for h in range(2)]
    for h in range(2):
        ca[h, f] = attn[:, h * 128:(h + 1) * 128]
    for h in range(2):
        m_ca[h].same(ca.at[h, f], *f_peers)
    st_yz[0].recv()
    st_far.same(mhalf(fi(zm, 1 - yl), 0), fdev(fzp))
    st_yz[1].recv()
    st_far.same(mhalf(fi(zp, 1 - yl), 1), fdev(fzm))
    st_far.same(halo.at[fi(zp, 1 - yl)], fdev(fzm))
    early = list(groups)
    gall = (gall0, gall1, gall2)
    pieces = ((0, 64), (64, 128), (128, 192))
    slot = lambda g, i: gall[g].at[pl.ds(2 * i, 2)]
    several = lambda n: [Group(gall[g].at[0:2 * n]) for g in range(3)]
    g_far, g_near, g_p = several(3), several(4), several(8)

    def g_send(g, h):
        g_far[g].same(gall[g].at[2 * d + h], *chips[:3])
        g_near[g].same(gall[g].at[2 * d + h], *chips[3:])
        g_p[g].same(gall[g].at[2 * d + h], partner)

    for h in range(2):
        m_ca[h].recv()
        for g, (lo, hi) in enumerate(pieces):
            gall[g][2 * d + h] = dot(wg[576 + lo:576 + hi, :], ca[h].reshape(512, 128)).astype(BF)
            if g == 0 or g == 1 and h == 1:
                g_send(g, h)
        if h == 0:
            g_send(1, 0)
    for h in range(2):
        g_send(2, h)

    st_far.recv()
    for i in range(8):
        mext[i * 64:(i + 1) * 64, 0:128] = halo[i, 0]
        mext[i * 64:(i + 1) * 64, 2176:2304] = halo[i, 1]

    for c in range(9):
        cols = slice(c * 256, (c + 1) * 256)
        r = dot(wg[0:576, :], mext[:, cols])
        gsum[:, cols] = r[0:192]
        w1m[:, cols] = r[192:384]
        ubuf[:, cols] = r[384:576].astype(BF)

    loc[1].wait()

    def diffuse(buf, t):
        lo, mid, hi = (buf[:, (t + k) * 128:(t + k + 1) * 128] for k in range(3))

        def pick(k):
            c = jnp.full((1, 128), adj_cols[k, t], jnp.int32)
            wlo, wmid, whi = ((c == t + i).astype(F32).astype(BF) for i in range(3))
            return lo * wlo + mid * wmid + hi * whi

        lhs = jnp.concatenate([lo, pick(1), pick(2), hi], axis=1)
        r = dot(lhs, adj[t])
        pos = lax.broadcasted_iota(jnp.int32, (1, 128), 1) + t * 128
        return r * (pos < nvalid).astype(F32)

    def first(t):
        cols = slice((t + 1) * 128, (t + 2) * 128)
        vbuf[:, cols] = (w1m[:, cols] + diffuse(ubuf, t)).astype(BF)

    def second(t):
        cols = slice((t + 1) * 128, (t + 2) * 128)
        gsum[:, cols] = gsum[:, cols] + diffuse(vbuf, t)

    first(0)
    first(15)
    tile = lambda i: vbuf.at[:, pl.ds(i * 128, 128)]
    m_vh = Group(vbuf.at[:, 0:256])
    m_vh.send(tile(1), tile(17), dleft)
    m_vh.send(tile(16), tile(0), dright)
    for t in range(1, 15):
        first(t)
    for t in range(1, 15):
        second(t)
    def swap(g):
        for group, ks in ((g_near, range(3, 7)), (g_far, range(3))):
            group[g].recv()
            for i in mine_of(ks, core):
                g_p[g].same(slot(g, i), partner)

    for m in early:
        m.sent()
    loc[2].wait()
    eye = lax.broadcasted_iota(jnp.int32, (64, 64), 0) == lax.broadcasted_iota(
        jnp.int32, (64, 64), 1
    )
    column = lambda row: jnp.sum(jnp.where(eye, row, 0.0), axis=1, keepdims=True)
    bcol = [column(bias[g:g + 1, :]) for g in range(3)]
    win = [w_in[g].astype(F32) for g in range(3)]
    wcol = [[column(win[g][i:i + 1]) for i in range(2)] for g in range(3)]

    def unpool(p):
        lo, hi = pieces[p]
        rows, count, g = slice(lo, hi), hi - lo, min(p, 2)
        part = slice(lo - 64 * g, hi - 64 * g)
        g_p[p].recv()
        for s in range(8):
            tiles = []
            for t in range(4 * s, 4 * s + 4):
                lhs = jnp.concatenate([gall[p][ccols[k, t]] for k in range(2)], axis=1)
                tiles.append(gall[p][t].astype(F32) + dot(lhs, ct[t]))
            gmix[s] = jnp.concatenate(tiles, axis=1).astype(BF)
        if p < 2:
            swap(p + 1)
        for n in range(8):
            cols = slice(n * 256, (n + 1) * 256)
            ecols = slice(n * 256 + 128, (n + 1) * 256 + 128)
            hi_n = cluster[:, cols] >> 9
            r = dot(gmix[...].reshape(8 * count, 512), ohlo[:, cols])
            acc = r[0:count]
            for s in range(1, 8):
                acc = jnp.where(hi_n == s, r[s * count:(s + 1) * count], acc)
            pre = acc + gsum[rows, ecols]
            xi = xin[:, cols].astype(F32)
            terms = wcol[g][0][part] * xi[0:1] + wcol[g][1][part] * xi[1:2] + bcol[g][part]
            if g == 0:
                gsum[rows, ecols] = terms + pre
                continue
            if g == 1:
                gsum[0:64, ecols] = jax.nn.sigmoid(gsum[0:64, ecols])
                gsum[rows, ecols] = jax.nn.sigmoid(terms + pre)
                continue
            update, reset = gsum[part, ecols], gsum[64 + lo - 128:64 + hi - 128, ecols]
            cand = jnp.tanh(terms + reset * pre)
            mk = (lax.broadcasted_iota(jnp.int32, (1, 256), 1) + n * 256 < nvalid).astype(F32)
            ms = state[part, cols].astype(F32) * mk
            out[part, cols] = ((update * ms + (1.0 - update) * cand) * mk).astype(BF)

    swap(0)
    unpool(0)
    m_vh.recv()
    second(0)
    second(15)
    unpool(1)
    unpool(2)

    for m in groups[len(early):]:
        m.sent()
    assert len(groups) == N_MSG


def body(
    state, inputs, adj_tiles, adj_cols, valid_rows, cluster_of, w_gates, w_input, bias, w_value,
    source_emb, target_emb, coarse_tiles, coarse_cols,
):
    vm = pl.BlockSpec(memory_space=pltpu.VMEM)
    sm = pl.BlockSpec(memory_space=pltpu.SMEM)
    hb = pl.BlockSpec(memory_space=pl.ANY)
    V = pltpu.VMEM
    return pl.pallas_call(
        kernel,
        out_shape=pltpu.VMEM(state.shape, BF),
        in_specs=[vm, vm, hb, sm, sm, vm, hb, vm, vm, vm, hb, hb, hb, sm],
        out_specs=vm,
        scratch_shapes=[
            V((512, 2304), BF),
            V((8, 2, 64, 128), BF),
            V((512, 2048), BF),
            V((64, 2048), BF),
            V((512, 2048), BF),
            V((2, 4, 2, 64, 256), BF),
            V((2, 8, 256), F32),
            V((4, 2, 64, 256), BF),
            V((8, 256), F32),
            V((4, 2, 64, 256), BF),
            V((8, 256), F32),
            V((7, 64, 256), BF),
            V((7, 1, 256), F32),
            V((10, 1, 512), F32),
            V((16, 4096), F32),
            V((96, 4096), BF),
            V((96, 512), BF),
            V((2048, 512), F32),
            V((2048, 512), BF),
            V((2, 2, 256), F32),
            V((2, 256), F32),
            V((2, 64, 256), F32),
            V((64, 256), F32),
            V((16, 64, 256), BF),
            V((2, 8, 64, 128), BF),
            V((32, 64, 128), BF),
            V((32, 64, 128), BF),
            V((32, 64, 128), BF),
            V((8, 64, 512), BF),
            V((192, 2304), BF),
            V((192, 2304), BF),
            V((192, 2304), F32),
            V((192, 2304), F32),
            V((16, 512, 128), BF),
            V((192, 4, 512), BF),
            V((768, 512), BF),
            V((32, 256, 128), BF),
            pltpu.SemaphoreType.DMA((N_MSG,)),
            pltpu.SemaphoreType.DMA((N_MSG,)),
            pltpu.SemaphoreType.DMA((5,)),
        ],
        compiler_params=pltpu.CompilerParams(collective_id=0, has_side_effects=True),
    )(
        state, inputs, adj_tiles.reshape(16, 512, 128), adj_cols.T, valid_rows,
        cluster_of.reshape(1, 2048), w_gates.reshape(192, 4, 512),
        jnp.transpose(w_input, (0, 2, 1)), bias, w_value.reshape(64, 64),
        jnp.transpose(source_emb, (1, 0, 2)), jnp.transpose(target_emb, (1, 0, 2)),
        coarse_tiles.reshape(32, 256, 128), coarse_cols.T,
    )


def solution(mesh):
    return jax.shard_map(
        body,
        mesh=mesh,
        in_specs=(
            P("feat", "dom"),
            P(None, "dom"),
            P("dom", None, None, None),
            P("dom", None),
            P("dom"),
            P("dom"),
            P(None, "feat", None, None),
            P(None, "feat", None),
            P(None, "feat"),
            P("feat", None, None),
            P("feat", None, None),
            P("feat", None, None),
            P(),
            P(),
        ),
        out_specs=P("feat", "dom"),
        check_vma=False,
    )
```

```python
import jax
import jax.numpy as jnp
from jax import lax
from jax.experimental import pallas as pl
from jax.experimental.pallas import tpu as pltpu
from jax.sharding import PartitionSpec as P

MESH = pl.DeviceIdType.MESH
BF = jnp.bfloat16
F32 = jnp.float32
N_MSG = 27


def dot(a, b, dims=((1,), (0,))):
    return lax.dot_general(a, b, (dims, ((), ())), preferred_element_type=F32)


def split3(v):
    a = v.astype(BF)
    r = v - a.astype(F32)
    b = r.astype(BF)
    c = (r - b.astype(F32)).astype(BF)
    return a, b, c


def kernel(
    state, xin, adj_hbm, adj_cols, valid, cluster, wg_hbm, w_in, bias, w_val, src_hbm, tgt_hbm,
    ct_hbm, ccols, out,
    mext, halo, ohlo, base, pl_lhs, pool, pcnt, r1, c1, s1, s1cnt, rs, rscnt, src, tgt, t6, s6, scores, expo, stat, stat_in, part, part_in,
    vals, ca, gall0, gall1, gall2, gmix, ubuf, vbuf, w1m, gsum, adj, wraw, wg, ct,
    ssem, rsem, lsem,
):
    d = lax.axis_index("dom")
    f = lax.axis_index("feat")
    core, x, yh = d % 2, (d // 2) % 4, d // 8
    z, yl = f // 2, f % 2
    zp, zm = (z + 1) % 4, (z + 3) % 4
    dev = lambda i: (i, f)
    fdev = lambda i: (d, i)
    partner = dev(d + 1 - 2 * core)
    hops = [(2, 1), (1, 1), (3, 1), (2, 0), (0, 1), (1, 0), (3, 0)]
    chip = lambda a, b: ((yh + b) % 2) * 8 + ((x + a) % 4) * 2
    chips = [dev(chip(a, b) + core) for a, b in hops]
    dleft, dright = dev((d + 15) % 16), dev((d + 1) % 16)
    fi = lambda a, b: a * 2 + b
    fy, fzp, fzm = f + 1 - 2 * yl, fi(zp, yl), fi(zm, yl)
    z2 = (z + 2) % 4
    f_peers = [fdev(fi(*i)) for i in ((z2, 1 - yl), (z2, yl), (zp, 1 - yl), (zm, 1 - yl))]
    f_peers += [fdev(fzp), fdev(fzm), fdev(fy)]

    groups = []

    class Group:
        def __init__(self, whole):
            self.whole, self.sems = whole, (ssem.at[len(groups)], rsem.at[len(groups)])
            groups.append(self)

        def copy(self, src_ref, dst_ref, to):
            return pltpu.make_async_remote_copy(
                src_ref=src_ref, dst_ref=dst_ref, send_sem=self.sems[0], recv_sem=self.sems[1],
                device_id=to, device_id_type=MESH,
            )

        def send(self, src_ref, dst_ref, to):
            self.copy(src_ref, dst_ref, to).start()

        def same(self, ref, *to):
            for i in to:
                self.send(ref, ref, i)

        def recv(self):
            self.copy(self.whole, self.whole, partner).wait_recv()

        def sent(self):
            self.copy(self.whole, self.whole, partner).wait_send()

    mine = pl.ds(pl.multiple_of((yh * 4 + x) * 512, 512), 512)
    loc = [
        pltpu.make_async_copy(wg_hbm, wraw, lsem.at[0]),
        pltpu.make_async_copy(adj_hbm, adj, lsem.at[1]),
        pltpu.make_async_copy(ct_hbm, ct, lsem.at[2]),
    ]
    tgt_rows = [pltpu.make_async_copy(tgt_hbm.at[r], tgt.at[pl.ds(r, 1)], lsem.at[3]) for r in range(10)]
    src_rows = pltpu.make_async_copy(src_hbm.at[:, :, mine], src, lsem.at[4])
    for c in tgt_rows + [src_rows] + loc:
        c.start()

    barrier = pltpu.get_barrier_semaphore()
    cross = dev((d + 15 + 2 * core) % 16)
    peers = chips + f_peers + [cross, partner]
    for p in peers:
        pl.semaphore_signal(barrier, inc=1, device_id=p, device_id_type=MESH)

    nvalid = valid[0]
    mask = (lax.broadcasted_iota(jnp.int32, (1, 2048), 1) < nvalid).astype(F32)
    masked32 = state[...].astype(F32) * mask
    myrows = pl.ds(pl.multiple_of(f * 64, 64), 64)
    own = pl.ds(128, 2048)
    base[...] = masked32.astype(BF)
    mext[myrows, own] = base[...]
    low = cluster[...] & 511
    high = cluster[...] >> 9
    row8 = lax.broadcasted_iota(jnp.int32, (8, 2048), 0)
    cnt_lhs = jnp.where(high == (row8 & 1) * 4 + (row8 >> 1), mask, 0.0).astype(BF)

    def pool_part(c, to_core):
        rows = pl.ds(pl.multiple_of(to_core * 256, 256), 256)
        row = lax.broadcasted_iota(jnp.int32, (256, 2048), 0) + to_core * 256
        ohlo[rows, :] = (row == low).astype(F32).astype(BF)
        for i in range(2):
            if c == 0:
                for slot in range(i * 4, i * 4 + 4):
                    hit = high == (slot % 2) * 4 + slot // 2
                    pl_lhs[slot * 64:(slot + 1) * 64, :] = base[...] * hit.astype(F32).astype(BF)
            res = dot(pl_lhs[i * 256:(i + 1) * 256, :], ohlo[rows, :], ((1,), (1,))).astype(BF)
            for k in range(4):
                slot = i * 4 + k
                pool[c, slot // 2, slot % 2] = res[k * 64:(k + 1) * 64]
        pcnt[c] = dot(cnt_lhs, ohlo[rows, :], ((1,), (1,)))

    pool_part(0, 1 - core)

    pl.semaphore_wait(barrier, len(peers))

    m_r1, m_c1 = Group(r1), Group(c1)
    m_r1.send(pool.at[0], r1, partner)
    m_c1.send(pcnt.at[0], c1, partner)
    mrow = lambda i: mext.at[pl.ds(pl.multiple_of(i * 64, 64), 64), own]
    mhalf = lambda i, h: mext.at[pl.ds(pl.multiple_of(i * 64 + h * 32, 32), 32), own]
    st_y = [Group(expo.at[0:n]) for n in (128, 160)]
    st_yz = [Group(expo.at[0:n]) for n in (256, 320)]
    st_z, st_far = Group(expo.at[0:576]), Group(expo.at[0:576])
    m_h = Group(halo.at[0])
    m_h.send(mext.at[myrows, pl.ds(128, 128)], halo.at[f, 1], dleft)
    m_h.send(mext.at[myrows, pl.ds(2048, 128)], halo.at[f, 0], dright)
    st_y[0].same(mhalf(f, 0), fdev(fy))
    st_z.same(mrow(f), fdev(fzp), fdev(fzm))
    pool_part(1, core)

    pltpu.make_async_copy(expo.at[0:160], expo.at[0:160], lsem.at[3]).wait()
    src_rows.wait()
    t6[...] = jnp.zeros_like(t6)
    s6[...] = jnp.zeros_like(s6)
    ta, tb, tc = split3(tgt[0:10, :])
    sa, sb, sc = split3(jnp.concatenate([src[r] for r in range(10)], axis=0))
    for k, (t, s) in enumerate([(ta, sa), (ta, sb), (tb, sa), (ta, sc), (tb, sb), (tc, sa)]):
        t6[k * 16:k * 16 + 10, :] = t
        s6[k * 16:k * 16 + 10, :] = s

    def score_step(j, peak):
        cols = pl.ds(pl.multiple_of((j * 2 + core) * 256, 256), 256)
        s = jnp.maximum(dot(t6[:, cols], s6[...], ((0,), (0,))), 0.0)
        scores[pl.ds(pl.multiple_of(j * 256, 256), 256), :] = s
        return jnp.maximum(peak, jnp.max(s.reshape(32, 8, 512), axis=0))

    m_r1.recv()
    m_c1.recv()
    s1[...] = (pool[1].astype(F32) + r1[...].astype(F32)).astype(BF)
    s1cnt[...] = pcnt[1] + c1[...]
    m_rs, m_rc = Group(rs.at[0:7]), Group(rscnt.at[0:7])
    for k, (a, b) in enumerate(hops):
        xx, yy = (x + a) % 4, (yh + b) % 2
        m_rs.send(s1.at[xx, yy], rs.at[k], chips[k])
        m_rc.send(s1cnt.at[pl.ds(xx * 2 + yy, 1)], rscnt.at[k], chips[k])

    peak = lax.fori_loop(0, 4, score_step, jnp.zeros((8, 512), F32))
    m_h.recv()
    st_y[1].same(mhalf(f, 1), fdev(fy))
    st_y[1].same(halo.at[f], fdev(fy))
    st_z.same(halo.at[f], fdev(fzp), fdev(fzm))
    peak = lax.fori_loop(4, 8, score_step, peak)
    peak = jnp.max(peak, axis=0, keepdims=True)

    def exp_step(j, total):
        rows = pl.ds(pl.multiple_of(j * 256, 256), 256)
        e = jnp.exp(scores[rows, :] - peak)
        expo[rows, :] = e.astype(BF)
        return total + jnp.sum(e.reshape(32, 8, 512), axis=0)

    total = lax.fori_loop(0, 8, exp_step, jnp.zeros((8, 512), F32))
    total = jnp.sum(total, axis=0, keepdims=True)
    both = jnp.concatenate([peak, total], axis=0)
    for h in range(2):
        stat[h] = both[:, h * 256:(h + 1) * 256]
    m_stat = Group(stat_in)
    m_stat.send(stat.at[1 - core], stat_in, partner)

    st_y[0].recv()
    st_yz[0].same(mhalf(fy, 0), fdev(fzp), fdev(fzm))
    st_z.recv()
    st_far.same(mhalf(fzm, 0), fdev(fzp))
    st_far.same(mhalf(fzp, 1), fdev(fzm))
    st_far.same(halo.at[fzm, 0], fdev(fzp))
    st_far.same(halo.at[fzp, 1], fdev(fzm))
    m_rs.recv()
    m_rc.recv()
    sums, cnt = s1[x, yh].astype(F32), s1cnt[pl.ds(x * 2 + yh, 1), :]
    for k in range(7):
        sums = sums + rs[k].astype(F32)
        cnt = cnt + rscnt[k]
    pooled = sums / jnp.maximum(cnt, 1.0)
    pa, pb, pc = split3(pooled)
    wv = w_val[...]
    vals[d] = (dot(wv, pa) + dot(wv, pb) + dot(wv, pc)).astype(BF)

    near, far = Group(vals.at[0:4]), Group(vals.at[0:3])
    for k in range(7):
        (far if k < 3 else near).same(vals.at[d], chips[k])
    st_y[1].recv()
    st_yz[1].same(mhalf(fy, 1), fdev(fzp), fdev(fzm))
    st_yz[1].same(halo.at[fy], fdev(fzp), fdev(fzm))
    loc[0].wait()
    for k in range(4):
        wg[k * 192:(k + 1) * 192, :] = wraw[:, k, :]

    def attend(total, chips_at):
        for i in chips_at:
            rows = pl.ds(pl.multiple_of(i * 128, 256), 256)
            total = total + dot(vals[i + core], expo[rows, :])
        return total

    mine_of = lambda ks, c: [chip(*hops[k]) + c for k in ks]
    at = lambda ks: [chip(*hops[k]) for k in ks]
    near.recv()
    att = attend(jnp.zeros((64, 512), F32), [chip(0, 0)] + at(range(3, 7)))
    far.recv()
    att = attend(att, at(range(3)))
    for h in range(2):
        part[h] = att[:, h * 256:(h + 1) * 256]
    m_part = Group(part_in)
    m_part.send(part.at[1 - core], part_in, partner)
    m_stat.recv()
    peaks = stat[core, 0:1, :], stat_in[0:1, :]
    top = jnp.maximum(*peaks)
    wa, wb = (jnp.exp(i - top) for i in peaks)
    inv = 1.0 / (stat[core, 1:2, :] * wa + stat_in[1:2, :] * wb)
    m_part.recv()
    attn = (pooled + part[core] * (wa * inv) + part_in[...] * (wb * inv)).astype(BF)
    m_ca = [Group(ca.at[0, 0:7]) for h in range(2)]
    for h in range(2):
        ca[h, f] = attn[:, h * 128:(h + 1) * 128]
    for h in range(2):
        m_ca[h].same(ca.at[h, f], *f_peers)
    st_yz[0].recv()
    st_far.same(mhalf(fi(zm, 1 - yl), 0), fdev(fzp))
    st_yz[1].recv()
    st_far.same(mhalf(fi(zp, 1 - yl), 1), fdev(fzm))
    st_far.same(halo.at[fi(zp, 1 - yl)], fdev(fzm))
    early = list(groups)
    gall = (gall0, gall1, gall2)
    pieces = ((0, 64), (64, 128), (128, 192))
    slot = lambda g, i: gall[g].at[pl.ds(2 * i, 2)]
    several = lambda n: [Group(gall[g].at[0:2 * n]) for g in range(3)]
    g_far, g_near, g_p = several(3), several(4), several(8)

    def g_send(g, h):
        g_far[g].same(gall[g].at[2 * d + h], *chips[:3])
        g_near[g].same(gall[g].at[2 * d + h], *chips[3:])
        g_p[g].same(gall[g].at[2 * d + h], partner)

    for h in range(2):
        m_ca[h].recv()
        for g, (lo, hi) in enumerate(pieces):
            gall[g][2 * d + h] = dot(wg[576 + lo:576 + hi, :], ca[h].reshape(512, 128)).astype(BF)
            if g == 0:
                g_send(g, h)
    for g in (1, 2):
        for h in range(2):
            g_send(g, h)

    st_far.recv()
    for i in range(8):
        mext[i * 64:(i + 1) * 64, 0:128] = halo[i, 0]
        mext[i * 64:(i + 1) * 64, 2176:2304] = halo[i, 1]

    for c in range(9):
        cols = slice(c * 256, (c + 1) * 256)
        r = dot(wg[0:576, :], mext[:, cols])
        gsum[:, cols] = r[0:192]
        w1m[:, cols] = r[192:384]
        ubuf[:, cols] = r[384:576].astype(BF)

    loc[1].wait()

    def diffuse(buf, t):
        lo, mid, hi = (buf[:, (t + k) * 128:(t + k + 1) * 128] for k in range(3))

        def pick(k):
            c = jnp.full((1, 128), adj_cols[k, t], jnp.int32)
            wlo, wmid, whi = ((c == t + i).astype(F32).astype(BF) for i in range(3))
            return lo * wlo + mid * wmid + hi * whi

        lhs = jnp.concatenate([lo, pick(1), pick(2), hi], axis=1)
        r = dot(lhs, adj[t])
        pos = lax.broadcasted_iota(jnp.int32, (1, 128), 1) + t * 128
        return r * (pos < nvalid).astype(F32)

    def first(t):
        cols = slice((t + 1) * 128, (t + 2) * 128)
        vbuf[:, cols] = (w1m[:, cols] + diffuse(ubuf, t)).astype(BF)

    def second(t):
        cols = slice((t + 1) * 128, (t + 2) * 128)
        gsum[:, cols] = gsum[:, cols] + diffuse(vbuf, t)

    first(0)
    first(15)
    tile = lambda i: vbuf.at[:, pl.ds(i * 128, 128)]
    m_vh = Group(vbuf.at[:, 0:256])
    m_vh.send(tile(1), tile(17), dleft)
    m_vh.send(tile(16), tile(0), dright)
    for t in range(1, 15):
        first(t)
    def swap(g):
        for group, ks in ((g_near, range(3, 7)), (g_far, range(3))):
            group[g].recv()
            for i in mine_of(ks, core):
                g_p[g].same(slot(g, i), partner)

    swap(0)
    for t in range(1, 15):
        second(t)
    for m in early:
        m.sent()
    loc[2].wait()
    eye = lax.broadcasted_iota(jnp.int32, (64, 64), 0) == lax.broadcasted_iota(
        jnp.int32, (64, 64), 1
    )
    column = lambda row: jnp.sum(jnp.where(eye, row, 0.0), axis=1, keepdims=True)
    bcol = [column(bias[g:g + 1, :]) for g in range(3)]
    win = [w_in[g].astype(F32) for g in range(3)]
    wcol = [[column(win[g][i:i + 1]) for i in range(2)] for g in range(3)]

    def unpool(p):
        lo, hi = pieces[p]
        rows, count, g = slice(lo, hi), hi - lo, min(p, 2)
        part = slice(lo - 64 * g, hi - 64 * g)
        g_p[p].recv()
        for s in range(8):
            tiles = []
            for t in range(4 * s, 4 * s + 4):
                lhs = jnp.concatenate([gall[p][ccols[k, t]] for k in range(2)], axis=1)
                tiles.append(gall[p][t].astype(F32) + dot(lhs, ct[t]))
            gmix[s] = jnp.concatenate(tiles, axis=1).astype(BF)
        if p < 2:
            swap(p + 1)
        for n in range(8):
            cols = slice(n * 256, (n + 1) * 256)
            ecols = slice(n * 256 + 128, (n + 1) * 256 + 128)
            hi_n = cluster[:, cols] >> 9
            r = dot(gmix[...].reshape(8 * count, 512), ohlo[:, cols])
            acc = r[0:count]
            for s in range(1, 8):
                acc = jnp.where(hi_n == s, r[s * count:(s + 1) * count], acc)
            pre = acc + gsum[rows, ecols]
            xi = xin[:, cols].astype(F32)
            terms = wcol[g][0][part] * xi[0:1] + wcol[g][1][part] * xi[1:2] + bcol[g][part]
            if g == 0:
                gsum[rows, ecols] = terms + pre
                continue
            if g == 1:
                gsum[0:64, ecols] = jax.nn.sigmoid(gsum[0:64, ecols])
                gsum[rows, ecols] = jax.nn.sigmoid(terms + pre)
                continue
            update, reset = gsum[part, ecols], gsum[64 + lo - 128:64 + hi - 128, ecols]
            cand = jnp.tanh(terms + reset * pre)
            mk = (lax.broadcasted_iota(jnp.int32, (1, 256), 1) + n * 256 < nvalid).astype(F32)
            ms = state[part, cols].astype(F32) * mk
            out[part, cols] = ((update * ms + (1.0 - update) * cand) * mk).astype(BF)

    unpool(0)
    m_vh.recv()
    second(0)
    second(15)
    unpool(1)
    unpool(2)

    for m in groups[len(early):]:
        m.sent()
    assert len(groups) == N_MSG


def body(
    state, inputs, adj_tiles, adj_cols, valid_rows, cluster_of, w_gates, w_input, bias, w_value,
    source_emb, target_emb, coarse_tiles, coarse_cols,
):
    vm = pl.BlockSpec(memory_space=pltpu.VMEM)
    sm = pl.BlockSpec(memory_space=pltpu.SMEM)
    hb = pl.BlockSpec(memory_space=pl.ANY)
    V = pltpu.VMEM
    return pl.pallas_call(
        kernel,
        out_shape=pltpu.VMEM(state.shape, BF),
        in_specs=[vm, vm, hb, sm, sm, vm, hb, vm, vm, vm, hb, hb, hb, sm],
        out_specs=vm,
        scratch_shapes=[
            V((512, 2304), BF),
            V((8, 2, 64, 128), BF),
            V((512, 2048), BF),
            V((64, 2048), BF),
            V((512, 2048), BF),
            V((2, 4, 2, 64, 256), BF),
            V((2, 8, 256), F32),
            V((4, 2, 64, 256), BF),
            V((8, 256), F32),
            V((4, 2, 64, 256), BF),
            V((8, 256), F32),
            V((7, 64, 256), BF),
            V((7, 1, 256), F32),
            V((10, 1, 512), F32),
            V((16, 4096), F32),
            V((96, 4096), BF),
            V((96, 512), BF),
            V((2048, 512), F32),
            V((2048, 512), BF),
            V((2, 2, 256), F32),
            V((2, 256), F32),
            V((2, 64, 256), F32),
            V((64, 256), F32),
            V((16, 64, 256), BF),
            V((2, 8, 64, 128), BF),
            V((32, 64, 128), BF),
            V((32, 64, 128), BF),
            V((32, 64, 128), BF),
            V((8, 64, 512), BF),
            V((192, 2304), BF),
            V((192, 2304), BF),
            V((192, 2304), F32),
            V((192, 2304), F32),
            V((16, 512, 128), BF),
            V((192, 4, 512), BF),
            V((768, 512), BF),
            V((32, 256, 128), BF),
            pltpu.SemaphoreType.DMA((N_MSG,)),
            pltpu.SemaphoreType.DMA((N_MSG,)),
            pltpu.SemaphoreType.DMA((5,)),
        ],
        compiler_params=pltpu.CompilerParams(collective_id=0, has_side_effects=True),
    )(
        state, inputs, adj_tiles.reshape(16, 512, 128), adj_cols.T, valid_rows,
        cluster_of.reshape(1, 2048), w_gates.reshape(192, 4, 512),
        jnp.transpose(w_input, (0, 2, 1)), bias, w_value.reshape(64, 64),
        jnp.transpose(source_emb, (1, 0, 2)), jnp.transpose(target_emb, (1, 0, 2)),
        coarse_tiles.reshape(32, 256, 128), coarse_cols.T,
    )


def solution(mesh):
    return jax.shard_map(
        body,
        mesh=mesh,
        in_specs=(
            P("feat", "dom"),
            P(None, "dom"),
            P("dom", None, None, None),
            P("dom", None),
            P("dom"),
            P("dom"),
            P(None, "feat", None, None),
            P(None, "feat", None),
            P(None, "feat"),
            P("feat", None, None),
            P("feat", None, None),
            P("feat", None, None),
            P(),
            P(),
        ),
        out_specs=P("feat", "dom"),
        check_vma=False,
    )
```
